32 devices in a mesh: grp: 4 (over z), fsdp: 8 (over y, x, core).
Axes of the slice: x: 2, y: 2, z: 4, core: 2. Of those that a mesh axis runs over, the one named last changes fastest.
Arguments:
- tokens: bfloat16 [12288, 1024], P(('grp', 'fsdp')), may hold values from -6 to 6
- segment: int32 [12288], P(('grp', 'fsdp')), may hold values from 0 to 12, as said below
- positions: int32 [12288], P(('grp', 'fsdp')), may hold values from 0 to 233, as said below
- parents: int32 [32, 13], P(('grp', 'fsdp')), may hold values from 0 to 4, as said below
- routes: int32 [12288, 8], P(('grp', 'fsdp')), may hold values from 0 to 15, all different within a row; in each aligned block of 384 rows (0 to 383, 384 to 767, ...) at most 240 rows name the same one
- attn_gain: bfloat16 [1024], P('fsdp'), may hold values from 0.25 to 1.75
- query_weight: bfloat16 [1024, 1024], P('fsdp', 'grp'), may hold values from -0.1875 to 0.1875
- key_matrix: bfloat16 [1024, 512], P('fsdp', 'grp'), may hold values from -0.1875 to 0.1875
- value_matrix: bfloat16 [1024, 512], P('fsdp', 'grp'), may hold values from -0.1875 to 0.1875
- out_weight: bfloat16 [1024, 1024], P('fsdp', 'grp'), may hold values from -0.75 to 0.75
- ffn_gain: bfloat16 [1024], P('fsdp'), may hold values from 0.25 to 1.75
- router_weight: bfloat16 [1024, 16], P('fsdp'), may hold values from -0.09375 to 0.09375
- gate_up_weight: bfloat16 [1024, 16, 1024], P('fsdp', 'grp'), may hold values from -0.1875 to 0.1875
- down_weight: bfloat16 [1024, 16, 512], P('fsdp', 'grp'), may hold values from -1 to 1
- cotangent: bfloat16 [12288, 1024], P(('grp', 'fsdp')), may hold values from -6 to 6
Outputs:
- output: bfloat16 [12288, 1024], P(('grp', 'fsdp'))
- input_grad: float32 [12288, 1024], P(('grp', 'fsdp'))
- attn_gain_grad: float32 [1024], P('fsdp')
- query_grad: float32 [1024, 1024], P('fsdp', 'grp')
- key_grad: float32 [1024, 512], P('fsdp', 'grp')
- value_grad: float32 [1024, 512], P('fsdp', 'grp')
- out_weight_grad: float32 [1024, 1024], P('fsdp', 'grp')
- ffn_gain_grad: float32 [1024], P('fsdp')
- router_grad: float32 [1024, 16], P('fsdp')
- gate_up_grad: float32 [1024, 16, 1024], P('fsdp', 'grp')
- down_grad: float32 [1024, 16, 512], P('fsdp', 'grp')
The draws below stay inside these ranges and needn't reach their ends.
Inputs may be any that keep to these rules, and one draw needn't show every extreme that they name: Within each tree segment ids never fall; segment 0 (the trunk) comes first, then the 4 branches, then the 8 leaves; every segment has tokens; the trunk has 31 * (6) tokens. parents[t, s] is the parent segment of segment s of tree t: 0 for the trunk itself and for the branches, a branch for every leaf. `positions`: A token's position is the number of tokens of its ancestors' segments plus its index within its own segment. `routes`: each row names 8 different experts; among the rows of one tree no expert is named by more than 240 rows.
All inputs are finite; a program needn't handle non-finite values.
Results may differ from the reference program's by a relative error of at most 0.018.
Values may be sent and summed in bfloat16 or wider, within the bound.
No kernel may reach another device: no remote copies, remote signals or barrier semaphores. Data moves between devices by JAX's collectives and lax.ppermute only.
A program may use at most 384 MiB of HBM per device.

```python
import math
import jax
import jax.numpy as jnp
import numpy as np
from jax import lax

MODEL_WIDTH = 1024
QUERY_HEADS = 16
KEY_VALUE_HEADS = 8
HEAD_SIZE = 64
FF = 512
TOP = 8
EXPERTS = 16
BRANCHES = 4
LEAVES = 8
TOKENS_PER_TREE = 384
SEGS = 13
CAP = 240
TREES = 32
TOKENS = 12288


def tree_layout(key):
    base_key = jax.random.fold_in(key, 911)
    length_key, parent_key = jax.random.split(base_key)
    unit_size = TOKENS_PER_TREE // 64
    length_pool = jnp.array([1, 1, 2, 2, 2, 3, 3, 3, 4, 4], dtype=jnp.int32)
    tree_keys = jax.random.split(length_key, TREES)
    shuffled = jax.vmap(lambda one_key: jax.random.permutation(one_key, length_pool))(tree_keys).astype(jnp.int32)
    longest = jnp.full((TREES, 1), 4, dtype=jnp.int32)
    trunk_units = jnp.full((TREES, 1), 31, dtype=jnp.int32)
    units = jnp.concatenate([trunk_units, longest, shuffled[:, :3], longest, shuffled[:, 3:]], axis=1)
    lengths = (units * unit_size).astype(jnp.int32)
    leaf_parents = jax.random.randint(parent_key, (TREES, LEAVES), 1, BRANCHES + 1, dtype=jnp.int32)
    leaf_parents = jnp.concatenate([jnp.ones((TREES, 1), jnp.int32), leaf_parents[:, 1:]], axis=1)
    parents = jnp.concatenate([jnp.zeros((TREES, 1 + BRANCHES), jnp.int32), leaf_parents], axis=1)
    return (lengths, parents)


def tree_segments(lengths):
    ends = jnp.cumsum(lengths, axis=1).astype(jnp.int32)
    places = jnp.arange(TOKENS_PER_TREE, dtype=jnp.int32)
    passed = (places[None, :, None] >= ends[:, None, :SEGS - 1]).astype(jnp.int32)
    return (jnp.sum(passed, axis=2).astype(jnp.int32), ends)


def draw_parents(key, part):
    lengths, parents = tree_layout(key)
    return parents


def draw_segment(key, part):
    lengths, parents = tree_layout(key)
    segment, ends = tree_segments(lengths)
    return segment.reshape(-1)


def draw_positions(key, part):
    lengths, parents = tree_layout(key)
    segment, ends = tree_segments(lengths)
    starts = ends - lengths
    seg_ids = jnp.arange(SEGS, dtype=jnp.int32)
    parent_length = jnp.sum(jnp.where(parents[:, :, None] == seg_ids[None, None, :], lengths[:, None, :], 0), axis=2).astype(jnp.int32)
    offsets = jnp.where(seg_ids[None, :] == 0, 0, lengths[:, :1] + jnp.where(parents == 0, 0, parent_length))
    shift_table = (offsets - starts).astype(jnp.int32)
    in_segment = segment[:, :, None] == seg_ids[None, None, :]
    base_shift = jnp.sum(jnp.where(in_segment, shift_table[:, None, :], 0), axis=2).astype(jnp.int32)
    places = jnp.arange(TOKENS_PER_TREE, dtype=jnp.int32)
    return (base_shift + places[None, :]).astype(jnp.int32).reshape(-1)


def spiked(values, rng, source, target, blocks, factor):
    owner, partner = [(jnp.arange(values.shape[dim]) // (values.shape[dim] // blocks)).reshape([-1 if axis == dim else 1 for axis in range(values.ndim)]) for dim in (source, target)]
    chosen = jax.random.permutation(rng, blocks)[partner]
    strong = (owner == chosen) | (owner == (partner + blocks // 2) % blocks)
    return jnp.where(strong, factor * values, values)


def block_levels(own_key, extent, pieces, smallest, high):
    def one(axis_at, blocks):
        steps = jax.random.uniform(jax.random.fold_in(jax.random.fold_in(own_key, 6), axis_at), (blocks,), jnp.float32, smallest / len(pieces), high / len(pieces))
        return jnp.repeat(jnp.exp(steps), extent[axis_at] // blocks).reshape((-1,) + (1,) * (len(extent) - axis_at - 1))

    loudness = one(*pieces[0])
    for cut in pieces[1:]:
        loudness = loudness * one(*cut)
    return loudness


def shared_out(stream_key, own, number, rows, count, top, bound, skew):
    sequence = jax.random.permutation(stream_key, count)
    crowded, ordinary = portions_of(count, rows * top, bound, skew, True), portions_of(count, rows * top, bound, skew, False)
    places = jnp.arange(count)

    def named(sizes, turn):
        used = int((sizes > 0).sum())
        fixed = max(1, used // 4)
        shifted = fixed + (places - fixed + turn * (used - fixed)) % max(1, count - fixed)
        return jnp.zeros((count,), jnp.int32).at[sequence[jnp.where(places < fixed, places, shifted)]].set(jnp.asarray(sizes, jnp.int32))

    sizes = jnp.where(number % 4 == 0, named(crowded, number // 4), named(ordinary, number - number // 4 - 1))
    mixed = jax.random.permutation(jax.random.fold_in(own, 3), count)
    giver, receiver = mixed[0:count // 2 * 2:2], mixed[1:count // 2 * 2:2]
    room = jnp.minimum(sizes[giver] - 1, bound - sizes[receiver]) // 2
    room = jnp.where((giver == sequence[0]) | (receiver == sequence[0]) | (sizes[receiver] == 0), 0, jnp.maximum(room, 0))
    shifted = jax.random.randint(jax.random.fold_in(own, 4), (count // 2,), 0, 1 << 20) % (room + 1)
    sizes = sizes.at[giver].add(-shifted).at[receiver].add(shifted)
    labels = jnp.searchsorted(jnp.cumsum(sizes), jnp.arange(rows * top), side="right").astype(jnp.int32)
    listing = labels.reshape(top, rows).T
    listing = listing[jax.random.permutation(jax.random.fold_in(own, 1), rows)]
    turn = jax.random.randint(jax.random.fold_in(own, 2), (rows, 1), 0, top)
    return jnp.take_along_axis(listing, (jnp.arange(top)[None, :] + turn) % top, axis=1)


def portions_of(amount, total, bound, lean, full):
    weights = [(1 << 20) // math.isqrt(standing ** lean) + 1 for standing in range(1, amount + 1)]
    largest = bound if full else min(bound, max(-(-total // amount), total * weights[0] // sum(weights)))
    least = 1 if total - largest >= amount - 1 else 0
    counts, surplus = [largest] + [least] * (amount - 1), total - largest - least * (amount - 1)
    while surplus > 0:
        free = [i for i in range(1, amount) if counts[i] < largest] or [i for i in range(1, amount) if counts[i] < bound]
        pool, budget = sum([weights[i] for i in free]), surplus
        for i in free:
            extra = min(bound - counts[i], max(1, budget * weights[i] // pool), surplus)
            counts[i] = counts[i] + extra
            surplus = surplus - extra
    return np.array(counts)


def scatter_about(rng, extent, deviation, reach, cuts=(), kind=jnp.bfloat16):
    loudness = block_levels(rng, extent, cuts, -0.22, 0.18) if cuts else 1.0
    values = jax.random.normal(rng, extent, jnp.float32) * deviation * loudness
    return jnp.minimum(jnp.maximum(values, -reach), reach).astype(kind)


def bell_draw_with(stream_key, shape, deviation, bound, cuts, heavy, held_as=jnp.bfloat16):
    values = deviation * jax.random.normal(stream_key, shape, jnp.float32)
    if cuts:
        values = values * block_levels(stream_key, shape, cuts, -0.22, 0.18)
    return jnp.clip(spiked(values, jax.random.fold_in(stream_key, 3), *heavy), -bound, bound).astype(held_as)


def setup_inputs(seed: int = 0) -> dict:
    key_of = jax.random.split(jax.random.key(seed), 16)
    tokens = scatter_about(key_of[0], (TOKENS, MODEL_WIDTH), 1.0, 6.0, ((0, 32),))
    segment = draw_segment(jax.random.fold_in(key_of[15], 71), 0)
    positions = draw_positions(jax.random.fold_in(key_of[15], 71), 0)
    parents = draw_parents(jax.random.fold_in(key_of[15], 71), 0)
    routes_keys = jax.random.split(jax.random.fold_in(key_of[4], 1), TOKENS // TOKENS_PER_TREE)
    routes_turns = jax.random.permutation(jax.random.fold_in(key_of[4], 3), TOKENS // TOKENS_PER_TREE)
    routes = jax.vmap(lambda own, number: shared_out(jax.random.fold_in(key_of[4], 2), own, number, TOKENS_PER_TREE, EXPERTS, TOP, CAP, 1))(routes_keys, routes_turns).reshape((TOKENS, TOP))
    attn_gain = jnp.clip(1.0 + 0.15 * jax.random.normal(key_of[5], (MODEL_WIDTH,), jnp.float32), 0.25, 1.75).astype(jnp.bfloat16)
    query_weight = scatter_about(key_of[6], (MODEL_WIDTH, QUERY_HEADS * HEAD_SIZE), MODEL_WIDTH ** -0.5, 0.1875, ((0, 8), (1, 4)))
    key_matrix = scatter_about(key_of[7], (MODEL_WIDTH, KEY_VALUE_HEADS * HEAD_SIZE), MODEL_WIDTH ** -0.5, 0.1875, ((0, 8), (1, 4)))
    value_matrix = scatter_about(key_of[8], (MODEL_WIDTH, KEY_VALUE_HEADS * HEAD_SIZE), MODEL_WIDTH ** -0.5, 0.1875, ((0, 8), (1, 4)))
    out_weight = scatter_about(key_of[9], (MODEL_WIDTH, QUERY_HEADS * HEAD_SIZE), (QUERY_HEADS * HEAD_SIZE // 16) ** -0.5, 0.75, ((0, 8), (1, 4)))
    ffn_gain = jnp.clip(1.0 + 0.15 * jax.random.normal(key_of[10], (MODEL_WIDTH,), jnp.float32), 0.25, 1.75).astype(jnp.bfloat16)
    router_weight = scatter_about(key_of[11], (MODEL_WIDTH, EXPERTS), (4 * MODEL_WIDTH) ** -0.5, 0.09375, ((0, 8),))
    gate_up_weight = scatter_about(key_of[12], (MODEL_WIDTH, EXPERTS, 2 * FF), MODEL_WIDTH ** -0.5, 0.1875, ((0, 8), (1, 4)))
    down_weight = scatter_about(key_of[13], (MODEL_WIDTH, EXPERTS, FF), (FF // 16) ** -0.5, 1.0, ((0, 8), (1, 4)))
    cotangent = bell_draw_with(key_of[14], (TOKENS, MODEL_WIDTH), 1.0, 6.0, ((0, 32),), (0, 1, 32, 2.75))
    return {"tokens": tokens, "segment": segment, "positions": positions, "parents": parents, "routes": routes, "attn_gain": attn_gain, "query_weight": query_weight, "key_matrix": key_matrix, "value_matrix": value_matrix, "out_weight": out_weight, "ffn_gain": ffn_gain, "router_weight": router_weight, "gate_up_weight": gate_up_weight, "down_weight": down_weight, "cotangent": cotangent}


EPSILON = 1e-06
ROPE_BASE = 10000.0
NEG_FILL = -1e+30

@jax.custom_vjp
def lower_precision(v):
    return lax.optimization_barrier(v.astype(jnp.bfloat16)).astype(jnp.float32)

@jax.custom_vjp
def lower_precision_backward(v):
    return v

def low_keep(v):
    return (lower_precision(v), None)

def low_pass(kept, grad):
    return (grad,)

def back_keep(v):
    return (v, None)

def back_low(kept, grad):
    return (lower_precision(grad),)
lower_precision.defvjp(low_keep, low_pass)
lower_precision_backward.defvjp(back_keep, back_low)

def angle_tables(positions, width):
    half_width = width // 2
    frequency = ROPE_BASE ** (-(jnp.arange(half_width, dtype=jnp.float32) * 2.0) / width)
    turned = positions.astype(jnp.float32)[:, None] * frequency[None, :]
    return (jnp.cos(turned)[:, None, :], jnp.sin(turned)[:, None, :])

def apply_rotation(values, cosine_lookup, sine_lookup):
    half_width = values.shape[-1] // 2
    first_half = values[..., :half_width]
    second_half = values[..., half_width:]
    return jnp.concatenate([first_half * cosine_lookup - second_half * sine_lookup, second_half * cosine_lookup + first_half * sine_lookup], axis=-1)

def rms_scale(values, gain):
    return values * lax.rsqrt(lax.optimization_barrier(jnp.mean(values * values, axis=-1, keepdims=True)) + EPSILON) * gain

def visible(segment, parents):
    seg_ids = jnp.arange(parents.shape[0], dtype=jnp.int32)
    parent_one = lax.optimization_barrier(jnp.sum(jnp.where(segment[:, None] == seg_ids[None, :], parents[None, :], 0), axis=1)).astype(jnp.int32)
    parent_two = lax.optimization_barrier(jnp.sum(jnp.where(parent_one[:, None] == seg_ids[None, :], parents[None, :], 0), axis=1)).astype(jnp.int32)
    key_seg = segment[None, :]
    related = (key_seg == segment[:, None]) | (key_seg == parent_one[:, None]) | (key_seg == parent_two[:, None])
    places = jnp.arange(segment.shape[0], dtype=jnp.int32)
    return related & (places[None, :] <= places[:, None])

def slot_table(route_rows, capacity, experts):
    flat_routes = route_rows.reshape(-1).astype(jnp.int32)
    one_hot = (flat_routes[:, None] == jnp.arange(experts, dtype=jnp.int32)[None, :]).astype(jnp.int32)
    earlier = jnp.cumsum(one_hot, axis=0).astype(jnp.int32) - one_hot
    slot_ranks = lax.optimization_barrier(jnp.sum(earlier * one_hot, axis=1)).astype(jnp.int32)
    slot_ids = flat_routes * capacity + slot_ranks
    entries = flat_routes.shape[0]
    inverse = jnp.full((experts * capacity,), entries, dtype=jnp.int32).at[slot_ids].set(jnp.arange(entries, dtype=jnp.int32))
    return (slot_ids.reshape(route_rows.shape), inverse)

def tree_forward(weight_set, inputs):
    attn_gain, query_weight, key_matrix, value_matrix, out_weight, ffn_gain, router_weight, gate_up_weight, down_weight = weight_set
    tree_rows, segment, positions, parents, route_rows = inputs
    highest_precision = lax.Precision.HIGHEST
    normalized_input = lower_precision(rms_scale(tree_rows, attn_gain))
    cosine_lookup, sine_lookup = angle_tables(positions, HEAD_SIZE)
    queries = lower_precision(apply_rotation(lower_precision_backward(jnp.dot(normalized_input, query_weight, precision=highest_precision)).reshape(TOKENS_PER_TREE, QUERY_HEADS, HEAD_SIZE), cosine_lookup, sine_lookup))
    rotated_keys = lower_precision(apply_rotation(lower_precision_backward(jnp.dot(normalized_input, key_matrix, precision=highest_precision)).reshape(TOKENS_PER_TREE, KEY_VALUE_HEADS, HEAD_SIZE), cosine_lookup, sine_lookup))
    values_lower_precision = lower_precision(lower_precision_backward(jnp.dot(normalized_input, value_matrix, precision=highest_precision))).reshape(TOKENS_PER_TREE, KEY_VALUE_HEADS, HEAD_SIZE)
    gathered_keys = jnp.repeat(rotated_keys, QUERY_HEADS // KEY_VALUE_HEADS, axis=1)
    gathered_values = jnp.repeat(values_lower_precision, QUERY_HEADS // KEY_VALUE_HEADS, axis=1)
    scores = lower_precision_backward(jnp.einsum('qhd,khd->hqk', queries, gathered_keys, precision=highest_precision) * (1.0 / math.sqrt(HEAD_SIZE)))
    scores = jnp.where(visible(segment, parents)[None], scores, NEG_FILL)
    attn_probs = lower_precision(jax.nn.softmax(scores, axis=-1))
    attended = lower_precision(lower_precision_backward(jnp.einsum('hqk,khd->qhd', attn_probs, gathered_values, precision=highest_precision).reshape(TOKENS_PER_TREE, QUERY_HEADS * HEAD_SIZE)))
    mixed_rows = tree_rows + lower_precision_backward(jnp.dot(attended, out_weight.T, precision=highest_precision))
    normed_two = lower_precision(rms_scale(mixed_rows, ffn_gain))
    logits = lower_precision_backward(jnp.dot(normed_two, router_weight, precision=highest_precision))
    gates = jax.nn.softmax(jnp.take_along_axis(logits, route_rows, axis=1), axis=-1)
    slot_ids, inverse = slot_table(route_rows, CAP, EXPERTS)
    padded = jnp.concatenate([normed_two, jnp.zeros((1, MODEL_WIDTH), dtype=jnp.float32)], axis=0)
    expert_rows = padded[inverse // TOP].reshape(EXPERTS, CAP, MODEL_WIDTH)
    gate_up = lower_precision_backward(jnp.einsum('ecd,def->ecf', expert_rows, gate_up_weight, precision=highest_precision))
    hidden = lower_precision(jax.nn.silu(gate_up[..., :FF]) * gate_up[..., FF:])
    expert_out = lower_precision_backward(jnp.einsum('ecf,def->ecd', hidden, down_weight, precision=highest_precision)).reshape(EXPERTS * CAP, MODEL_WIDTH)
    return mixed_rows + lax.optimization_barrier(jnp.sum(gates[:, :, None] * expert_out[slot_ids], axis=1))

def reference(tokens, segment, positions, parents, routes, attn_gain, query_weight, key_matrix, value_matrix, out_weight, ffn_gain, router_weight, gate_up_weight, down_weight, cotangent):
    weight_set = (attn_gain.astype(jnp.float32), query_weight.astype(jnp.float32), key_matrix.astype(jnp.float32), value_matrix.astype(jnp.float32), out_weight.astype(jnp.float32), ffn_gain.astype(jnp.float32), router_weight.astype(jnp.float32), gate_up_weight.astype(jnp.float32), down_weight.astype(jnp.float32))
    tree_rows = tokens.astype(jnp.float32).reshape(TREES, TOKENS_PER_TREE, MODEL_WIDTH)
    tree_inputs = (segment.reshape(TREES, TOKENS_PER_TREE), positions.reshape(TREES, TOKENS_PER_TREE), parents, routes.reshape(TREES, TOKENS_PER_TREE, TOP))
    checked = jax.checkpoint(tree_forward)

    def forward(weights_in, rows_all):

        def advance(carry_in, inputs):
            return (carry_in, checked(weights_in, (inputs[0], inputs[1], inputs[2], inputs[3], inputs[4])))
        _, tree_outs = lax.scan(advance, jnp.zeros((), jnp.float32), (rows_all,) + tree_inputs)
        return tree_outs
    result, pullback = jax.vjp(forward, weight_set, tree_rows)
    weight_grads, row_grads = pullback(cotangent.astype(jnp.float32).reshape(TREES, TOKENS_PER_TREE, MODEL_WIDTH))
    return (result.reshape(TOKENS, MODEL_WIDTH).astype(jnp.bfloat16), row_grads.reshape(TOKENS, MODEL_WIDTH), weight_grads[0], weight_grads[1], weight_grads[2], weight_grads[3], weight_grads[4], weight_grads[5], weight_grads[6], weight_grads[7], weight_grads[8])
```

```python
import math

import jax
import jax.numpy as jnp
from jax import lax
from jax.experimental import pallas as pl
from jax.experimental.pallas import tpu as pltpu
from jax.sharding import PartitionSpec as P

MODEL_WIDTH = 1024
HEAD_SIZE = 64
FF = 512
HALF = FF // 2
EXPERTS = 16
T = 384
LANES = 128
EPSILON = 1e-06
ROPE_BASE = 10000.0
NEG_FILL = -1e30
SCALE = 1.0 / math.sqrt(HEAD_SIZE)
BF = jnp.bfloat16
F32 = jnp.float32

NT = (((1,), (1,)), ((), ()))
TN = (((0,), (0,)), ((), ()))

VM = pl.BlockSpec(memory_space=pltpu.VMEM)
SM = pl.BlockSpec(memory_space=pltpu.SMEM)
ANY = pl.BlockSpec(memory_space=pl.ANY)


def dot(a, b):
    return jnp.dot(a, b, preferred_element_type=F32)


def dotg(a, b, dims, **kw):
    return lax.dot_general(a, b, dims, preferred_element_type=F32, **kw)


def call(body, outs, in_specs, out_specs, scratch, args, name, vmem=48, flops=0):
    nbytes = sum(math.prod(a.shape) * a.dtype.itemsize for a in args)
    nbytes += sum(math.prod(s) * jnp.dtype(d).itemsize for s, d in outs)
    return pl.pallas_call(
        body,
        out_shape=[jax.ShapeDtypeStruct(s, d) for s, d in outs],
        in_specs=in_specs,
        out_specs=out_specs,
        scratch_shapes=scratch,
        compiler_params=pltpu.CompilerParams(vmem_limit_bytes=vmem << 20),
        cost_estimate=pl.CostEstimate(
            flops=int(flops), transcendentals=0, bytes_accessed=int(nbytes)
        ),
        name=name,
    )(*args)


def low_half(shape):
    return lax.broadcasted_iota(jnp.int32, shape, 1) < HEAD_SIZE


def turn(part, cos, sin, first):
    partner = jnp.where(first, pltpu.roll(part, 96, 1), pltpu.roll(part, 32, 1))
    return part * cos + partner * sin


def first_of_head(shape):
    return (lax.broadcasted_iota(jnp.int32, shape, 1) % HEAD_SIZE) < HEAD_SIZE // 2


def attn_fwd(x_ref, gain_ref, w_ref, cos_ref, sin_ref, bias_ref, n1_ref, qkv_ref, att_ref):
    x = x_ref[...].astype(F32)
    r1 = lax.rsqrt(jnp.mean(x * x, axis=1, keepdims=True) + EPSILON)
    n1 = (x * r1 * gain_ref[...]).astype(BF)
    n1_ref[...] = n1
    cos = cos_ref[...]
    sin = sin_ref[...]
    first = first_of_head((T, LANES))
    for b in range(4):
        raw = dot(n1, w_ref[:, b * 512 : (b + 1) * 512])
        for s in range(4):
            part = raw[:, s * LANES : (s + 1) * LANES]
            if s < 3:
                part = turn(part, cos, sin, first)
            qkv_ref[b, :, s * LANES : (s + 1) * LANES] = part.astype(BF)
    low = low_half((LANES, LANES))

    def block(b, carry):
        for c in range(3):
            rows = slice(c * LANES, (c + 1) * LANES)
            seen = (c + 1) * LANES
            keys = qkv_ref[b, :seen, 256:384]
            vals = qkv_ref[b, :seen, 384:512]
            bias = bias_ref[rows, :seen]
            for tile in range(2):
                cols = slice(tile * LANES, (tile + 1) * LANES)
                q = qkv_ref[b, rows, cols]
                parts = []
                for half in range(2):
                    qm = jnp.where(low if half == 0 else ~low, q, jnp.zeros_like(q))
                    s = dotg(qm, keys, NT) * SCALE + bias
                    p = jnp.exp(s - jnp.max(s, axis=1, keepdims=True))
                    p = p * (1.0 / jnp.sum(p, axis=1, keepdims=True))
                    parts.append(dot(p.astype(BF), vals))
                att_ref[b, rows, cols] = jnp.where(low, parts[0], parts[1]).astype(BF)
        return carry

    lax.fori_loop(0, 4, block, 0)


def soft_gates(n2, rt, mask):
    logits = dotg(n2, rt, NT)
    top = jnp.max(jnp.where(mask > 0, logits, NEG_FILL), axis=1, keepdims=True)
    e = jnp.where(mask > 0, jnp.exp(jnp.minimum(logits - top, 0.0)), 0.0)
    return e / jnp.sum(e, axis=1, keepdims=True)


def mid(x_ref, att_ref, wo_ref, gain_ref, rt_ref, mask_ref, h1_ref, n2_ref, gates_ref):
    att = jnp.concatenate([att_ref[b] for b in range(4)], axis=1)
    h1 = x_ref[...].astype(F32) + dotg(att, wo_ref[...], NT)
    h1_ref[...] = h1
    r2 = lax.rsqrt(jnp.mean(h1 * h1, axis=1, keepdims=True) + EPSILON)
    n2 = (h1 * r2 * gain_ref[...]).astype(BF)
    n2_ref[...] = n2
    gates_ref[...] = soft_gates(n2, rt_ref[...], mask_ref[...].astype(F32))


def gate_rest(nx_ref, ny_ref, na_ref, nb_ref, rt_ref, mx_ref, my_ref, md_ref, out_ref):
    rt = rt_ref[...]
    out_ref[0:T] = soft_gates(nx_ref[...], rt, mx_ref[...].astype(F32))
    out_ref[T : 2 * T] = soft_gates(ny_ref[...], rt, my_ref[...].astype(F32))
    nd = jnp.concatenate([na_ref[...], nb_ref[...]], axis=0)
    out_ref[2 * T : 3 * T] = soft_gates(nd, rt, md_ref[...].astype(F32))


ROWS = 4 * T


def expert(e_ref, x0, xx, xy, xa, xb, y0, yx, yy, ya, yb, g0, gr, w0, w1,
           gh_o, dgu_o, dw0_o, dw1_o, dgate_o,
           X, Y, G, W, GH, DGU, DW, si, so):
    half = T // 2
    srcs = [
        (w0, W.at[0]), (w1, W.at[1]),
        (x0, X.at[0:T]), (y0, Y.at[0:T]), (g0, G.at[0:T]), (gr, G.at[T:ROWS]),
        (xx, X.at[T : 2 * T]), (yx, Y.at[T : 2 * T]),
        (xy, X.at[2 * T : 3 * T]), (yy, Y.at[2 * T : 3 * T]),
        (xa, X.at[3 * T : 3 * T + half]), (xb, X.at[3 * T + half : ROWS]),
        (ya, Y.at[3 * T : 3 * T + half]), (yb, Y.at[3 * T + half : ROWS]),
    ]
    copies = [pltpu.make_async_copy(s, d, si.at[i]) for i, (s, d) in enumerate(srcs)]
    for c in copies:
        c.start()
    need = [(0, 1, 2, 3, 4, 5), (6, 7), (8, 9), (10, 11, 12, 13)]
    e = e_ref[0]

    def tree(t, carry):
        for k in range(4):
            @pl.when(t == k)
            def _():
                for i in need[k]:
                    copies[i].wait()
        rows = pl.ds(pl.multiple_of(t * T, T), T)
        xt = X[rows, :]
        yt = Y[rows, :]
        lanes = lax.broadcasted_iota(jnp.int32, (T, LANES), 1)
        gate = jnp.sum(jnp.where(lanes == e, G[rows, :], 0.0), axis=1, keepdims=True)
        dgate = jnp.zeros((T, 1), F32)
        for u in range(2):
            gu = dot(xt, W[u, :, 0 : 2 * HALF])
            dh = dot(yt, W[u, :, 2 * HALF : 3 * HALF])
            g = gu[:, :HALF]
            up = gu[:, HALF:]
            s = 1.0 / (1.0 + jnp.exp(-g))
            silu = g * s
            hid = silu * up
            GH[rows, u * HALF : (u + 1) * HALF] = (gate * hid).astype(BF)
            dgate = dgate + jnp.sum(dh * hid, axis=1, keepdims=True)
            dh = dh * gate
            base = u * 2 * HALF
            DGU[rows, base : base + HALF] = (dh * up * (s * (1.0 + g * (1.0 - s)))).astype(BF)
            DGU[rows, base + HALF : base + 2 * HALF] = (dh * silu).astype(BF)
        dgate_o[rows, :] = jnp.where(lanes == e, dgate, 0.0)
        return carry

    lax.fori_loop(0, 4, tree, 0)
    outs = [pltpu.make_async_copy(GH, gh_o, so.at[0]), pltpu.make_async_copy(DGU, dgu_o, so.at[1])]
    outs[0].start()
    outs[1].start()
    for u in range(2):
        DW[u, :, 0 : 2 * HALF] = dotg(X[...], DGU[:, u * 2 * HALF : (u + 1) * 2 * HALF], TN).astype(BF)
        DW[u, :, 2 * HALF : 3 * HALF] = dotg(Y[...], GH[:, u * HALF : (u + 1) * HALF], TN).astype(BF)
        o = pltpu.make_async_copy(DW.at[u], (dw1_o if u else dw0_o), so.at[2 + u])
        o.start()
        outs.append(o)
    for o in outs:
        o.wait()


def run_expert(e, xs, ys, gs, w0, w1):
    args = (e, *xs, *ys, *gs, w0, w1)
    rows = MODEL_WIDTH
    return call(
        expert,
        [((ROWS, FF), BF), ((ROWS, 2 * FF), BF), ((rows, 3 * HALF), BF), ((rows, 3 * HALF), BF),
         ((ROWS, LANES), F32)],
        [SM] + [ANY] * 14,
        [ANY] * 4 + [VM],
        [
            pltpu.VMEM((ROWS, MODEL_WIDTH), BF), pltpu.VMEM((ROWS, MODEL_WIDTH), BF),
            pltpu.VMEM((ROWS, LANES), F32), pltpu.VMEM((2, rows, 3 * HALF), BF),
            pltpu.VMEM((ROWS, FF), BF), pltpu.VMEM((ROWS, 2 * FF), BF),
            pltpu.VMEM((2, rows, 3 * HALF), BF),
            pltpu.SemaphoreType.DMA((14,)), pltpu.SemaphoreType.DMA((4,)),
        ],
        args, "expert", 56, 2 * ROWS * rows * 3 * FF * 2,
    )


def back_body(lo, m, width, first_col, splits, n):
    def body(*refs):
        acts = refs[0:4]
        ws = refs[4:12]
        outs = refs[12 : 12 + n]
        A, W, sem = refs[12 + n :]
        copies = []
        for k in range(4):
            for u in range(2):
                i = 2 * k + u
                a = acts[k].at[lo : lo + m, u * width : (u + 1) * width]
                w = ws[i].at[:, first_col : first_col + width]
                h, j = i // 4, i % 4
                copies.append((
                    pltpu.make_async_copy(a, A.at[h, :, j * width : (j + 1) * width], sem.at[0, i]),
                    pltpu.make_async_copy(w, W.at[h, :, j * width : (j + 1) * width], sem.at[1, i]),
                ))
        for a, w in copies:
            a.start()
            w.start()
        for a, w in copies[:4]:
            a.wait()
            w.wait()
        total = dotg(A[0], W[0], NT)
        for a, w in copies[4:]:
            a.wait()
            w.wait()
        total = total + dotg(A[1], W[1], NT)
        for o, (r0, r1) in zip(outs, splits):
            o[...] = total[r0:r1].astype(o.dtype)
    return body


def run_back(acts, ws, lo, m, width, first_col, splits, dtypes, name):
    return call(
        back_body(lo, m, width, first_col, splits, len(splits)),
        [((r1 - r0, MODEL_WIDTH), d) for (r0, r1), d in zip(splits, dtypes)],
        [ANY] * 12,
        [VM] * len(splits),
        [
            pltpu.VMEM((2, m, 4 * width), BF), pltpu.VMEM((2, MODEL_WIDTH, 4 * width), BF),
            pltpu.SemaphoreType.DMA((2, 8)),
        ],
        (*acts, *ws), name, 48, 2 * m * MODEL_WIDTH * 8 * width,
    )


def columns_of(rowwise, lane):
    ones = jnp.ones((T, LANES), F32)
    total = dotg(rowwise, ones, TN, precision=lax.Precision.HIGHEST)
    lanes = lax.broadcasted_iota(jnp.int32, total.shape, 1)
    return jnp.where(lanes == lane, total, 0.0)


def join(p_ref, rx_ref, ry_ref, g0_ref, gx_ref, gy_ref, gd_ref, gates_ref, h1_ref, n2_ref,
         gain_ref, rt_ref, dy_ref, wo_ref, att_ref, dh1_ref, datt_ref, dwo_ref):
    gates = gates_ref[...]
    dg = g0_ref[...] + gx_ref[...] + gy_ref[...] + gd_ref[...]
    dl = (gates * (dg - jnp.sum(gates * dg, axis=1, keepdims=True))).astype(BF)
    dn2 = p_ref[...] + rx_ref[...].astype(F32) + ry_ref[...].astype(F32) + dot(dl, rt_ref[...])
    h1 = h1_ref[...]
    gain = gain_ref[...]
    r2 = lax.rsqrt(jnp.mean(h1 * h1, axis=1, keepdims=True) + EPSILON)
    gd = gain * dn2
    inner = jnp.mean(gd * h1, axis=1, keepdims=True)
    dh1 = dy_ref[...].astype(F32) + r2 * gd - h1 * (r2 * r2 * r2 * inner)
    dh1_ref[...] = dh1
    db = dh1.astype(BF)
    for b in range(4):
        cols = slice(b * 256, (b + 1) * 256)
        datt_ref[b] = dot(db, wo_ref[:, cols]).astype(BF)
        dwo_ref[:, cols] = dotg(db, att_ref[b], TN).astype(BF)
    extra = dotg(n2_ref[...], dl, TN) + columns_of(dn2 * h1 * r2, EXPERTS)
    dwo_ref[:, 1024:1152] = extra.astype(BF)


def attn_bwd(x_ref, gain_ref, w_ref, cos_ref, sin_ref, bias_ref, n1_ref, qkv_ref, datt_ref, dh1_ref,
             dx_ref, dw_ref, dqkv, dk, dv):
    low = low_half((LANES, LANES))
    first = first_of_head((T, LANES))

    def block(b, carry):
        dk[...] = jnp.zeros_like(dk)
        dv[...] = jnp.zeros_like(dv)
        for c in range(3):
            rows = slice(c * LANES, (c + 1) * LANES)
            seen = (c + 1) * LANES
            keys = qkv_ref[b, :seen, 256:384]
            vals = qkv_ref[b, :seen, 384:512]
            bias = bias_ref[rows, :seen]
            cos = cos_ref[rows, :]
            sin = sin_ref[rows, :]
            for tile in range(2):
                cols = slice(tile * LANES, (tile + 1) * LANES)
                q = qkv_ref[b, rows, cols]
                do = datt_ref[b, rows, cols]
                dq = []
                for half in range(2):
                    keep = low if half == 0 else ~low
                    qm = jnp.where(keep, q, jnp.zeros_like(q))
                    dm = jnp.where(keep, do, jnp.zeros_like(do))
                    s = dotg(qm, keys, NT) * SCALE + bias
                    p = jnp.exp(s - jnp.max(s, axis=1, keepdims=True))
                    p = p * (1.0 / jnp.sum(p, axis=1, keepdims=True))
                    dp = dotg(dm, vals, NT)
                    ds = (p * (dp - jnp.sum(p * dp, axis=1, keepdims=True))).astype(BF)
                    dq.append(dot(ds, keys))
                    dk[:seen] += dotg(ds, qm, TN)
                    dv[:seen] += dotg(p.astype(BF), dm, TN)
                dqt = jnp.where(low, dq[0], dq[1]) * SCALE
                dqkv[b, rows, cols] = turn(dqt, cos, -sin, first[rows]).astype(BF)
        dqkv[b, :, 256:384] = turn(dk[...] * SCALE, cos_ref[...], -sin_ref[...], first).astype(BF)
        dqkv[b, :, 384:512] = dv[...].astype(BF)
        return carry

    lax.fori_loop(0, 4, block, 0)
    n1 = n1_ref[...]
    dn1 = jnp.zeros((T, MODEL_WIDTH), F32)
    for b in range(4):
        cols = slice(b * 512, (b + 1) * 512)
        dw_ref[:, cols] = dotg(n1, dqkv[b], TN).astype(BF)
        dn1 = dn1 + dotg(dqkv[b], w_ref[:, cols], NT)
    x = x_ref[...].astype(F32)
    gain = gain_ref[...]
    r1 = lax.rsqrt(jnp.mean(x * x, axis=1, keepdims=True) + EPSILON)
    gd = gain * dn1
    inner = jnp.mean(gd * x, axis=1, keepdims=True)
    dx_ref[...] = dh1_ref[...] + r1 * gd - x * (r1 * r1 * r1 * inner)
    dw_ref[:, 2048:2176] = columns_of(dn1 * x * r1, 0).astype(BF)


def visible_bias(segment, parents):
    ids = jnp.arange(parents.shape[0], dtype=jnp.int32)
    one = jnp.sum(jnp.where(segment[:, None] == ids[None, :], parents[None, :], 0), axis=1)
    two = jnp.sum(jnp.where(one[:, None] == ids[None, :], parents[None, :], 0), axis=1)
    key = segment[None, :]
    related = (key == segment[:, None]) | (key == one[:, None]) | (key == two[:, None])
    places = jnp.arange(segment.shape[0], dtype=jnp.int32)
    return jnp.where(related & (places[None, :] <= places[:, None]), 0.0, NEG_FILL).astype(F32)


def turn_tables(positions):
    half = HEAD_SIZE // 2
    lane = jnp.arange(LANES, dtype=jnp.int32)
    frequency = ROPE_BASE ** (-((lane % half).astype(F32) * 2.0) / HEAD_SIZE)
    angle = positions.astype(F32)[:, None] * frequency[None, :]
    sign = jnp.where(lane % HEAD_SIZE < half, -1.0, 1.0).astype(F32)
    return jnp.cos(angle), jnp.sin(angle) * sign[None, :]


def make_shards(groups, fsdp):
    ring = list(range(0, groups, 1))
    if groups == 4:
        ring = [0, 1, 3, 2]
    place = [ring.index(g) for g in range(groups)]
    rest = fsdp // 8

    def shifted(k):
        return [(ring[p], ring[(p + k) % groups]) for p in range(groups)]

    def flip(bits):
        return [(i, i ^ bits) for i in range(fsdp)]

    low_groups = None if rest == 1 else [[8 * r + j for j in range(8)] for r in range(rest)]
    rest_groups = [[8 * r + j for r in range(rest)] for j in range(8)]

    def z_next(a):
        return lax.ppermute(a, "grp", shifted(1))

    def to_x(a):
        return lax.ppermute(a, "fsdp", flip(2))

    def to_y(a):
        return lax.ppermute(a, "fsdp", flip(4))

    def to_diag(a):
        return lax.ppermute(a, "fsdp", flip(6))

    def to_core(a):
        return lax.ppermute(a, "fsdp", flip(1))

    def plane(a):
        half = a.shape[0] // 2
        ax = to_x(a)
        ay = to_y(a)
        return (a, ax, ay, to_x(ay[:half]), to_y(ax[half:]))

    def z_sum(blocks):
        total = blocks[0].astype(F32)
        for k in range(1, groups):
            total = total + lax.ppermute(blocks[k], "grp", shifted(groups - k)).astype(F32)
        return total

    def shards(tokens, segment, positions, parents, routes, attn_gain, query_weight, key_matrix,
               value_matrix, out_weight, ffn_gain, router_weight, gate_up_weight, down_weight, cotangent):
        dr = query_weight.shape[0]
        mine = lax.axis_index("fsdp")
        spot = jnp.array(place, jnp.int32)[lax.axis_index("grp")]
        ring_ids = jnp.array(ring, jnp.int32)

        def swapped(w):
            return [w[:, 0:64], w[:, 128:192], w[:, 64:128], w[:, 192:256]]

        own_qkv = jnp.concatenate(swapped(query_weight) + [key_matrix, value_matrix], axis=1)
        own_out = jnp.concatenate(swapped(out_weight), axis=1)

        def z_gather(a):
            got = [a]
            for _ in range(groups - 1):
                got.append(z_next(got[-1]))
            return got

        w_qkv = lax.all_gather(jnp.concatenate(z_gather(own_qkv), axis=1), "fsdp", axis=0, tiled=True)
        w_out = lax.all_gather(jnp.concatenate(z_gather(own_out), axis=1), "fsdp", axis=0, tiled=True)
        small = jnp.concatenate([router_weight.T, attn_gain[None], ffn_gain[None]], axis=0)
        small = lax.all_gather(small, "fsdp", axis=1, tiled=True)
        router_t = jnp.concatenate([small[:16], jnp.zeros((LANES - 16, MODEL_WIDTH), BF)], axis=0)
        gain_one = small[16:17].astype(F32)
        gain_two = small[17:18].astype(F32)

        gu = gate_up_weight.reshape(dr, 4, 2, 2, HALF)
        dn = down_weight.reshape(dr, 4, 1, 2, HALF)
        parts = jnp.concatenate([gu, dn], axis=2)
        parts = jnp.transpose(parts, (1, 3, 0, 2, 4)).reshape(8, dr, 3 * HALF)
        unit = lax.all_to_all(parts, "fsdp", 0, 0, axis_index_groups=low_groups)
        unit = unit.reshape(8 * dr, 3 * HALF)
        if rest > 1:
            unit = lax.all_gather(unit, "fsdp", axis=0, tiled=True, axis_index_groups=rest_groups)
        units = z_gather(unit)
        pairs = [(u, to_core(u)) for u in units]

        bias = visible_bias(segment, parents[0])
        cos, sin = turn_tables(positions)
        lanes = jnp.arange(LANES, dtype=jnp.int32)
        mask = jnp.sum((routes[:, :, None] == lanes[None, None, :]).astype(F32), axis=1).astype(BF)
        mask_rest = (to_x(mask), to_y(mask), to_diag(mask))
        dys = plane(cotangent)

        n1, qkv, att = call(
            attn_fwd,
            [((T, MODEL_WIDTH), BF), ((4, T, 512), BF), ((4, T, 256), BF)],
            [VM] * 6, [VM] * 3, [],
            (tokens, gain_one, w_qkv, cos, sin, bias), "attn_fwd", 48, 3.0e9,
        )
        h1, n2, gates = call(
            mid,
            [((T, MODEL_WIDTH), F32), ((T, MODEL_WIDTH), BF), ((T, LANES), F32)],
            [VM] * 6, [VM] * 3, [],
            (tokens, att, w_out, gain_two, router_t, mask), "mid", 48, 1.0e9,
        )
        xs = plane(n2)
        gates_rest, = call(
            gate_rest, [((3 * T, LANES), F32)], [VM] * 8, [VM], [],
            (*xs[1:], router_t, *mask_rest), "gate_rest", 48, 0.4e9,
        )

        chip = (mine // 2) % 4
        order = list(range(1, groups)) + [0]
        done = {}
        ring_acc = None
        for k in order:
            e = (4 * ring_ids[(spot - k) % groups] + chip).astype(jnp.int32).reshape(1)
            gh, dgu, dw_own, dw_sib, dgate = run_expert(e, xs, dys, (gates, gates_rest), *pairs[k])
            got = to_core(dw_sib)
            grad = dw_own.astype(F32) + got.astype(F32)
            if ring_acc is not None:
                grad = grad + z_next(ring_acc).astype(F32)
            ring_acc = grad.astype(BF)
            done[k] = (gh, dgu, dgate)
        ghs = [done[k][0] for k in range(groups)]
        dgus = [done[k][1] for k in range(groups)]
        dgate = sum(done[k][2] for k in range(groups))
        ws = [w for pair in pairs for w in pair]
        half = T // 2
        whole = ((0, T),)
        split = ((0, half), (half, T))

        def spread(acts, width, first_col, name):
            da, db = run_back(acts, ws, 3 * T, T, width, first_col, split, (BF, BF), name + "_d")
            ra = to_x(da)
            rb = to_y(db)
            xa, xb, ya, yb = run_back(
                acts, ws, T, 2 * T, width, first_col,
                ((0, half), (half, T), (T, T + half), (T + half, 2 * T)), (BF,) * 4, name + "_xy",
            )
            own, = run_back(acts, ws, 0, T, width, first_col, whole, (F32,), name + "_o")
            xb = (xb.astype(F32) + rb.astype(F32)).astype(BF)
            ya = (ya.astype(F32) + ra.astype(F32)).astype(BF)
            rx = jnp.concatenate([to_x(xa), to_x(xb)], axis=0)
            ry = jnp.concatenate([to_y(ya), to_y(yb)], axis=0)
            return own, rx, ry

        gate_parts = (
            dgate[:T], to_x(dgate[T : 2 * T]), to_y(dgate[2 * T : 3 * T]), to_diag(dgate[3 * T :]),
        )
        p_n2, rx_n2, ry_n2 = spread(dgus, 2 * HALF, 0, "dn2")
        dh1, datt, dwo = call(
            join,
            [((T, MODEL_WIDTH), F32), ((4, T, 256), BF), ((MODEL_WIDTH, 1152), BF)],
            [VM] * 15, [VM] * 3, [],
            (p_n2, rx_n2, ry_n2, *gate_parts, gates, h1, n2, gain_two, router_t, cotangent, w_out, att),
            "join", 48, 2.0e9,
        )
        dx, dwqkv = call(
            attn_bwd,
            [((T, MODEL_WIDTH), F32), ((MODEL_WIDTH, 2176), BF)],
            [VM] * 10, [VM] * 2,
            [pltpu.VMEM((4, T, 512), BF), pltpu.VMEM((T, LANES), F32), pltpu.VMEM((T, LANES), F32)],
            (tokens, gain_one, w_qkv, cos, sin, bias, n1, qkv, datt, dh1), "attn_bwd", 48, 6.0e9,
        )

        p_out, rx_out, ry_out = spread(ghs, HALF, 2 * HALF, "out")
        output = (h1 + p_out + rx_out.astype(F32) + ry_out.astype(F32)).astype(BF)

        if rest > 1:
            ring_acc = lax.psum_scatter(
                ring_acc, "fsdp", scatter_dimension=0, tiled=True, axis_index_groups=rest_groups
            )
        back = lax.all_to_all(ring_acc.reshape(8, dr, 3 * HALF), "fsdp", 0, 0, axis_index_groups=low_groups)
        back = back.astype(F32).reshape(4, 2, dr, 3, HALF)
        back = jnp.transpose(back, (2, 0, 3, 1, 4))
        gate_up_grad = back[:, :, :2].reshape(dr, 4, 2 * FF)
        down_grad = back[:, :, 2].reshape(dr, 4, FF)

        rs_out = lax.psum_scatter(dwo, "fsdp", scatter_dimension=0, tiled=True)
        rs_qkv = lax.psum_scatter(dwqkv, "fsdp", scatter_dimension=0, tiled=True)
        z_out = z_sum([
            jnp.concatenate([rs_out[:, k * 256 : (k + 1) * 256], rs_out[:, 1024:]], axis=1)
            for k in range(groups)
        ])
        z_qkv = z_sum([
            jnp.concatenate([rs_qkv[:, k * 512 : (k + 1) * 512], rs_qkv[:, 2048:]], axis=1)
            for k in range(groups)
        ])
        return (
            output,
            dx,
            z_qkv[:, 512],
            jnp.concatenate(swapped(z_qkv[:, :256]), axis=1),
            z_qkv[:, 256:384],
            z_qkv[:, 384:512],
            jnp.concatenate(swapped(z_out[:, :256]), axis=1),
            z_out[:, 256 + EXPERTS],
            z_out[:, 256 : 256 + EXPERTS],
            gate_up_grad,
            down_grad,
        )

    return shards


def solution(mesh):
    both = ("grp", "fsdp")
    in_specs = (
        P(both, None), P(both), P(both), P(both, None), P(both, None),
        P("fsdp"), P("fsdp", "grp"), P("fsdp", "grp"), P("fsdp", "grp"), P("fsdp", "grp"),
        P("fsdp"), P("fsdp", None), P("fsdp", "grp", None), P("fsdp", "grp", None), P(both, None),
    )
    out_specs = (
        P(both, None), P(both, None), P("fsdp"),
        P("fsdp", "grp"), P("fsdp", "grp"), P("fsdp", "grp"), P("fsdp", "grp"),
        P("fsdp"), P("fsdp", None), P("fsdp", "grp", None), P("fsdp", "grp", None),
    )
    shards = make_shards(mesh.shape["grp"], mesh.shape["fsdp"])
    return jax.shard_map(shards, mesh=mesh, in_specs=in_specs, out_specs=out_specs, check_vma=False)
```

```python
import math

import jax
import jax.numpy as jnp
from jax import lax
from jax.experimental import pallas as pl
from jax.experimental.pallas import tpu as pltpu
from jax.sharding import PartitionSpec as P

MODEL_WIDTH = 1024
HEAD_SIZE = 64
FF = 512
HALF = FF // 2
EXPERTS = 16
T = 384
LANES = 128
EPSILON = 1e-06
ROPE_BASE = 10000.0
NEG_FILL = -1e30
SCALE = 1.0 / math.sqrt(HEAD_SIZE)
BF = jnp.bfloat16
F32 = jnp.float32
COST = 0.02

NT = (((1,), (1,)), ((), ()))
TN = (((0,), (0,)), ((), ()))

VM = pl.BlockSpec(memory_space=pltpu.VMEM)
SM = pl.BlockSpec(memory_space=pltpu.SMEM)
ANY = pl.BlockSpec(memory_space=pl.ANY)


def dot(a, b):
    return jnp.dot(a, b, preferred_element_type=F32)


def dotg(a, b, dims, **kw):
    return lax.dot_general(a, b, dims, preferred_element_type=F32, **kw)


def call(body, outs, in_specs, out_specs, scratch, args, name, vmem=48, flops=0):
    nbytes = sum(math.prod(a.shape) * a.dtype.itemsize for a in args)
    nbytes += sum(math.prod(s) * jnp.dtype(d).itemsize for s, d in outs)
    return pl.pallas_call(
        body,
        out_shape=[jax.ShapeDtypeStruct(s, d) for s, d in outs],
        in_specs=in_specs,
        out_specs=out_specs,
        scratch_shapes=scratch,
        compiler_params=pltpu.CompilerParams(vmem_limit_bytes=vmem << 20),
        cost_estimate=pl.CostEstimate(
            flops=int(flops * COST), transcendentals=0, bytes_accessed=int(nbytes * COST)
        ),
        name=name,
    )(*args)


def after(x, *deps):
    return lax.optimization_barrier((x, *deps))[0]


def low_half(shape):
    return lax.broadcasted_iota(jnp.int32, shape, 1) < HEAD_SIZE


def turn(part, cos, sin, first):
    partner = jnp.where(first, pltpu.roll(part, 96, 1), pltpu.roll(part, 32, 1))
    return part * cos + partner * sin


def first_of_head(shape):
    return (lax.broadcasted_iota(jnp.int32, shape, 1) % HEAD_SIZE) < HEAD_SIZE // 2


def attn_fwd(x_ref, gain_ref, w_ref, cos_ref, sin_ref, bias_ref, n1_ref, qkv_ref, att_ref):
    x = x_ref[...].astype(F32)
    r1 = lax.rsqrt(jnp.mean(x * x, axis=1, keepdims=True) + EPSILON)
    n1 = (x * r1 * gain_ref[...]).astype(BF)
    n1_ref[...] = n1
    cos = cos_ref[...]
    sin = sin_ref[...]
    first = first_of_head((T, LANES))
    for b in range(4):
        raw = dot(n1, w_ref[:, b * 512 : (b + 1) * 512])
        for s in range(4):
            part = raw[:, s * LANES : (s + 1) * LANES]
            if s < 3:
                part = turn(part, cos, sin, first)
            qkv_ref[b, :, s * LANES : (s + 1) * LANES] = part.astype(BF)
    low = low_half((LANES, LANES))

    def block(b, carry):
        for c in range(3):
            rows = slice(c * LANES, (c + 1) * LANES)
            seen = (c + 1) * LANES
            keys = qkv_ref[b, :seen, 256:384]
            vals = qkv_ref[b, :seen, 384:512]
            bias = bias_ref[rows, :seen]
            for tile in range(2):
                cols = slice(tile * LANES, (tile + 1) * LANES)
                q = qkv_ref[b, rows, cols]
                parts = []
                for half in range(2):
                    qm = jnp.where(low if half == 0 else ~low, q, jnp.zeros_like(q))
                    s = dotg(qm, keys, NT) * SCALE + bias
                    p = jnp.exp(s - jnp.max(s, axis=1, keepdims=True))
                    p = p * (1.0 / jnp.sum(p, axis=1, keepdims=True))
                    parts.append(dot(p.astype(BF), vals))
                att_ref[b, rows, cols] = jnp.where(low, parts[0], parts[1]).astype(BF)
        return carry

    lax.fori_loop(0, 4, block, 0)


def soft_gates(n2, rt, mask):
    logits = dotg(n2, rt, NT)
    top = jnp.max(jnp.where(mask > 0, logits, NEG_FILL), axis=1, keepdims=True)
    e = jnp.where(mask > 0, jnp.exp(jnp.minimum(logits - top, 0.0)), 0.0)
    return e / jnp.sum(e, axis=1, keepdims=True)


def mid(x_ref, att_ref, wo_ref, gain_ref, rt_ref, mask_ref, h1_ref, n2_ref, gates_ref):
    att = jnp.concatenate([att_ref[b] for b in range(4)], axis=1)
    h1 = x_ref[...].astype(F32) + dotg(att, wo_ref[...], NT)
    h1_ref[...] = h1
    r2 = lax.rsqrt(jnp.mean(h1 * h1, axis=1, keepdims=True) + EPSILON)
    n2 = (h1 * r2 * gain_ref[...]).astype(BF)
    n2_ref[...] = n2
    gates_ref[...] = soft_gates(n2, rt_ref[...], mask_ref[...].astype(F32))


def gate_rest(nx_ref, ny_ref, na_ref, nb_ref, rt_ref, mx_ref, my_ref, md_ref, out_ref):
    rt = rt_ref[...]
    out_ref[0:T] = soft_gates(nx_ref[...], rt, mx_ref[...].astype(F32))
    out_ref[T : 2 * T] = soft_gates(ny_ref[...], rt, my_ref[...].astype(F32))
    nd = jnp.concatenate([na_ref[...], nb_ref[...]], axis=0)
    out_ref[2 * T : 3 * T] = soft_gates(nd, rt, md_ref[...].astype(F32))


ROWS = 4 * T


def expert(e_ref, x0, xx, xy, xa, xb, y0, yx, yy, ya, yb, g0, gr, w0, w1, dgate_i,
           gh_o, dgu_o, dw0_o, dw1_o, dgate_o,
           X, Y, G, W, GH, DGU, DW, si, so):
    half = T // 2
    srcs = [
        (w0, W.at[0]), (w1, W.at[1]),
        (x0, X.at[0:T]), (y0, Y.at[0:T]), (g0, G.at[0:T]), (gr, G.at[T:ROWS]),
        (xx, X.at[T : 2 * T]), (yx, Y.at[T : 2 * T]),
        (xy, X.at[2 * T : 3 * T]), (yy, Y.at[2 * T : 3 * T]),
        (xa, X.at[3 * T : 3 * T + half]), (xb, X.at[3 * T + half : ROWS]),
        (ya, Y.at[3 * T : 3 * T + half]), (yb, Y.at[3 * T + half : ROWS]),
    ]
    copies = [pltpu.make_async_copy(s, d, si.at[i]) for i, (s, d) in enumerate(srcs)]
    for c in copies:
        c.start()
    need = [(0, 1, 2, 3, 4, 5), (6, 7), (8, 9), (10, 11, 12, 13)]
    e = e_ref[0]

    def tree(t, carry):
        for k in range(4):
            @pl.when(t == k)
            def _():
                for i in need[k]:
                    copies[i].wait()
        rows = pl.ds(pl.multiple_of(t * T, T), T)
        xt = X[rows, :]
        yt = Y[rows, :]
        lanes = lax.broadcasted_iota(jnp.int32, (T, LANES), 1)
        gate = jnp.sum(jnp.where(lanes == e, G[rows, :], 0.0), axis=1, keepdims=True)
        dgate = jnp.zeros((T, 1), F32)
        for u in range(2):
            gu = dot(xt, W[u, :, 0 : 2 * HALF])
            dh = dot(yt, W[u, :, 2 * HALF : 3 * HALF])
            g = gu[:, :HALF]
            up = gu[:, HALF:]
            s = 1.0 / (1.0 + jnp.exp(-g))
            silu = g * s
            hid = silu * up
            GH[rows, u * HALF : (u + 1) * HALF] = (gate * hid).astype(BF)
            dgate = dgate + jnp.sum(dh * hid, axis=1, keepdims=True)
            dh = dh * gate
            base = u * 2 * HALF
            DGU[rows, base : base + HALF] = (dh * up * (s * (1.0 + g * (1.0 - s)))).astype(BF)
            DGU[rows, base + HALF : base + 2 * HALF] = (dh * silu).astype(BF)
        dgate_o[rows, :] = dgate_i[rows, :] + jnp.where(lanes == e, dgate, 0.0)
        return carry

    lax.fori_loop(0, 4, tree, 0)
    outs = [pltpu.make_async_copy(GH, gh_o, so.at[0]), pltpu.make_async_copy(DGU, dgu_o, so.at[1])]
    outs[0].start()
    outs[1].start()
    for u in range(2):
        DW[u, :, 0 : 2 * HALF] = dotg(X[...], DGU[:, u * 2 * HALF : (u + 1) * 2 * HALF], TN).astype(BF)
        DW[u, :, 2 * HALF : 3 * HALF] = dotg(Y[...], GH[:, u * HALF : (u + 1) * HALF], TN).astype(BF)
        o = pltpu.make_async_copy(DW.at[u], (dw1_o if u else dw0_o), so.at[2 + u])
        o.start()
        outs.append(o)
    for o in outs:
        o.wait()


def run_expert(e, xs, ys, gs, w0, w1, dgate):
    args = (e, *xs, *ys, *gs, w0, w1, dgate)
    rows = MODEL_WIDTH
    return call(
        expert,
        [((ROWS, FF), BF), ((ROWS, 2 * FF), BF), ((rows, 3 * HALF), BF), ((rows, 3 * HALF), BF),
         ((ROWS, LANES), F32)],
        [SM] + [ANY] * 14 + [VM],
        [ANY] * 4 + [VM],
        [
            pltpu.VMEM((ROWS, MODEL_WIDTH), BF), pltpu.VMEM((ROWS, MODEL_WIDTH), BF),
            pltpu.VMEM((ROWS, LANES), F32), pltpu.VMEM((2, rows, 3 * HALF), BF),
            pltpu.VMEM((ROWS, FF), BF), pltpu.VMEM((ROWS, 2 * FF), BF),
            pltpu.VMEM((2, rows, 3 * HALF), BF),
            pltpu.SemaphoreType.DMA((14,)), pltpu.SemaphoreType.DMA((4,)),
        ],
        args, "expert", 56, 2 * ROWS * rows * 3 * FF * 2,
    )


def back_body(lo, m, width, first_col, splits, n, tail):
    def body(*refs):
        acts = refs[0:4]
        ws = refs[4:12]
        outs = refs[12 + tail : 12 + tail + n]
        A, W, sem = refs[12 + tail + n :]
        copies = []
        for k in range(4):
            for u in range(2):
                i = 2 * k + u
                a = acts[k].at[lo : lo + m, u * width : (u + 1) * width]
                w = ws[i].at[:, first_col : first_col + width]
                h, j = i // 4, i % 4
                copies.append((
                    pltpu.make_async_copy(a, A.at[h, :, j * width : (j + 1) * width], sem.at[0, i]),
                    pltpu.make_async_copy(w, W.at[h, :, j * width : (j + 1) * width], sem.at[1, i]),
                ))
        for a, w in copies:
            a.start()
            w.start()
        for a, w in copies[:4]:
            a.wait()
            w.wait()
        total = dotg(A[0], W[0], NT)
        for a, w in copies[4:]:
            a.wait()
            w.wait()
        total = total + dotg(A[1], W[1], NT)
        for o, (r0, r1) in zip(outs, splits):
            o[:, 0:MODEL_WIDTH] = total[r0:r1].astype(o.dtype)
            if tail:
                o[:, MODEL_WIDTH:] = refs[12][lo + r0 : lo + r1, :].astype(o.dtype)
    return body


def run_back(acts, ws, extra, lo, m, width, first_col, splits, dtypes, name):
    cols = MODEL_WIDTH + (0 if extra is None else LANES)
    extras = () if extra is None else (extra,)
    return call(
        back_body(lo, m, width, first_col, splits, len(splits), len(extras)),
        [((r1 - r0, cols), d) for (r0, r1), d in zip(splits, dtypes)],
        [ANY] * 12 + [VM] * len(extras),
        [VM] * len(splits),
        [
            pltpu.VMEM((2, m, 4 * width), BF), pltpu.VMEM((2, MODEL_WIDTH, 4 * width), BF),
            pltpu.SemaphoreType.DMA((2, 8)),
        ],
        (*acts, *ws, *extras), name, 48, 2 * m * MODEL_WIDTH * 8 * width,
    )


def columns_of(rowwise, lane):
    ones = jnp.ones((T, LANES), F32)
    total = dotg(rowwise, ones, TN, precision=lax.Precision.HIGHEST)
    lanes = lax.broadcasted_iota(jnp.int32, total.shape, 1)
    return jnp.where(lanes == lane, total, 0.0)


def join(p_ref, rxa_ref, rxb_ref, rya_ref, ryb_ref, gates_ref, h1_ref, n2_ref,
         gain_ref, rt_ref, dy_ref, wo_ref, att_ref, dh1_ref, datt_ref, dwo_ref):
    gates = gates_ref[...]
    rx = jnp.concatenate([rxa_ref[...], rxb_ref[...]], axis=0).astype(F32)
    ry = jnp.concatenate([rya_ref[...], ryb_ref[...]], axis=0).astype(F32)
    total = p_ref[...] + rx + ry
    dg = total[:, MODEL_WIDTH:]
    dl = (gates * (dg - jnp.sum(gates * dg, axis=1, keepdims=True))).astype(BF)
    dn2 = total[:, :MODEL_WIDTH] + dot(dl, rt_ref[...])
    h1 = h1_ref[...]
    gain = gain_ref[...]
    r2 = lax.rsqrt(jnp.mean(h1 * h1, axis=1, keepdims=True) + EPSILON)
    gd = gain * dn2
    inner = jnp.mean(gd * h1, axis=1, keepdims=True)
    dh1 = dy_ref[...].astype(F32) + r2 * gd - h1 * (r2 * r2 * r2 * inner)
    dh1_ref[...] = dh1
    db = dh1.astype(BF)
    for b in range(4):
        cols = slice(b * 256, (b + 1) * 256)
        datt_ref[b] = dot(db, wo_ref[:, cols]).astype(BF)
        dwo_ref[:, cols] = dotg(db, att_ref[b], TN).astype(BF)
    extra = dotg(n2_ref[...], dl, TN) + columns_of(dn2 * h1 * r2, EXPERTS)
    dwo_ref[:, 1024:1152] = extra.astype(BF)


def attn_bwd(x_ref, gain_ref, w_ref, cos_ref, sin_ref, bias_ref, n1_ref, qkv_ref, datt_ref, dh1_ref,
             dx_ref, dw_ref, dqkv, dk, dv):
    low = low_half((LANES, LANES))
    first = first_of_head((T, LANES))

    def block(b, carry):
        dk[...] = jnp.zeros_like(dk)
        dv[...] = jnp.zeros_like(dv)
        for c in range(3):
            rows = slice(c * LANES, (c + 1) * LANES)
            seen = (c + 1) * LANES
            keys = qkv_ref[b, :seen, 256:384]
            vals = qkv_ref[b, :seen, 384:512]
            bias = bias_ref[rows, :seen]
            cos = cos_ref[rows, :]
            sin = sin_ref[rows, :]
            for tile in range(2):
                cols = slice(tile * LANES, (tile + 1) * LANES)
                q = qkv_ref[b, rows, cols]
                do = datt_ref[b, rows, cols]
                dq = []
                for half in range(2):
                    keep = low if half == 0 else ~low
                    qm = jnp.where(keep, q, jnp.zeros_like(q))
                    dm = jnp.where(keep, do, jnp.zeros_like(do))
                    s = dotg(qm, keys, NT) * SCALE + bias
                    p = jnp.exp(s - jnp.max(s, axis=1, keepdims=True))
                    p = p * (1.0 / jnp.sum(p, axis=1, keepdims=True))
                    dp = dotg(dm, vals, NT)
                    ds = (p * (dp - jnp.sum(p * dp, axis=1, keepdims=True))).astype(BF)
                    dq.append(dot(ds, keys))
                    dk[:seen] += dotg(ds, qm, TN)
                    dv[:seen] += dotg(p.astype(BF), dm, TN)
                dqt = jnp.where(low, dq[0], dq[1]) * SCALE
                dqkv[b, rows, cols] = turn(dqt, cos, -sin, first[rows]).astype(BF)
        dqkv[b, :, 256:384] = turn(dk[...] * SCALE, cos_ref[...], -sin_ref[...], first).astype(BF)
        dqkv[b, :, 384:512] = dv[...].astype(BF)
        return carry

    lax.fori_loop(0, 4, block, 0)
    n1 = n1_ref[...]
    dn1 = jnp.zeros((T, MODEL_WIDTH), F32)
    for b in range(4):
        cols = slice(b * 512, (b + 1) * 512)
        dw_ref[:, cols] = dotg(n1, dqkv[b], TN).astype(BF)
        dn1 = dn1 + dotg(dqkv[b], w_ref[:, cols], NT)
    x = x_ref[...].astype(F32)
    gain = gain_ref[...]
    r1 = lax.rsqrt(jnp.mean(x * x, axis=1, keepdims=True) + EPSILON)
    gd = gain * dn1
    inner = jnp.mean(gd * x, axis=1, keepdims=True)
    dx_ref[...] = dh1_ref[...] + r1 * gd - x * (r1 * r1 * r1 * inner)
    dw_ref[:, 2048:2176] = columns_of(dn1 * x * r1, 0).astype(BF)


def visible_bias(segment, parents):
    ids = jnp.arange(parents.shape[0], dtype=jnp.int32)
    one = jnp.sum(jnp.where(segment[:, None] == ids[None, :], parents[None, :], 0), axis=1)
    two = jnp.sum(jnp.where(one[:, None] == ids[None, :], parents[None, :], 0), axis=1)
    key = segment[None, :]
    related = (key == segment[:, None]) | (key == one[:, None]) | (key == two[:, None])
    places = jnp.arange(segment.shape[0], dtype=jnp.int32)
    return jnp.where(related & (places[None, :] <= places[:, None]), 0.0, NEG_FILL).astype(F32)


def turn_tables(positions):
    half = HEAD_SIZE // 2
    lane = jnp.arange(LANES, dtype=jnp.int32)
    frequency = ROPE_BASE ** (-((lane % half).astype(F32) * 2.0) / HEAD_SIZE)
    angle = positions.astype(F32)[:, None] * frequency[None, :]
    sign = jnp.where(lane % HEAD_SIZE < half, -1.0, 1.0).astype(F32)
    return jnp.cos(angle), jnp.sin(angle) * sign[None, :]


def make_shards(groups, fsdp):
    ring = list(range(0, groups, 1))
    if groups == 4:
        ring = [0, 1, 3, 2]
    place = [ring.index(g) for g in range(groups)]
    rest = fsdp // 8

    def shifted(k):
        return [(ring[p], ring[(p + k) % groups]) for p in range(groups)]

    def flip(bits):
        return [(i, i ^ bits) for i in range(fsdp)]

    low_groups = None if rest == 1 else [[8 * r + j for j in range(8)] for r in range(rest)]
    rest_groups = [[8 * r + j for r in range(rest)] for j in range(8)]

    def z_next(a):
        return lax.ppermute(a, "grp", shifted(1))

    def to_x(a):
        return lax.ppermute(a, "fsdp", flip(2))

    def to_y(a):
        return lax.ppermute(a, "fsdp", flip(4))

    def to_diag(a):
        return lax.ppermute(a, "fsdp", flip(6))

    def to_core(a):
        return lax.ppermute(a, "fsdp", flip(1))

    def plane(a):
        half = a.shape[0] // 2
        ax = to_x(a)
        ay = to_y(a)
        return (a, ax, ay, to_x(ay[:half]), to_y(ax[half:]))

    def z_sum(blocks):
        total = blocks[0].astype(F32)
        for k in range(1, groups):
            total = total + lax.ppermute(blocks[k], "grp", shifted(groups - k)).astype(F32)
        return total

    def shards(tokens, segment, positions, parents, routes, attn_gain, query_weight, key_matrix,
               value_matrix, out_weight, ffn_gain, router_weight, gate_up_weight, down_weight, cotangent):
        dr = query_weight.shape[0]
        mine = lax.axis_index("fsdp")
        spot = jnp.array(place, jnp.int32)[lax.axis_index("grp")]
        ring_ids = jnp.array(ring, jnp.int32)

        def swapped(w):
            return [w[:, 0:64], w[:, 128:192], w[:, 64:128], w[:, 192:256]]

        def z_gather(a):
            got = [a]
            for _ in range(groups - 1):
                got.append(z_next(got[-1]))
            return got

        own_qkv = jnp.concatenate(swapped(query_weight) + [key_matrix, value_matrix], axis=1)
        cols_qkv = jnp.concatenate(z_gather(own_qkv), axis=1)
        w_qkv = lax.all_gather(cols_qkv, "fsdp", axis=0, tiled=True)
        own_out = after(jnp.concatenate(swapped(out_weight), axis=1), cols_qkv)
        cols_out = jnp.concatenate(z_gather(own_out), axis=1)
        w_out = lax.all_gather(cols_out, "fsdp", axis=0, tiled=True)

        small = jnp.concatenate([router_weight.T, attn_gain[None], ffn_gain[None]], axis=0)
        small = jnp.concatenate([small.reshape(-1), routes.T.astype(BF).reshape(-1)])
        small = lax.all_gather(small, "fsdp", axis=0, tiled=False)
        rows = jnp.transpose(small[:, : 18 * dr].reshape(fsdp, 18, dr), (1, 0, 2)).reshape(18, -1)
        router_t = jnp.concatenate([rows[:16], jnp.zeros((LANES - 16, MODEL_WIDTH), BF)], axis=0)
        gain_one = rows[16:17].astype(F32)
        gain_two = rows[17:18].astype(F32)
        lanes = jnp.arange(LANES, dtype=jnp.int32)

        def route_mask(bits):
            got = lax.dynamic_index_in_dim(small, mine ^ bits, 0, keepdims=False)[18 * dr :]
            got = got.reshape(-1, T).T.astype(jnp.int32)
            return jnp.sum((got[:, :, None] == lanes[None, None, :]).astype(F32), axis=1).astype(BF)

        masks = [route_mask(bits) for bits in (0, 2, 4, 6)]

        gu = gate_up_weight.reshape(dr, 4, 2, 2, HALF)
        dn = down_weight.reshape(dr, 4, 1, 2, HALF)
        parts = jnp.concatenate([gu, dn], axis=2)
        parts = jnp.transpose(parts, (1, 3, 0, 2, 4)).reshape(8, dr, 3 * HALF)
        unit = lax.all_to_all(parts, "fsdp", 0, 0, axis_index_groups=low_groups)
        unit = unit.reshape(8 * dr, 3 * HALF)
        if rest > 1:
            unit = lax.all_gather(unit, "fsdp", axis=0, tiled=True, axis_index_groups=rest_groups)

        bias = visible_bias(segment, parents[0])
        cos, sin = turn_tables(positions)

        tokens_f = after(tokens, unit, cols_out, bias, cos, sin, *masks)
        dy_x = to_x(cotangent)
        dy_y = to_y(cotangent)
        units = z_gather(unit)
        n1, qkv, att = call(
            attn_fwd,
            [((T, MODEL_WIDTH), BF), ((4, T, 512), BF), ((4, T, 256), BF)],
            [VM] * 6, [VM] * 3, [],
            (tokens_f, gain_one, w_qkv, cos, sin, bias), "attn_fwd", 48, 3.0e9,
        )
        half = T // 2
        att, dy_x, dy_y = lax.optimization_barrier((att, dy_x, dy_y))
        dy_a = to_x(dy_y[:half])
        dy_b = to_y(dy_x[half:])
        h1, n2, gates = call(
            mid,
            [((T, MODEL_WIDTH), F32), ((T, MODEL_WIDTH), BF), ((T, LANES), F32)],
            [VM] * 6, [VM] * 3, [],
            (tokens, att, w_out, gain_two, router_t, masks[0]), "mid", 48, 1.0e9,
        )
        n2, dy_a, dy_b, u1 = lax.optimization_barrier((n2, dy_a, dy_b, units[1]))
        units[1] = u1
        dys = (cotangent, dy_x, dy_y, dy_a, dy_b)
        pairs = [(u, to_core(u)) for u in units]
        xs = plane(n2)
        gates_rest, = call(
            gate_rest, [((3 * T, LANES), F32)], [VM] * 8, [VM], [],
            (*xs[1:], router_t, *masks[1:]), "gate_rest", 48, 0.4e9,
        )

        chip = (mine // 2) % 4
        order = list(range(1, groups)) + [0]
        ghs = [None] * groups
        dgus = [None] * groups
        mine_dw = []
        dgate = jnp.zeros((ROWS, LANES), F32)
        for k in order:
            e = (4 * ring_ids[(spot - k) % groups] + chip).astype(jnp.int32).reshape(1)
            ghs[k], dgus[k], dw_own, dw_sib, dgate = run_expert(
                e, xs, dys, (gates, gates_rest), *pairs[k], dgate
            )
            mine_dw.append((dw_own, to_core(dw_sib)))

        def chip_sum(i, *more):
            total = mine_dw[i][0].astype(F32) + mine_dw[i][1].astype(F32)
            for m in more:
                total = total + m.astype(F32)
            return total.astype(BF)

        ws = [w for pair in pairs for w in pair]
        xy_splits = ((0, half), (half, T), (T, T + half), (T + half, 2 * T))

        def back(acts, extra, width, first_col, lo, m, splits, dtypes, name):
            return run_back(acts, ws, extra, lo, m, width, first_col, splits, dtypes, name)

        hop = z_next(chip_sum(0))
        dgus[0], hop = lax.optimization_barrier((dgus[0], hop))
        args = (dgus, dgate, 2 * HALF, 0)
        da, db = back(*args, 3 * T, T, ((0, half), (half, T)), (BF, BF), "dn2_d")
        hop = z_next(chip_sum(1, hop))
        ra = to_x(da)
        rb = to_y(db)
        xa, xb, ya, yb = back(*args, T, 2 * T, xy_splits, (BF,) * 4, "dn2_xy")
        rxa = to_x(xa)
        ryb = to_y(yb)
        ra = after(ra, xa)
        rxb = to_x((xb.astype(F32) + rb.astype(F32)).astype(BF))
        rya = to_y((ya.astype(F32) + ra.astype(F32)).astype(BF))
        own, = back(*args, 0, T, ((0, T),), (F32,), "dn2_o")
        ghs[0] = after(ghs[0], own)
        args = (ghs, None, HALF, 2 * HALF)
        oda, odb = back(*args, 3 * T, T, ((0, half), (half, T)), (BF, BF), "out_d")
        oxa, oxb, oya, oyb = back(*args, T, 2 * T, xy_splits, (BF,) * 4, "out_xy")
        own, hop, oda, odb, oxa = lax.optimization_barrier((own, hop, oda, odb, oxa))
        dh1, datt, dwo = call(
            join,
            [((T, MODEL_WIDTH), F32), ((4, T, 256), BF), ((MODEL_WIDTH, 1152), BF)],
            [VM] * 13, [VM] * 3, [],
            (own, rxa, rxb, rya, ryb, gates, h1, n2, gain_two, router_t, cotangent, w_out, att),
            "join", 48, 2.0e9,
        )
        rs_out = lax.psum_scatter(dwo, "fsdp", scatter_dimension=0, tiled=True)
        hop = z_next(chip_sum(2, hop))
        oda, odb, oxa, oyb, _ = lax.optimization_barrier((oda, odb, oxa, oyb, dh1))
        ra = to_x(oda)
        rb = to_y(odb)
        orxa = to_x(oxa)
        oryb = to_y(oyb)
        dx, dwqkv = call(
            attn_bwd,
            [((T, MODEL_WIDTH), F32), ((MODEL_WIDTH, 2176), BF)],
            [VM] * 10, [VM] * 2,
            [pltpu.VMEM((4, T, 512), BF), pltpu.VMEM((T, LANES), F32), pltpu.VMEM((T, LANES), F32)],
            (tokens, gain_one, w_qkv, cos, sin, bias, n1, qkv, datt, dh1), "attn_bwd", 48, 6.0e9,
        )
        ra, rb, hop, orxa, oryb, ghs[0], dwqkv = lax.optimization_barrier(
            (ra, rb, hop, orxa, oryb, ghs[0], dwqkv)
        )
        rs_qkv = lax.psum_scatter(dwqkv, "fsdp", scatter_dimension=0, tiled=True)
        orxb = to_x((oxb.astype(F32) + rb.astype(F32)).astype(BF))
        orya = to_y((oya.astype(F32) + ra.astype(F32)).astype(BF))
        oown, = back(ghs, None, HALF, 2 * HALF, 0, T, ((0, T),), (F32,), "out_o")

        acc = chip_sum(3, hop)
        if rest > 1:
            acc = lax.psum_scatter(
                acc, "fsdp", scatter_dimension=0, tiled=True, axis_index_groups=rest_groups
            )
        home = lax.all_to_all(acc.reshape(8, dr, 3 * HALF), "fsdp", 0, 0, axis_index_groups=low_groups)
        home = home.astype(F32).reshape(4, 2, dr, 3, HALF)
        home = jnp.transpose(home, (2, 0, 3, 1, 4))
        gate_up_grad = home[:, :, :2].reshape(dr, 4, 2 * FF)
        down_grad = home[:, :, 2].reshape(dr, 4, FF)

        z_out = z_sum([
            jnp.concatenate([rs_out[:, k * 256 : (k + 1) * 256], rs_out[:, 1024:]], axis=1)
            for k in range(groups)
        ])
        received = jnp.concatenate([orxa, orxb], axis=0).astype(F32)
        received = received + jnp.concatenate([orya, oryb], axis=0).astype(F32)
        output = (h1 + oown + received).astype(BF)
        z_qkv = z_sum([
            jnp.concatenate([rs_qkv[:, k * 512 : (k + 1) * 512], rs_qkv[:, 2048:]], axis=1)
            for k in range(groups)
        ])
        return (
            output,
            dx,
            z_qkv[:, 512],
            jnp.concatenate(swapped(z_qkv[:, :256]), axis=1),
            z_qkv[:, 256:384],
            z_qkv[:, 384:512],
            jnp.concatenate(swapped(z_out[:, :256]), axis=1),
            z_out[:, 256 + EXPERTS],
            z_out[:, 256 : 256 + EXPERTS],
            gate_up_grad,
            down_grad,
        )

    return shards


def solution(mesh):
    both = ("grp", "fsdp")
    in_specs = (
        P(both, None), P(both), P(both), P(both, None), P(both, None),
        P("fsdp"), P("fsdp", "grp"), P("fsdp", "grp"), P("fsdp", "grp"), P("fsdp", "grp"),
        P("fsdp"), P("fsdp", None), P("fsdp", "grp", None), P("fsdp", "grp", None), P(both, None),
    )
    out_specs = (
        P(both, None), P(both, None), P("fsdp"),
        P("fsdp", "grp"), P("fsdp", "grp"), P("fsdp", "grp"), P("fsdp", "grp"),
        P("fsdp"), P("fsdp", None), P("fsdp", "grp", None), P("fsdp", "grp", None),
    )
    shards = make_shards(mesh.shape["grp"], mesh.shape["fsdp"])
    return jax.shard_map(shards, mesh=mesh, in_specs=in_specs, out_specs=out_specs, check_vma=False)
```

```python
import math

import jax
import jax.numpy as jnp
from jax import lax
from jax.experimental import pallas as pl
from jax.experimental.pallas import tpu as pltpu
from jax.sharding import PartitionSpec as P

MODEL_WIDTH = 1024
HEAD_SIZE = 64
FF = 512
HALF = FF // 2
EXPERTS = 16
T = 384
LANES = 128
EPSILON = 1e-06
ROPE_BASE = 10000.0
NEG_FILL = -1e30
SCALE = 1.0 / math.sqrt(HEAD_SIZE)
BF = jnp.bfloat16
F32 = jnp.float32
COST = 0.02
VMEM_MIB = 62

NT = (((1,), (1,)), ((), ()))
TN = (((0,), (0,)), ((), ()))

VM = pl.BlockSpec(memory_space=pltpu.VMEM)
SM = pl.BlockSpec(memory_space=pltpu.SMEM)
HB = pl.BlockSpec(memory_space=pltpu.HBM)


def dot(a, b):
    return jnp.dot(a, b, preferred_element_type=F32)


def dotg(a, b, dims, **kw):
    return lax.dot_general(a, b, dims, preferred_element_type=F32, **kw)


def call(body, outs, in_specs, out_specs, scratch, args, name, vmem=48, flops=0):
    nbytes = sum(math.prod(a.shape) * a.dtype.itemsize for a in args)
    nbytes += sum(math.prod(s) * jnp.dtype(d).itemsize for s, d in outs)
    return pl.pallas_call(
        body,
        out_shape=[jax.ShapeDtypeStruct(s, d) for s, d in outs],
        in_specs=in_specs,
        out_specs=out_specs,
        scratch_shapes=scratch,
        compiler_params=pltpu.CompilerParams(vmem_limit_bytes=VMEM_MIB << 20),
        cost_estimate=pl.CostEstimate(
            flops=int(flops * COST), transcendentals=0, bytes_accessed=int(nbytes * COST)
        ),
        name=name,
    )(*args)


def after(x, *deps):
    return lax.optimization_barrier((x, *deps))[0]


def low_half(shape):
    return lax.broadcasted_iota(jnp.int32, shape, 1) < HEAD_SIZE


def turn(part, cos, sin, first):
    partner = jnp.where(first, pltpu.roll(part, 96, 1), pltpu.roll(part, 32, 1))
    return part * cos + partner * sin


def first_of_head(shape):
    return (lax.broadcasted_iota(jnp.int32, shape, 1) % HEAD_SIZE) < HEAD_SIZE // 2


def attn_rows(qkv_ref, bias_ref, b, c, low):
    rows = slice(c * LANES, (c + 1) * LANES)
    seen = (c + 1) * LANES
    qa = qkv_ref[b, rows, 0:LANES]
    qb = qkv_ref[b, rows, LANES : 2 * LANES]
    zero = jnp.zeros_like(qa)
    q = jnp.concatenate(
        [jnp.where(low, qa, zero), jnp.where(low, qb, zero), jnp.where(low, zero, qa), jnp.where(low, zero, qb)], axis=0
    )
    keys = qkv_ref[b, :seen, 256:384]
    bias = bias_ref[rows, :seen]
    s = dotg(q, keys, NT) * SCALE + jnp.concatenate([bias] * 4, axis=0)
    p = jnp.exp(s - jnp.max(s, axis=1, keepdims=True))
    p = p * (1.0 / jnp.sum(p, axis=1, keepdims=True))
    return rows, seen, q, keys, p


def fetch(pairs, sems, first=0):
    copies = [pltpu.make_async_copy(a, b, sems.at[first + i]) for i, (a, b) in enumerate(pairs)]
    for c in copies:
        c.start()
    return copies


def wait(copies):
    for c in copies:
        c.wait()


def attn_fwd(places, dr):
    n = len(places)

    def body(mine_ref, *refs):
        pieces = refs[:n]
        x_h, cos_h, sin_h, bias_h, wo_h = refs[n : n + 5]
        w_h, n1_h, qkv_h, att_h, h1_h, n2_h, rows_h = refs[n + 5 : n + 12]
        x, cos, sin, bias, wo, w, n1, qkv, att, h1, n2, small, si, so = refs[n + 12 :]
        mine = mine_ref[0]
        pairs = [(x_h, x), (cos_h, cos), (sin_h, sin)]
        for p, (bits, off, rows) in zip(pieces, places):
            at = 0 if bits is None else pl.multiple_of((mine ^ bits) * dr + off, math.gcd(dr, off))
            pairs.append((p, w.at[pl.ds(at, rows)]))
        pairs += [(bias_h, bias), (wo_h, wo)]
        copies = fetch(pairs, si)
        wait(copies[:-1])
        outs = fetch([(w.at[:, 0:2048], w_h)], so)
        small[...] = w[:, 2048:2176].astype(F32).T
        outs += fetch([(small, rows_h)], so, 7)
        attn_fwd_body(x, small.at[16:17], w, cos, sin, bias, n1, qkv, att)
        outs += fetch([(n1, n1_h), (qkv, qkv_h), (att, att_h)], so, 1)
        copies[-1].wait()
        mid(x, att, wo, small.at[17:18], h1, n2)
        outs += fetch([(n2, n2_h), (h1, h1_h)], so, 4)
        wait(outs)

    return body


def attn_fwd_body(x_ref, gain_ref, w_ref, cos_ref, sin_ref, bias_ref, n1_ref, qkv_ref, att_ref):
    x = x_ref[...].astype(F32)
    r1 = lax.rsqrt(jnp.mean(x * x, axis=1, keepdims=True) + EPSILON)
    n1 = (x * r1 * gain_ref[...]).astype(BF)
    n1_ref[...] = n1
    cos = cos_ref[...]
    sin = sin_ref[...]
    first = first_of_head((T, LANES))
    low = low_half((LANES, LANES))
    for b in range(4):
        raw = dot(n1, w_ref[:, b * 512 : (b + 1) * 512])
        for s in range(4):
            part = raw[:, s * LANES : (s + 1) * LANES]
            if s < 3:
                part = turn(part, cos, sin, first)
            qkv_ref[b, :, s * LANES : (s + 1) * LANES] = part.astype(BF)

    def block(b, carry):
        for c in range(3):
            rows, seen, q, keys, p = attn_rows(qkv_ref, bias_ref, b, c, low)
            o = dot(p.astype(BF), qkv_ref[b, :seen, 384:512])
            att_ref[b, rows, 0:LANES] = jnp.where(low, o[0:LANES], o[2 * LANES : 3 * LANES]).astype(BF)
            att_ref[b, rows, LANES : 2 * LANES] = jnp.where(low, o[LANES : 2 * LANES], o[3 * LANES :]).astype(BF)
        return carry

    for b in range(4):
        block(b, 0)


def soft_gates(n2, rt, mask):
    logits = dotg(n2, rt, NT)
    top = jnp.max(jnp.where(mask > 0, logits, NEG_FILL), axis=1, keepdims=True)
    e = jnp.where(mask > 0, jnp.exp(jnp.minimum(logits - top, 0.0)), 0.0)
    return e / jnp.sum(e, axis=1, keepdims=True)


def route_mask(routes):
    ids = lax.broadcasted_iota(jnp.int32, (LANES, T), 0).astype(F32)
    hit = jnp.zeros((LANES, T), F32)
    for i in range(8):
        hit = hit + jnp.where(ids == routes[i : i + 1, :], 1.0, 0.0)
    return hit.T


def mid(x_ref, att_ref, wo_ref, gain_ref, h1_ref, n2_ref):
    att = jnp.concatenate([att_ref[b] for b in range(4)], axis=1)
    h1 = x_ref[...].astype(F32) + dotg(att, wo_ref[...], NT)
    h1_ref[...] = h1
    r2 = lax.rsqrt(jnp.mean(h1 * h1, axis=1, keepdims=True) + EPSILON)
    n2_ref[...] = (h1 * r2 * gain_ref[...]).astype(BF)


ROWS = 4 * T
WIDE = 2 * HALF
UNIT = 3 * HALF
TREE = [slice(t * T, (t + 1) * T) for t in range(4)]


def token_pairs(srcs, dst):
    pairs, at = [], 0
    for r in srcs:
        pairs.append((r, dst.at[at : at + r.shape[0]]))
        at += r.shape[0]
    return pairs


def chip_pairs(src, chip, dst):
    return [
        (src.at[pl.ds(pl.multiple_of((chip ^ t) * T, T), T)], dst.at[t * T : (t + 1) * T]) for t in range(4)
    ]


def tree_waits(hx, hy):
    return [hx[0:1] + hy[0:1], hx[1:2] + hy[1:2], hx[2:3] + hy[2:3], hx[3:] + hy[3:]]


def act(t, e, X, Y, W, GT, GH, DGU):
    rows = TREE[t]
    lanes = lax.broadcasted_iota(jnp.int32, (T, LANES), 1)
    gate = jnp.sum(jnp.where(lanes == e, GT[rows, :], 0.0), axis=1, keepdims=True)
    dgate = jnp.zeros((T, 1), F32)
    for u in range(2):
        gu = dot(X[rows, :], W[u, :, 0:WIDE])
        dh = dot(Y[rows, :], W[u, :, WIDE:UNIT])
        g = gu[:, :HALF]
        up = gu[:, HALF:]
        s = 0.5 * jnp.tanh(0.5 * g) + 0.5
        silu = g * s
        hid = silu * up
        GH[rows, u * HALF : (u + 1) * HALF] = (gate * hid).astype(BF)
        dgate = dgate + jnp.sum(dh * hid, axis=1, keepdims=True)
        dh = dh * gate
        base = u * WIDE
        DGU[rows, base : base + HALF] = (dh * up * (s + silu * (1.0 - s))).astype(BF)
        DGU[rows, base + HALF : base + WIDE] = (dh * silu).astype(BF)
    return jnp.where(lanes == e, dgate, 0.0)


def wgrad(X, Y, GH, DGU, DW):
    step = 256
    for r in range(MODEL_WIDTH // step):
        cols = slice(r * step, (r + 1) * step)
        dg = dotg(X[:, cols], DGU[...], TN)
        dd = dotg(Y[:, cols], GH[...], TN)
        for u in range(2):
            DW[u, cols, 0:WIDE] = dg[:, u * WIDE : (u + 1) * WIDE].astype(BF)
            DW[u, cols, WIDE:UNIT] = dd[:, u * HALF : (u + 1) * HALF].astype(BF)


def stage_scratch(n, extra, loads, stores):
    return [
        pltpu.VMEM((ROWS, MODEL_WIDTH), BF), pltpu.VMEM((ROWS, MODEL_WIDTH), BF),
        pltpu.VMEM((n, 2, MODEL_WIDTH, UNIT), BF),
        pltpu.VMEM((n, ROWS, FF), BF), pltpu.VMEM((n, ROWS, 2 * FF), BF),
        pltpu.VMEM((ROWS, LANES), F32), pltpu.VMEM((ROWS, LANES), F32),
        *extra,
        pltpu.SemaphoreType.DMA((loads,)), pltpu.SemaphoreType.DMA((stores,)),
    ]


def load_tokens(xs, dyg, chip, X, Y, head, rest, si):
    px, py = token_pairs(xs, X), chip_pairs(dyg, chip, Y)
    order = px[0:1] + head + py[0:1] + px[1:] + py[1:] + rest
    copies = fetch(order, si)
    n = 1 + len(head)
    cx = copies[0:1] + copies[n + 1 : n + 5]
    cy = copies[n : n + 1] + copies[n + 5 : n + 8]
    return copies[1:n], tree_waits(cx, cy), copies[n + 8 :]


def stage_a(e_ref, *refs):
    xs, dyg, ws = refs[0:5], refs[5], refs[6:8]
    rt_h, routes = refs[8], refs[9:13]
    gh_h, dgu_h, dwo_h, dws_h, gates_h, dgate_h = refs[13:19]
    X, Y, W, GH, DGU, GT, DG, DW, rt, si, so = refs[19:]
    head, trees, _ = load_tokens(
        xs, dyg, e_ref[4], X, Y, [(rt_h, rt)] + [(ws[i], W.at[0, i]) for i in range(2)], [], si
    )
    wait(head)
    router = rt[...].astype(BF)
    for t in range(4):
        wait(trees[t])
        GT[TREE[t], :] = soft_gates(X[TREE[t], :], router, route_mask(routes[t][...].astype(F32)))
        DG[TREE[t], :] = act(t, e_ref[1], X, Y, W.at[0], GT, GH.at[0], DGU.at[0])
    outs = fetch([(GH.at[0], gh_h), (DGU.at[0], dgu_h), (GT, gates_h), (DG, dgate_h)], so)
    wgrad(X, Y, GH.at[0], DGU.at[0], DW)
    outs += fetch([(DW.at[0], dwo_h), (DW.at[1], dws_h)], so, 4)
    wait(outs)


ACT_OUT = [((ROWS, FF), BF), ((ROWS, 2 * FF), BF)]
GATE_OUT = [((ROWS, LANES), F32)]
DW_OUT = [((MODEL_WIDTH, UNIT), BF)] * 2
DW_VMEM = pltpu.VMEM((2, MODEL_WIDTH, UNIT), BF)
EXPERT_FLOPS = 2 * ROWS * MODEL_WIDTH * 3 * FF


def run_stage_a(e, xs, dyg, pair, rt, routes):
    extra = [DW_VMEM, pltpu.VMEM((LANES, MODEL_WIDTH), F32)]
    return call(
        stage_a, ACT_OUT + DW_OUT + GATE_OUT * 2, [SM] + [HB] * 9 + [VM] * 4, [HB] * 6,
        stage_scratch(1, extra, 12, 6), (e, *xs, dyg, *pair, rt, *routes), "stage_a", 48, 2 * EXPERT_FLOPS,
    )


def stage_b(e_ref, *refs):
    xs, dyg, ws = refs[0:5], refs[5], refs[6:10]
    gates_h, dgate_i = refs[10:12]
    gh0_h, dgu0_h, gh2_h, dgu2_h, dgate_h, dwo_h, dws_h = refs[12:19]
    X, Y, W, GH, DGU, GT, DG, DW, si, so = refs[19:]
    hw = [(ws[i], W.at[i // 2, i % 2]) for i in range(4)]
    head, trees, second = load_tokens(
        xs, dyg, e_ref[4], X, Y, hw[0:2] + [(gates_h, GT), (dgate_i, DG)], hw[2:], si
    )
    wait(head)
    for t in range(4):
        wait(trees[t])
        DG[TREE[t], :] += act(t, e_ref[0], X, Y, W.at[0], GT, GH.at[0], DGU.at[0])
    outs = fetch([(GH.at[0], gh0_h), (DGU.at[0], dgu0_h)], so)
    wait(second)
    for t in range(4):
        DG[TREE[t], :] += act(t, e_ref[2], X, Y, W.at[1], GT, GH.at[1], DGU.at[1])
    outs += fetch([(GH.at[1], gh2_h), (DGU.at[1], dgu2_h), (DG, dgate_h)], so, 2)
    wgrad(X, Y, GH.at[1], DGU.at[1], DW)
    outs += fetch([(DW.at[0], dwo_h), (DW.at[1], dws_h)], so, 5)
    wait(outs)


def run_stage_b(e, xs, dyg, ws, gates, dgate):
    return call(
        stage_b, ACT_OUT * 2 + GATE_OUT + DW_OUT, [SM] + [HB] * 12, [HB] * 7,
        stage_scratch(2, [DW_VMEM], 15, 7), (e, *xs, dyg, *ws, gates, dgate), "stage_b", 48, 3 * EXPERT_FLOPS,
    )


def stage_c(e_ref, *refs):
    xs, dyg, ws = refs[0:5], refs[5], refs[6:14]
    gates_h, dgate_i = refs[14:16]
    dgus = refs[16:19]
    gh_h, dgu_h, dgate_h, parts_h = refs[19:23]
    X, Y, W, GH, DGU, GT, DG, WB, DF, OUT, si, so = refs[23:]
    late = [(ws[i].at[:, 0:WIDE], WB.at[:, i * WIDE : (i + 1) * WIDE]) for i in range(6)]
    late += [(dgus[i].at[T:ROWS], DF.at[:, 2 * i * FF : 2 * (i + 1) * FF]) for i in range(3)]
    head, trees, late = load_tokens(
        xs, dyg, e_ref[4], X, Y,
        [(ws[6 + i], W.at[0, i]) for i in range(2)] + [(gates_h, GT), (dgate_i, DG)], late, si,
    )
    wait(head)
    for t in range(4):
        wait(trees[t])
        DG[TREE[t], :] += act(t, e_ref[3], X, Y, W.at[0], GT, GH.at[0], DGU.at[0])
    outs = fetch([(GH.at[0], gh_h), (DGU.at[0], dgu_h), (DG, dgate_h)], so)
    wait(late)
    w = jnp.concatenate([WB[...]] + [W[0, i, :, 0:WIDE] for i in range(2)], axis=1)
    for i, t in enumerate((3, 1, 2)):
        a = jnp.concatenate([DF[TREE[t - 1], :], DGU[0, TREE[t], :]], axis=1)
        OUT[i, :, 0:MODEL_WIDTH] = dotg(a, w, NT).astype(BF)
        OUT[i, :, MODEL_WIDTH:] = DG[TREE[t], :].astype(BF)
        outs += fetch([(OUT.at[i], parts_h.at[e_ref[4] ^ t])], so, 3 + i)
    wait(outs)


def run_stage_c(e, xs, dyg, ws, gates, dgate, dgus):
    cols = MODEL_WIDTH + LANES
    extra = [
        pltpu.VMEM((MODEL_WIDTH, 6 * WIDE), BF), pltpu.VMEM((3 * T, 6 * FF), BF), pltpu.VMEM((3, T, cols), BF),
    ]
    return call(
        stage_c, ACT_OUT + GATE_OUT + [((4, T, cols), BF)], [SM] + [HB] * 19, [HB] * 4,
        stage_scratch(1, extra, 22, 6), (e, *xs, dyg, *ws, gates, dgate, *dgus), "stage_c", 48, 2 * EXPERT_FLOPS,
    )


def back_pairs(acts, ws, lo, m, width, first_col, A, W):
    pairs = []
    for k in range(4):
        pairs.append((acts[k].at[lo : lo + m], A.at[:, k * 2 * width : (k + 1) * 2 * width]))
        for u in range(2):
            at = (2 * k + u) * width
            pairs.append((ws[2 * k + u].at[:, first_col : first_col + width], W.at[:, at : at + width]))
    return pairs


def late_stage(n, own):
    def body(e_ref, *refs):
        xs, dyg, acts = refs[0:5], refs[5], refs[6 : 6 + 2 * n]
        refs = refs[6 + 2 * n :]
        pairs = []
        if own:
            dgus, ws, dgate_h = refs[0:4], refs[4:12], refs[12]
            refs = refs[13:]
        dws, refs = refs[: 2 * n], refs[2 * n :]
        if own:
            own_h, refs = refs[0], refs[1:]
        X, Y, GH, DGU, DW, si, so = refs[:7]
        if own:
            A, W, DG, O = refs[7:]
            pairs = back_pairs(dgus, ws, 0, T, WIDE, 0, A, W) + [(dgate_h.at[0:T], DG)]
        first = len(pairs)
        pairs += chip_pairs(dyg, e_ref[4], Y) + [(acts[0], GH.at[0])] + token_pairs(xs, X) + [(acts[1], DGU.at[0])]
        for i in range(1, n):
            pairs += [(acts[2 * i], GH.at[i]), (acts[2 * i + 1], DGU.at[i])]
        copies = fetch(pairs, si)
        outs = []
        if own:
            wait(copies[:first])
            O[:, 0:MODEL_WIDTH] = dotg(A[...], W[...], NT)
            O[:, MODEL_WIDTH:] = DG[...]
            outs += fetch([(O, own_h)], so, 2 * n)
        for i in range(n):
            wait(copies[first + (11 if i else 0) + 2 * (i - 1) * (i > 0) : first + 11 + 2 * i])
            wgrad(X, Y, GH.at[i], DGU.at[i], DW.at[i])
            outs += fetch([(DW.at[i, 0], dws[2 * i]), (DW.at[i, 1], dws[2 * i + 1])], so, 2 * i)
        wait(outs)

    return body


def run_late(e, xs, dyg, acts, back=()):
    n = len(acts) // 2
    cols = MODEL_WIDTH + LANES
    args = (e, *xs, dyg, *acts, *back)
    outs = DW_OUT * n
    scratch = [
        pltpu.VMEM((ROWS, MODEL_WIDTH), BF), pltpu.VMEM((ROWS, MODEL_WIDTH), BF),
        pltpu.VMEM((n, ROWS, FF), BF), pltpu.VMEM((n, ROWS, 2 * FF), BF),
        pltpu.VMEM((n, 2, MODEL_WIDTH, UNIT), BF),
        pltpu.SemaphoreType.DMA((22 + 2 * n,)), pltpu.SemaphoreType.DMA((2 * n + 1,)),
    ]
    if back:
        outs = outs + [((T, cols), F32)]
        scratch += [
            pltpu.VMEM((T, 8 * WIDE), BF), pltpu.VMEM((MODEL_WIDTH, 8 * WIDE), BF),
            pltpu.VMEM((T, LANES), F32), pltpu.VMEM((T, cols), F32),
        ]
    return call(
        late_stage(n, bool(back)), outs, [SM] + [HB] * (len(args) - 1), [HB] * len(outs), scratch,
        args, "late_stage", 52, 2 * EXPERT_FLOPS,
    )


def last_stage(e_ref, *refs):
    xs, dyg, gh_h, dgu_h = refs[0:5], refs[5], refs[6], refs[7]
    ghs, ws = refs[8:12], refs[12:20]
    dwo_h, dws_h, parts_h, own_h = refs[20:24]
    X, Y, GH, DGU, DW, A, W, O, OF, si, so = refs[24:]
    pairs = chip_pairs(dyg, e_ref[4], Y) + [(gh_h, GH)] + token_pairs(xs, X) + [(dgu_h, DGU)]
    pairs += back_pairs(ghs, ws, 0, ROWS, HALF, WIDE, A, W)
    copies = fetch(pairs, si)
    wait(copies[:11])
    wgrad(X, Y, GH, DGU, DW)
    outs = fetch([(DW.at[0], dwo_h), (DW.at[1], dws_h)], so)
    wait(copies[11:])
    for i, t in enumerate((3, 1, 2, 0)):
        total = dotg(A[TREE[t], :], W[...], NT)
        dst = O.at[i] if t else OF
        dst[...] = total.astype(BF) if t else total
        outs += fetch([(dst, parts_h.at[e_ref[4] ^ t] if t else own_h)], so, 2 + i)
    wait(outs)


def run_last(e, xs, dyg, acts, ghs, ws):
    args = (e, *xs, dyg, *acts, *ghs, *ws)
    return call(
        last_stage, DW_OUT + [((4, T, MODEL_WIDTH), BF), ((T, MODEL_WIDTH), F32)],
        [SM] + [HB] * (len(args) - 1), [HB] * 4,
        [
            pltpu.VMEM((ROWS, MODEL_WIDTH), BF), pltpu.VMEM((ROWS, MODEL_WIDTH), BF),
            pltpu.VMEM((ROWS, FF), BF), pltpu.VMEM((ROWS, 2 * FF), BF), DW_VMEM,
            pltpu.VMEM((ROWS, 8 * HALF), BF), pltpu.VMEM((MODEL_WIDTH, 8 * HALF), BF),
            pltpu.VMEM((3, T, MODEL_WIDTH), BF), pltpu.VMEM((T, MODEL_WIDTH), F32),
            pltpu.SemaphoreType.DMA((23,)), pltpu.SemaphoreType.DMA((6,)),
        ],
        args, "last_stage", 52, 2 * EXPERT_FLOPS,
    )


def settle(dr):
    def body(home_h, gu_ref, dn_ref, H, sem):
        c = pltpu.make_async_copy(home_h, H, sem.at[0])
        c.start()
        c.wait()
        for e in range(4):
            for h in range(2):
                part = H[2 * e + h].astype(F32)
                cols = slice(h * HALF, (h + 1) * HALF)
                gu_ref[:, e, cols] = part[:, 0:HALF]
                gu_ref[:, e, FF + h * HALF : FF + (h + 1) * HALF] = part[:, HALF:WIDE]
                dn_ref[:, e, cols] = part[:, WIDE:UNIT]

    return body


def columns_of(rowwise, lane):
    total = jnp.sum(rowwise, axis=0, keepdims=True)
    total = jnp.broadcast_to(total, (LANES, MODEL_WIDTH)).T
    lanes = lax.broadcasted_iota(jnp.int32, total.shape, 1)
    return jnp.where(lanes == lane, total, 0.0)


def join(e_ref, p_h, parts_h, gates_h, h1_h, n2_h, dy_h, wo_h, att_h, small_h,
         dh1_h, datt_h, dwo_h, P, R, GT, H1, N2, DY, WO, ATT, SMALL, DH1, DATT, DWO, si, so):
    copies = fetch(
        [(p_h, P)] + [(parts_h.at[e_ref[4] ^ t], R.at[t - 1]) for t in (1, 2, 3)]
        + [(gates_h.at[0:T], GT), (h1_h, H1), (dy_h, DY),
         (small_h, SMALL), (wo_h, WO), (att_h, ATT), (n2_h, N2)], si
    )
    wait(copies[0:8])
    gates = GT[...]
    total = P[...] + R[0].astype(F32) + R[1].astype(F32) + R[2].astype(F32)
    dg = total[:, MODEL_WIDTH:]
    dl = (gates * (dg - jnp.sum(gates * dg, axis=1, keepdims=True))).astype(BF)
    dn2 = total[:, :MODEL_WIDTH] + dot(dl, SMALL[...].astype(BF))
    h1 = H1[...]
    gain = SMALL[17:18]
    r2 = lax.rsqrt(jnp.mean(h1 * h1, axis=1, keepdims=True) + EPSILON)
    gd = gain * dn2
    inner = jnp.mean(gd * h1, axis=1, keepdims=True)
    dh1 = DY[...].astype(F32) + r2 * gd - h1 * (r2 * r2 * r2 * inner)
    DH1[...] = dh1
    db = dh1.astype(BF)
    outs = fetch([(DH1, dh1_h)], so)
    wait(copies[8:])
    for b in range(4):
        cols = slice(b * 256, (b + 1) * 256)
        DATT[b] = dot(db, WO[:, cols]).astype(BF)
        DWO[:, cols] = dotg(db, ATT[b], TN).astype(BF)
    outs += fetch([(DATT, datt_h)], so, 1)
    extra = dotg(N2[...], dl, TN) + columns_of(dn2 * h1 * r2, EXPERTS)
    DWO[:, 1024:1152] = extra.astype(BF)
    outs += fetch([(DWO, dwo_h)], so, 2)
    wait(outs)


def run_join(args):
    cols = MODEL_WIDTH + LANES
    return call(
        join,
        [((T, MODEL_WIDTH), F32), ((4, T, 256), BF), ((MODEL_WIDTH, 1152), BF)],
        [SM] + [HB] * 9, [HB] * 3,
        [
            pltpu.VMEM((T, cols), F32), pltpu.VMEM((3, T, cols), BF), pltpu.VMEM((T, LANES), F32), pltpu.VMEM((T, MODEL_WIDTH), F32),
            pltpu.VMEM((T, MODEL_WIDTH), BF), pltpu.VMEM((T, MODEL_WIDTH), BF),
            pltpu.VMEM((MODEL_WIDTH, MODEL_WIDTH), BF), pltpu.VMEM((4, T, 256), BF),
            pltpu.VMEM((LANES, MODEL_WIDTH), F32),
            pltpu.VMEM((T, MODEL_WIDTH), F32), pltpu.VMEM((4, T, 256), BF), pltpu.VMEM((MODEL_WIDTH, 1152), BF),
            pltpu.SemaphoreType.DMA((12,)), pltpu.SemaphoreType.DMA((3,)),
        ],
        args, "join", 40, 2.0e9,
    )


def attn_bwd(split, dr):
    def body(mine_ref, x_h, w_h, cos_h, sin_h, bias_h, n1_h, qkv_h, datt_h, dh1_h, small_h, *refs):
        n = 3 if split else 2
        dx_h, grads_h = refs[0], refs[1:n]
        x, w, cos, sin, bias, n1, qkv, datt, dh1, gain, dx, dw, dqkv, dk, dv, si, so = refs[n : n + 17]
        copies = fetch(
            [(bias_h, bias), (qkv_h, qkv), (datt_h, datt), (cos_h, cos), (sin_h, sin), (n1_h, n1),
             (w_h, w), (x_h, x), (dh1_h, dh1), (small_h.at[16:24], gain)], si
        )
        wait(copies[0:5])
        attn_bwd_heads(cos, sin, bias, qkv, datt, dqkv, dk, dv)
        wait(copies[5:])
        attn_bwd_body(x, gain.at[0:1], w, n1, dh1, dx, dw, dqkv)
        outs = fetch([(dx, dx_h)], so)
        if split:
            for r in range(4):
                mine = 2 * r + (mine_ref[0] & 1)
                for i, j in enumerate((mine, mine ^ 1)):
                    src = dw.at[pl.ds(pl.multiple_of(j * dr, dr), dr)]
                    outs += fetch([(src, grads_h[i].at[r * dr : (r + 1) * dr])], so, 1 + 2 * r + i)
        else:
            outs += fetch([(dw, grads_h[0])], so, 1)
        wait(outs)

    return body


def run_attn_bwd(split, dr, args):
    grads = [((4 * dr, 2176), BF)] * 2 if split else [((MODEL_WIDTH, 2176), BF)]
    tile = pltpu.VMEM((T, LANES), F32)
    return call(
        attn_bwd(split, dr),
        [((T, MODEL_WIDTH), F32)] + grads,
        [SM] + [HB] * 10, [HB] * (1 + len(grads)),
        [
            pltpu.VMEM((T, MODEL_WIDTH), BF), pltpu.VMEM((MODEL_WIDTH, 2048), BF), tile, tile,
            pltpu.VMEM((T, T), F32), pltpu.VMEM((T, MODEL_WIDTH), BF), pltpu.VMEM((4, T, 512), BF),
            pltpu.VMEM((4, T, 256), BF), pltpu.VMEM((T, MODEL_WIDTH), F32), pltpu.VMEM((8, MODEL_WIDTH), F32),
            pltpu.VMEM((T, MODEL_WIDTH), F32),
            pltpu.VMEM((MODEL_WIDTH, 2176), BF), pltpu.VMEM((4, T, 512), BF), tile, tile,
            pltpu.SemaphoreType.DMA((10,)), pltpu.SemaphoreType.DMA((9,)),
        ],
        args, "attn_bwd", 40, 6.0e9,
    )


def attn_bwd_heads(cos_ref, sin_ref, bias_ref, qkv_ref, datt_ref, dqkv, dk, dv):
    low = low_half((LANES, LANES))
    first = first_of_head((T, LANES))

    def block(b, carry):
        for c in (2, 1, 0):
            rows, seen, q, keys, p = attn_rows(qkv_ref, bias_ref, b, c, low)
            da = datt_ref[b, rows, 0:LANES]
            db = datt_ref[b, rows, LANES : 2 * LANES]
            zero = jnp.zeros_like(da)
            do = jnp.concatenate(
                [jnp.where(low, da, zero), jnp.where(low, db, zero), jnp.where(low, zero, da), jnp.where(low, zero, db)],
                axis=0,
            )
            dp = dotg(do, qkv_ref[b, :seen, 384:512], NT)
            ds = (p * (dp - jnp.sum(p * dp, axis=1, keepdims=True))).astype(BF)
            dq = dot(ds, keys) * SCALE
            dkc = dotg(ds, q, TN)
            dvc = dotg(p.astype(BF), do, TN)
            if c == 2:
                dk[...] = dkc
                dv[...] = dvc
            else:
                dk[:seen] += dkc
                dv[:seen] += dvc
            cos = cos_ref[rows, :]
            sin = -sin_ref[rows, :]
            ta = jnp.where(low, dq[0:LANES], dq[2 * LANES : 3 * LANES])
            tb = jnp.where(low, dq[LANES : 2 * LANES], dq[3 * LANES :])
            dqkv[b, rows, 0:LANES] = turn(ta, cos, sin, first[rows]).astype(BF)
            dqkv[b, rows, LANES : 2 * LANES] = turn(tb, cos, sin, first[rows]).astype(BF)
        dqkv[b, :, 256:384] = turn(dk[...] * SCALE, cos_ref[...], -sin_ref[...], first).astype(BF)
        dqkv[b, :, 384:512] = dv[...].astype(BF)
        return carry

    for b in range(4):
        block(b, 0)


def attn_bwd_body(x_ref, gain_ref, w_ref, n1_ref, dh1_ref, dx_ref, dw_ref, dqkv):
    n1 = n1_ref[...]
    cat = jnp.concatenate([dqkv[b] for b in range(4)], axis=1)
    dn1 = dotg(cat, w_ref[...], NT)
    dw_ref[:, 0:2048] = dotg(n1, cat, TN).astype(BF)
    x = x_ref[...].astype(F32)
    gain = gain_ref[...]
    r1 = lax.rsqrt(jnp.mean(x * x, axis=1, keepdims=True) + EPSILON)
    gd = gain * dn1
    inner = jnp.mean(gd * x, axis=1, keepdims=True)
    dx_ref[...] = dh1_ref[...] + r1 * gd - x * (r1 * r1 * r1 * inner)
    dw_ref[:, 2048:2176] = columns_of(dn1 * x * r1, 0).astype(BF)
def visible_bias(segment, parents):
    ids = jnp.arange(parents.shape[0], dtype=jnp.int32)
    one = jnp.sum(jnp.where(segment[:, None] == ids[None, :], parents[None, :], 0), axis=1)
    two = jnp.sum(jnp.where(one[:, None] == ids[None, :], parents[None, :], 0), axis=1)
    key = segment[None, :]
    related = (key == segment[:, None]) | (key == one[:, None]) | (key == two[:, None])
    places = jnp.arange(segment.shape[0], dtype=jnp.int32)
    return jnp.where(related & (places[None, :] <= places[:, None]), 0.0, NEG_FILL).astype(F32)


def turn_tables(positions):
    half = HEAD_SIZE // 2
    lane = jnp.arange(LANES, dtype=jnp.int32)
    frequency = ROPE_BASE ** (-((lane % half).astype(F32) * 2.0) / HEAD_SIZE)
    angle = positions.astype(F32)[:, None] * frequency[None, :]
    sign = jnp.where(lane % HEAD_SIZE < half, -1.0, 1.0).astype(F32)
    return jnp.cos(angle), jnp.sin(angle) * sign[None, :]


def make_shards(groups, fsdp):
    ring = list(range(0, groups, 1))
    if groups == 4:
        ring = [0, 1, 3, 2]
    place = [ring.index(g) for g in range(groups)]
    rest = fsdp // 8

    def shifted(k):
        return [(ring[p], ring[(p + k) % groups]) for p in range(groups)]

    def flip(bits):
        return [(i, i ^ bits) for i in range(fsdp)]

    low_groups = None if rest == 1 else [[8 * r + j for j in range(8)] for r in range(rest)]
    core_groups = [[8 * r + 2 * c + k for c in range(4)] for r in range(rest) for k in range(2)]
    rest_groups = [[8 * r + j for r in range(rest)] for j in range(8)]

    def z_next(a):
        return lax.ppermute(a, "grp", shifted(1))

    def to_x(a):
        return lax.ppermute(a, "fsdp", flip(2))

    def to_y(a):
        return lax.ppermute(a, "fsdp", flip(4))

    def to_diag(a):
        return lax.ppermute(a, "fsdp", flip(6))

    def to_core(a):
        return lax.ppermute(a, "fsdp", flip(1))

    def plane(top, bot):
        xb = to_x(bot)
        yt = to_y(top)
        xt = to_x(top)
        yb = to_y(bot)
        return (top, bot, xt, xb, yt, yb, to_x(yt), to_y(xb))

    def swap(a):
        return lax.all_to_all(a, "fsdp", 0, 0, axis_index_groups=core_groups)

    def z_sum(blocks):
        total = blocks[0].astype(F32)
        for k in range(1, groups):
            total = total + lax.ppermute(blocks[k], "grp", shifted(groups - k)).astype(F32)
        return total

    def shards(tokens, segment, positions, parents, routes, attn_gain, query_weight, key_matrix,
               value_matrix, out_weight, ffn_gain, router_weight, gate_up_weight, down_weight, cotangent):
        dr = query_weight.shape[0]
        mine = lax.axis_index("fsdp")
        spot = jnp.array(place, jnp.int32)[lax.axis_index("grp")]
        ring_ids = jnp.array(ring, jnp.int32)

        def swapped(w):
            return [w[:, 0:64], w[:, 128:192], w[:, 64:128], w[:, 192:256]]

        def z_gather(a):
            got = [a]
            for _ in range(groups - 1):
                got.append(z_next(got[-1]))
            return got

        half = T // 2
        tie = lax.optimization_barrier
        own_qkv = jnp.concatenate(swapped(query_weight) + [key_matrix, value_matrix], axis=1)
        own_out = jnp.concatenate(swapped(out_weight), axis=1)

        def z_all(a):
            return [a] + [lax.ppermute(a, "grp", shifted(k)) for k in range(1, groups)]

        route_rows = routes.T.astype(BF)
        route_rows = [route_rows, to_x(route_rows), to_y(route_rows), to_diag(route_rows)]
        blocks = z_all(jnp.concatenate([own_qkv, own_out], axis=1))

        gu = gate_up_weight.reshape(dr, 4, 2, 2, HALF)
        dn = down_weight.reshape(dr, 4, 1, 2, HALF)
        parts = jnp.concatenate([gu, dn], axis=2)
        parts = jnp.transpose(parts, (1, 3, 0, 2, 4)).reshape(8, dr, 3 * HALF)
        unit = lax.all_to_all(parts, "fsdp", 0, 0, axis_index_groups=low_groups)
        unit = unit.reshape(8 * dr, 3 * HALF)
        if rest > 1:
            unit = lax.all_gather(unit, "fsdp", axis=0, tiled=True, axis_index_groups=rest_groups)

        bias = visible_bias(segment, parents[0])
        cos, sin = turn_tables(positions)
        chip = (mine // 2) % 4
        planes = ring_ids[(spot - jnp.arange(groups, dtype=jnp.int32)) % groups]
        e = jnp.concatenate([4 * planes + chip, chip[None]]).astype(jnp.int32)
        small = jnp.concatenate(
            [router_weight, attn_gain[:, None], ffn_gain[:, None], jnp.zeros((dr, LANES - 18), BF)], axis=1
        )
        bias, cos, sin, e, small, unit, *blocks = tie((bias, cos, sin, e, small, unit, *blocks))
        cols_qkv = jnp.concatenate([b[:, :512] for b in blocks] + [small], axis=1)
        cols_out = jnp.concatenate([b[:, 512:] for b in blocks], axis=1)
        mine_s = mine.astype(jnp.int32).reshape(1)
        units_1 = z_next(unit)
        if rest == 1:
            h = dr // 2
            qx = to_x(cols_qkv)
            qy = to_y(cols_qkv)
            qc = to_core(cols_qkv)
            qx, qy, qc, units_1 = tie((qx, qy, qc, units_1))
            qa = to_x(qy[:h])
            qb = to_y(qx[h:])
            pieces = [cols_qkv, qx, qy, qa, qb, qc, to_core(qx), to_core(qy), to_core(qa), to_core(qb)]
            places = [(0, 0, dr), (2, 0, dr), (4, 0, dr), (6, 0, h), (6, h, h),
                      (1, 0, dr), (3, 0, dr), (5, 0, dr), (7, 0, h), (7, h, h)]
        else:
            pieces = [lax.all_gather(cols_qkv, "fsdp", axis=0, tiled=True)]
            places = [(None, 0, MODEL_WIDTH)]
        w_out = lax.all_gather(cols_out, "fsdp", axis=0, tiled=True)
        core_0 = to_core(after(unit, *pieces))
        dyg = lax.all_gather(after(cotangent, cols_out), "fsdp", axis=0, tiled=True, axis_index_groups=core_groups)
        tokens_f = after(tokens, *pieces)
        units_2 = z_next(units_1)
        w_qkv, n1, qkv, att, h1, n2, small = call(
            attn_fwd(places, dr),
            [((MODEL_WIDTH, 2048), BF), ((T, MODEL_WIDTH), BF), ((4, T, 512), BF), ((4, T, 256), BF),
             ((T, MODEL_WIDTH), F32), ((T, MODEL_WIDTH), BF), ((LANES, MODEL_WIDTH), F32)],
            [SM] + [HB] * (len(pieces) + 5), [HB] * 7,
            [
                pltpu.VMEM((T, MODEL_WIDTH), BF), pltpu.VMEM((T, LANES), F32), pltpu.VMEM((T, LANES), F32),
                pltpu.VMEM((T, T), F32), pltpu.VMEM((MODEL_WIDTH, MODEL_WIDTH), BF),
                pltpu.VMEM((MODEL_WIDTH, 2176), BF), pltpu.VMEM((T, MODEL_WIDTH), BF),
                pltpu.VMEM((4, T, 512), BF), pltpu.VMEM((4, T, 256), BF), pltpu.VMEM((T, MODEL_WIDTH), F32),
                pltpu.VMEM((T, MODEL_WIDTH), BF), pltpu.VMEM((LANES, MODEL_WIDTH), F32),
                pltpu.SemaphoreType.DMA((len(pieces) + 5,)), pltpu.SemaphoreType.DMA((8,)),
            ],
            (mine_s, *pieces, tokens_f, cos, sin, bias, w_out), "attn_fwd", 40, 4.0e9,
        )
        n2, core_0 = tie((n2, core_0))
        nx = to_x(n2)
        ny = to_y(n2)
        core_1 = to_core(after(units_1, n2))
        nx, ny, units_2 = tie((nx, ny, units_2))
        xs = (n2, nx, ny, to_x(ny[:half]), to_y(nx[half:]))
        core_1, *xs = tie((core_1, *xs))
        units_3 = z_next(units_2)
        core_2 = to_core(units_2)

        def chip_sum(pair, *more):
            total = pair[0].astype(F32) + pair[1].astype(F32)
            for m in more:
                total = total + m.astype(F32)
            return total.astype(BF)

        gh1, dgu1, own_1, sib_1, gates, dgate = run_stage_a(e, xs, dyg, (units_1, core_1), small, route_rows)
        core_2, gates = tie((core_2, gates))
        sib_1 = to_core(sib_1)
        gh0, dgu0, gh2, dgu2, dgate, own_2, sib_2 = run_stage_b(
            e, xs, dyg, (unit, core_0, units_2, core_2), gates, dgate
        )
        units_3, sib_1, dgate = tie((units_3, sib_1, dgate))
        core_3 = to_core(units_3)
        ws = (unit, core_0, units_1, core_1, units_2, core_2, units_3, core_3)
        sum_1, dgate = tie((chip_sum((own_1, sib_1)), dgate))
        hop = z_next(sum_1)
        sib_2 = to_core(sib_2)
        gh3, dgu3, dgate, parts = run_stage_c(e, xs, dyg, ws, gates, dgate, (dgu0, dgu1, dgu2))
        sib_2, dgate, parts = tie((sib_2, dgate, parts))
        parts = swap(parts)
        dgus = (dgu0, dgu1, dgu2, dgu3)
        own_3, sib_3, own = run_late(e, xs, dyg, (gh3, dgu3), (*dgus, *ws, dgate))
        hop, own, gh0 = tie((hop, own, gh0))
        sum_2, gh0 = tie((chip_sum((own_2, sib_2), hop), gh0))
        hop = z_next(sum_2)
        sib_3 = to_core(sib_3)
        own_0, sib_0, outs, oown = run_last(e, xs, dyg, (gh0, dgu0), (gh0, gh1, gh2, gh3), ws)
        parts, own, outs, sib_3 = tie((parts, own, outs, sib_3))
        sib_0 = to_core(sib_0)
        dh1, datt, dwo = run_join((e, own, parts, gates, h1, n2, cotangent, w_out, att, small))
        hop, dh1, sib_0 = tie((hop, dh1, sib_0))
        sum_3, dh1, outs = tie((chip_sum((own_3, sib_3), hop), dh1, outs))
        hop = z_next(sum_3)
        outs = swap(outs)
        rs_out = lax.psum_scatter(dwo, "fsdp", scatter_dimension=0, tiled=True)
        dx, *dw = run_attn_bwd(
            rest == 1, dr, (mine_s, tokens, w_qkv, cos, sin, bias, n1, qkv, datt, dh1, small)
        )
        hop, outs, *dw = tie((hop, outs, *dw))
        if rest == 1:
            sib, rs_out = tie((to_core(dw[1]), rs_out))
            total = swap(chip_sum((dw[0], sib)).reshape(4, dr, -1))
            own_0, total = tie((own_0, total))
            rs_qkv = jnp.sum(total.astype(F32), axis=0).astype(BF)
        else:
            rs_qkv = lax.psum_scatter(dw[0], "fsdp", scatter_dimension=0, tiled=True)

        acc = chip_sum((own_0, sib_0), hop)
        if rest > 1:
            acc = lax.psum_scatter(
                acc, "fsdp", scatter_dimension=0, tiled=True, axis_index_groups=rest_groups
            )
        home = lax.all_to_all(acc.reshape(8, dr, 3 * HALF), "fsdp", 0, 0, axis_index_groups=low_groups)
        gate_up_grad, down_grad = call(
            settle(dr), [((dr, 4, 2 * FF), F32), ((dr, 4, FF), F32)], [HB], [VM] * 2,
            [pltpu.VMEM((8, dr, UNIT), BF), pltpu.SemaphoreType.DMA((1,))], (home,), "settle", 48, 0,
        )

        near = [
            lax.dynamic_index_in_dim(outs, chip ^ t, 0, keepdims=False).astype(F32) for t in (1, 2, 3)
        ]
        output = (h1 + oown + near[0] + near[1] + near[2]).astype(BF)
        z_qkv = z_sum([
            jnp.concatenate(
                [rs_qkv[:, k * 512 : (k + 1) * 512], rs_out[:, k * 256 : (k + 1) * 256],
                 rs_out[:, 1024 : 1024 + 64], rs_qkv[:, 2048 : 2048 + 64]], axis=1
            )
            for k in range(groups)
        ])
        z_out = z_qkv[:, 512:]
        return (
            output,
            dx,
            z_out[:, 320],
            jnp.concatenate(swapped(z_qkv[:, :256]), axis=1),
            z_qkv[:, 256:384],
            z_qkv[:, 384:512],
            jnp.concatenate(swapped(z_out[:, :256]), axis=1),
            z_out[:, 256 + EXPERTS],
            z_out[:, 256 : 256 + EXPERTS],
            gate_up_grad,
            down_grad,
        )

    return shards


def solution(mesh):
    both = ("grp", "fsdp")
    in_specs = (
        P(both, None), P(both), P(both), P(both, None), P(both, None),
        P("fsdp"), P("fsdp", "grp"), P("fsdp", "grp"), P("fsdp", "grp"), P("fsdp", "grp"),
        P("fsdp"), P("fsdp", None), P("fsdp", "grp", None), P("fsdp", "grp", None), P(both, None),
    )
    out_specs = (
        P(both, None), P(both, None), P("fsdp"),
        P("fsdp", "grp"), P("fsdp", "grp"), P("fsdp", "grp"), P("fsdp", "grp"),
        P("fsdp"), P("fsdp", None), P("fsdp", "grp", None), P("fsdp", "grp", None),
    )
    shards = make_shards(mesh.shape["grp"], mesh.shape["fsdp"])
    return jax.shard_map(shards, mesh=mesh, in_specs=in_specs, out_specs=out_specs, check_vma=False)
```

```python
import math

import jax
import jax.numpy as jnp
from jax import lax
from jax.experimental import pallas as pl
from jax.experimental.pallas import tpu as pltpu
from jax.sharding import PartitionSpec as P

MODEL_WIDTH = 1024
HEAD_SIZE = 64
FF = 512
HALF = FF // 2
EXPERTS = 16
T = 384
LANES = 128
EPSILON = 1e-06
ROPE_BASE = 10000.0
NEG_FILL = -1e30
SCALE = 1.0 / math.sqrt(HEAD_SIZE)
BF = jnp.bfloat16
F32 = jnp.float32
COST = 1.0
VMEM_MIB = 62

NT = (((1,), (1,)), ((), ()))
TN = (((0,), (0,)), ((), ()))

VM = pl.BlockSpec(memory_space=pltpu.VMEM)
SM = pl.BlockSpec(memory_space=pltpu.SMEM)
HB = pl.BlockSpec(memory_space=pltpu.HBM)


def dot(a, b):
    return jnp.dot(a, b, preferred_element_type=F32)


def dotg(a, b, dims, **kw):
    return lax.dot_general(a, b, dims, preferred_element_type=F32, **kw)


def call(body, outs, in_specs, out_specs, scratch, args, name, vmem=48, flops=0):
    nbytes = sum(math.prod(a.shape) * a.dtype.itemsize for a in args)
    nbytes += sum(math.prod(s) * jnp.dtype(d).itemsize for s, d in outs)
    return pl.pallas_call(
        body,
        out_shape=[jax.ShapeDtypeStruct(s, d) for s, d in outs],
        in_specs=in_specs,
        out_specs=out_specs,
        scratch_shapes=scratch,
        compiler_params=pltpu.CompilerParams(vmem_limit_bytes=VMEM_MIB << 20),
        cost_estimate=pl.CostEstimate(
            flops=int(flops * COST), transcendentals=0, bytes_accessed=int(nbytes * COST)
        ),
        name=name,
    )(*args)


def after(x, *deps):
    return lax.optimization_barrier((x, *deps))[0]


def low_half(shape):
    return lax.broadcasted_iota(jnp.int32, shape, 1) < HEAD_SIZE


def turn(part, cos, sin, first):
    partner = jnp.where(first, pltpu.roll(part, 96, 1), pltpu.roll(part, 32, 1))
    return part * cos + partner * sin


def first_of_head(shape):
    return (lax.broadcasted_iota(jnp.int32, shape, 1) % HEAD_SIZE) < HEAD_SIZE // 2


def attn_rows(qkv_ref, bias_ref, b, c, low):
    rows = slice(c * LANES, (c + 1) * LANES)
    seen = (c + 1) * LANES
    qa = qkv_ref[b, rows, 0:LANES]
    qb = qkv_ref[b, rows, LANES : 2 * LANES]
    zero = jnp.zeros_like(qa)
    q = jnp.concatenate(
        [jnp.where(low, qa, zero), jnp.where(low, qb, zero), jnp.where(low, zero, qa), jnp.where(low, zero, qb)], axis=0
    )
    keys = qkv_ref[b, :seen, 256:384]
    bias = bias_ref[rows, :seen]
    s = dotg(q, keys, NT) * SCALE + jnp.concatenate([bias] * 4, axis=0)
    p = jnp.exp(s - jnp.max(s, axis=1, keepdims=True))
    p = p * (1.0 / jnp.sum(p, axis=1, keepdims=True))
    return rows, seen, q, keys, p


def fetch(pairs, sems, first=0):
    copies = [pltpu.make_async_copy(a, b, sems.at[first + i]) for i, (a, b) in enumerate(pairs)]
    for c in copies:
        c.start()
    return copies


def wait(copies):
    for c in copies:
        c.wait()


def attn_fwd(places, dr):
    n = len(places)

    def body(mine_ref, *refs):
        pieces = refs[:n]
        x_h, cos_h, sin_h, bias_h, wo_h = refs[n : n + 5]
        w_h, n1_h, qkv_h, att_h, h1_h, n2_h, rows_h = refs[n + 5 : n + 12]
        x, cos, sin, bias, wo, w, n1, qkv, att, h1, n2, small, si, so = refs[n + 12 :]
        mine = mine_ref[0]
        pairs = [(x_h, x), (cos_h, cos), (sin_h, sin)]
        for p, (bits, off, rows) in zip(pieces, places):
            at = 0 if bits is None else pl.multiple_of((mine ^ bits) * dr + off, math.gcd(dr, off))
            pairs.append((p, w.at[pl.ds(at, rows)]))
        pairs += [(bias_h, bias), (wo_h, wo)]
        copies = fetch(pairs, si)
        wait(copies[:-1])
        outs = fetch([(w.at[:, 0:2048], w_h)], so)
        small[...] = w[:, 2048:2176].astype(F32).T
        outs += fetch([(small, rows_h)], so, 7)
        attn_fwd_body(x, small.at[16:17], w, cos, sin, bias, n1, qkv, att)
        outs += fetch([(n1, n1_h), (qkv, qkv_h), (att, att_h)], so, 1)
        copies[-1].wait()
        mid(x, att, wo, small.at[17:18], h1, n2)
        outs += fetch([(n2, n2_h), (h1, h1_h)], so, 4)
        wait(outs)

    return body


def attn_fwd_body(x_ref, gain_ref, w_ref, cos_ref, sin_ref, bias_ref, n1_ref, qkv_ref, att_ref):
    x = x_ref[...].astype(F32)
    r1 = lax.rsqrt(jnp.mean(x * x, axis=1, keepdims=True) + EPSILON)
    n1 = (x * r1 * gain_ref[...]).astype(BF)
    n1_ref[...] = n1
    cos = cos_ref[...]
    sin = sin_ref[...]
    first = first_of_head((T, LANES))
    low = low_half((LANES, LANES))
    for b in range(4):
        raw = dot(n1, w_ref[:, b * 512 : (b + 1) * 512])
        for s in range(4):
            part = raw[:, s * LANES : (s + 1) * LANES]
            if s < 3:
                part = turn(part, cos, sin, first)
            qkv_ref[b, :, s * LANES : (s + 1) * LANES] = part.astype(BF)

    def block(b, carry):
        for c in range(3):
            rows, seen, q, keys, p = attn_rows(qkv_ref, bias_ref, b, c, low)
            o = dot(p.astype(BF), qkv_ref[b, :seen, 384:512])
            att_ref[b, rows, 0:LANES] = jnp.where(low, o[0:LANES], o[2 * LANES : 3 * LANES]).astype(BF)
            att_ref[b, rows, LANES : 2 * LANES] = jnp.where(low, o[LANES : 2 * LANES], o[3 * LANES :]).astype(BF)
        return carry

    for b in range(4):
        block(b, 0)


def soft_gates(n2, rt, mask):
    logits = dotg(n2, rt, NT)
    top = jnp.max(jnp.where(mask > 0, logits, NEG_FILL), axis=1, keepdims=True)
    e = jnp.where(mask > 0, jnp.exp(jnp.minimum(logits - top, 0.0)), 0.0)
    return e / jnp.sum(e, axis=1, keepdims=True)


def route_mask(routes):
    ids = lax.broadcasted_iota(jnp.int32, (LANES, T), 0).astype(F32)
    hit = jnp.zeros((LANES, T), F32)
    for i in range(8):
        hit = hit + jnp.where(ids == routes[i : i + 1, :], 1.0, 0.0)
    return hit.T


def mid(x_ref, att_ref, wo_ref, gain_ref, h1_ref, n2_ref):
    att = jnp.concatenate([att_ref[b] for b in range(4)], axis=1)
    h1 = x_ref[...].astype(F32) + dotg(att, wo_ref[...], NT)
    h1_ref[...] = h1
    r2 = lax.rsqrt(jnp.mean(h1 * h1, axis=1, keepdims=True) + EPSILON)
    n2_ref[...] = (h1 * r2 * gain_ref[...]).astype(BF)


ROWS = 4 * T
WIDE = 2 * HALF
UNIT = 3 * HALF
TREE = [slice(t * T, (t + 1) * T) for t in range(4)]


def token_pairs(srcs, dst):
    pairs, at = [], 0
    for r in srcs:
        pairs.append((r, dst.at[at : at + r.shape[0]]))
        at += r.shape[0]
    return pairs


def chip_pairs(src, chip, dst):
    return [
        (src.at[pl.ds(pl.multiple_of((chip ^ t) * T, T), T)], dst.at[t * T : (t + 1) * T]) for t in range(4)
    ]


def act(t, e, X, Y, W, GT, GH, DGU):
    rows = TREE[t]
    lanes = lax.broadcasted_iota(jnp.int32, (T, LANES), 1)
    gate = jnp.sum(jnp.where(lanes == e, GT[rows, :], 0.0), axis=1, keepdims=True)
    dgate = jnp.zeros((T, 1), F32)
    for u in range(2):
        gu = dot(X[rows, :], W[u, :, 0:WIDE])
        dh = dot(Y[rows, :], W[u, :, WIDE:UNIT])
        g = gu[:, :HALF]
        up = gu[:, HALF:]
        s = 0.5 * jnp.tanh(0.5 * g) + 0.5
        silu = g * s
        hid = silu * up
        GH[rows, u * HALF : (u + 1) * HALF] = (gate * hid).astype(BF)
        dgate = dgate + jnp.sum(dh * hid, axis=1, keepdims=True)
        dh = dh * gate
        base = u * WIDE
        DGU[rows, base : base + HALF] = (dh * up * (s + silu * (1.0 - s))).astype(BF)
        DGU[rows, base + HALF : base + WIDE] = (dh * silu).astype(BF)
    return jnp.where(lanes == e, dgate, 0.0)


def wgrad_down(Y, GH, DW):
    step = 256
    for r in range(MODEL_WIDTH // step):
        cols = slice(r * step, (r + 1) * step)
        dd = dotg(Y[:, cols], GH[...], TN)
        for u in range(2):
            DW[u, cols, WIDE:UNIT] = dd[:, u * HALF : (u + 1) * HALF].astype(BF)


def wgrad_up(X, DGU, DW):
    step = 256
    for r in range(MODEL_WIDTH // step):
        cols = slice(r * step, (r + 1) * step)
        dg = dotg(X[:, cols], DGU[...], TN)
        for u in range(2):
            DW[u, cols, 0:WIDE] = dg[:, u * WIDE : (u + 1) * WIDE].astype(BF)


def wgrad(X, Y, GH, DGU, DW):
    wgrad_down(Y, GH, DW)
    wgrad_up(X, DGU, DW)


def stage_scratch(n, extra, loads, stores):
    return [
        pltpu.VMEM((ROWS, MODEL_WIDTH), BF), pltpu.VMEM((ROWS, MODEL_WIDTH), BF),
        pltpu.VMEM((n, 2, MODEL_WIDTH, UNIT), BF),
        pltpu.VMEM((n, ROWS, FF), BF), pltpu.VMEM((n, ROWS, 2 * FF), BF),
        pltpu.VMEM((ROWS, LANES), F32), pltpu.VMEM((ROWS, LANES), F32),
        *extra,
        pltpu.SemaphoreType.DMA((loads,)), pltpu.SemaphoreType.DMA((stores,)),
    ]


def load_tokens(xs, dyg, chip, X, Y, head, rest, si):
    px, py = token_pairs(xs, X), chip_pairs(dyg, chip, Y)
    urgent = fetch(px[0:1] + head + py[0:1], si)
    wait(urgent)
    n = len(urgent)
    more = fetch([px[1], py[1], px[2], py[2], px[3], px[4], py[3]] + rest, si, n)
    return [[], more[0:2], more[2:4], more[4:7]], more[7:]


def stage_a(e_ref, *refs):
    xs, dyg, ws = refs[0:5], refs[5], refs[6:8]
    rt_h, routes = refs[8], refs[9:13]
    gh_h, dgu_h, dwo_h, dws_h, gates_h, dgate_h = refs[13:19]
    X, Y, W, GH, DGU, GT, DG, DW, rt, si, so = refs[19:]
    trees, _ = load_tokens(
        xs, dyg, e_ref[4], X, Y, [(rt_h, rt)] + [(ws[i], W.at[0, i]) for i in range(2)], [], si
    )
    router = rt[...].astype(BF)
    for t in range(4):
        wait(trees[t])
        GT[TREE[t], :] = soft_gates(X[TREE[t], :], router, route_mask(routes[t][...].astype(F32)))
        DG[TREE[t], :] = act(t, e_ref[1], X, Y, W.at[0], GT, GH.at[0], DGU.at[0])
    outs = fetch([(GH.at[0], gh_h), (DGU.at[0], dgu_h), (GT, gates_h), (DG, dgate_h)], so)
    wgrad(X, Y, GH.at[0], DGU.at[0], DW)
    outs += fetch([(DW.at[0], dwo_h), (DW.at[1], dws_h)], so, 4)
    wait(outs)


ACT_OUT = [((ROWS, FF), BF), ((ROWS, 2 * FF), BF)]
GATE_OUT = [((ROWS, LANES), F32)]
DW_OUT = [((MODEL_WIDTH, UNIT), BF)] * 2
DW_VMEM = pltpu.VMEM((2, MODEL_WIDTH, UNIT), BF)
EXPERT_FLOPS = 2 * ROWS * MODEL_WIDTH * 3 * FF


def run_stage_a(e, xs, dyg, pair, rt, routes):
    extra = [DW_VMEM, pltpu.VMEM((LANES, MODEL_WIDTH), F32)]
    return call(
        stage_a, ACT_OUT + DW_OUT + GATE_OUT * 2, [SM] + [HB] * 9 + [VM] * 4, [HB] * 6,
        stage_scratch(1, extra, 12, 6), (e, *xs, dyg, *pair, rt, *routes), "stage_a", 48, 2 * EXPERT_FLOPS,
    )


def stage_b(e_ref, *refs):
    xs, dyg, ws = refs[0:5], refs[5], refs[6:10]
    gates_h, dgate_i = refs[10:12]
    gh0_h, dgu0_h, gh2_h, dgu2_h, dgate_h, dwo_h, dws_h = refs[12:19]
    X, Y, W, GH, DGU, GT, DG, DW, si, so = refs[19:]
    hw = [(ws[i], W.at[i // 2, i % 2]) for i in range(4)]
    trees, second = load_tokens(
        xs, dyg, e_ref[4], X, Y, hw[0:2] + [(gates_h, GT), (dgate_i, DG)], hw[2:], si
    )
    for t in range(4):
        wait(trees[t])
        DG[TREE[t], :] += act(t, e_ref[0], X, Y, W.at[0], GT, GH.at[0], DGU.at[0])
    outs = fetch([(GH.at[0], gh0_h), (DGU.at[0], dgu0_h)], so)
    wait(second)
    for t in range(4):
        DG[TREE[t], :] += act(t, e_ref[2], X, Y, W.at[1], GT, GH.at[1], DGU.at[1])
    outs += fetch([(GH.at[1], gh2_h), (DGU.at[1], dgu2_h), (DG, dgate_h)], so, 2)
    wgrad(X, Y, GH.at[1], DGU.at[1], DW)
    outs += fetch([(DW.at[0], dwo_h), (DW.at[1], dws_h)], so, 5)
    wait(outs)


def run_stage_b(e, xs, dyg, ws, gates, dgate):
    return call(
        stage_b, ACT_OUT * 2 + GATE_OUT + DW_OUT, [SM] + [HB] * 12, [HB] * 7,
        stage_scratch(2, [DW_VMEM], 15, 7), (e, *xs, dyg, *ws, gates, dgate), "stage_b", 48, 3 * EXPERT_FLOPS,
    )


def stage_c(e_ref, *refs):
    xs, dyg, ws = refs[0:5], refs[5], refs[6:14]
    gates_h, dgate_i = refs[14:16]
    dgus = refs[16:19]
    gh_h, dgu_h, dgate_h, parts_h = refs[19:23]
    X, Y, W, GH, DGU, GT, DG, WB, DF, OUT, si, so = refs[23:]
    late = [(ws[i].at[:, 0:WIDE], WB.at[:, i * WIDE : (i + 1) * WIDE]) for i in range(6)]
    late += [(dgus[i].at[T:ROWS], DF.at[:, 2 * i * FF : 2 * (i + 1) * FF]) for i in range(3)]
    trees, late = load_tokens(
        xs, dyg, e_ref[4], X, Y,
        [(ws[6 + i], W.at[0, i]) for i in range(2)] + [(gates_h, GT), (dgate_i, DG)], late, si,
    )
    for t in range(4):
        wait(trees[t])
        DG[TREE[t], :] += act(t, e_ref[3], X, Y, W.at[0], GT, GH.at[0], DGU.at[0])
    outs = fetch([(GH.at[0], gh_h), (DGU.at[0], dgu_h), (DG, dgate_h)], so)
    wait(late)
    w = jnp.concatenate([WB[...]] + [W[0, i, :, 0:WIDE] for i in range(2)], axis=1)
    for i, t in enumerate((3, 1, 2)):
        a = jnp.concatenate([DF[TREE[t - 1], :], DGU[0, TREE[t], :]], axis=1)
        OUT[i, :, 0:MODEL_WIDTH] = dotg(a, w, NT).astype(BF)
        OUT[i, :, MODEL_WIDTH:] = DG[TREE[t], :].astype(BF)
        outs += fetch([(OUT.at[i], parts_h.at[e_ref[4] ^ t])], so, 3 + i)
    wait(outs)


def run_stage_c(e, xs, dyg, ws, gates, dgate, dgus):
    cols = MODEL_WIDTH + LANES
    extra = [
        pltpu.VMEM((MODEL_WIDTH, 6 * WIDE), BF), pltpu.VMEM((3 * T, 6 * FF), BF), pltpu.VMEM((3, T, cols), BF),
    ]
    return call(
        stage_c, ACT_OUT + GATE_OUT + [((4, T, cols), BF)], [SM] + [HB] * 19, [HB] * 4,
        stage_scratch(1, extra, 22, 6), (e, *xs, dyg, *ws, gates, dgate, *dgus), "stage_c", 48, 2 * EXPERT_FLOPS,
    )


def back_pairs(acts, ws, lo, m, width, first_col, A, W):
    pairs = []
    for k in range(4):
        pairs.append((acts[k].at[lo : lo + m], A.at[:, k * 2 * width : (k + 1) * 2 * width]))
        for u in range(2):
            at = (2 * k + u) * width
            pairs.append((ws[2 * k + u].at[:, first_col : first_col + width], W.at[:, at : at + width]))
    return pairs


def late_stage(e_ref, *refs):
    xs, dyg, gh_h, dgu_h = refs[0:5], refs[5], refs[6], refs[7]
    dgus, ws, dgate_h = refs[8:12], refs[12:20], refs[20]
    dwo_h, dws_h, own_h = refs[21:24]
    X, Y, GH, DGU, DW, A, W, DG, O, si, so = refs[24:]
    first = fetch(chip_pairs(dyg, e_ref[4], Y) + [(gh_h, GH)], si)
    wait(first)
    second = fetch(token_pairs(xs, X) + [(dgu_h, DGU)], si, 5)
    third = fetch(back_pairs(dgus, ws, 0, T, WIDE, 0, A, W) + [(dgate_h.at[0:T], DG)], si, 11)
    wgrad_down(Y, GH, DW)
    wait(second)
    wgrad_up(X, DGU, DW)
    outs = fetch([(DW.at[0], dwo_h), (DW.at[1], dws_h)], so)
    wait(third)
    O[:, 0:MODEL_WIDTH] = dotg(A[...], W[...], NT)
    O[:, MODEL_WIDTH:] = DG[...]
    outs += fetch([(O, own_h)], so, 2)
    wait(outs)


def run_late(e, xs, dyg, acts, back):
    cols = MODEL_WIDTH + LANES
    args = (e, *xs, dyg, *acts, *back)
    return call(
        late_stage, DW_OUT + [((T, cols), F32)], [SM] + [HB] * (len(args) - 1), [HB] * 3,
        [
            pltpu.VMEM((ROWS, MODEL_WIDTH), BF), pltpu.VMEM((ROWS, MODEL_WIDTH), BF),
            pltpu.VMEM((ROWS, FF), BF), pltpu.VMEM((ROWS, 2 * FF), BF), DW_VMEM,
            pltpu.VMEM((T, 8 * WIDE), BF), pltpu.VMEM((MODEL_WIDTH, 8 * WIDE), BF),
            pltpu.VMEM((T, LANES), F32), pltpu.VMEM((T, cols), F32),
            pltpu.SemaphoreType.DMA((24,)), pltpu.SemaphoreType.DMA((3,)),
        ],
        args, "late_stage", 52, 2 * EXPERT_FLOPS,
    )


def last_stage(e_ref, *refs):
    xs, dyg, gh_h, dgu_h = refs[0:5], refs[5], refs[6], refs[7]
    ghs, ws = refs[8:12], refs[12:20]
    dwo_h, dws_h, parts_h, own_h = refs[20:24]
    X, Y, GH, DGU, DW, A, W, O, OF, si, so = refs[24:]
    first = fetch(chip_pairs(dyg, e_ref[4], Y) + [(gh_h, GH)], si)
    wait(first)
    second = fetch(token_pairs(xs, X) + [(dgu_h, DGU)], si, 5)
    third = fetch(back_pairs(ghs, ws, 0, ROWS, HALF, WIDE, A, W), si, 11)
    wgrad_down(Y, GH, DW)
    wait(second)
    wgrad_up(X, DGU, DW)
    outs = fetch([(DW.at[0], dwo_h), (DW.at[1], dws_h)], so)
    wait(third)
    for i, t in enumerate((3, 1, 2, 0)):
        total = dotg(A[TREE[t], :], W[...], NT)
        dst = O.at[i] if t else OF
        dst[...] = total.astype(BF) if t else total
        outs += fetch([(dst, parts_h.at[e_ref[4] ^ t] if t else own_h)], so, 2 + i)
    wait(outs)


def run_last(e, xs, dyg, acts, ghs, ws):
    args = (e, *xs, dyg, *acts, *ghs, *ws)
    return call(
        last_stage, DW_OUT + [((4, T, MODEL_WIDTH), BF), ((T, MODEL_WIDTH), F32)],
        [SM] + [HB] * (len(args) - 1), [HB] * 4,
        [
            pltpu.VMEM((ROWS, MODEL_WIDTH), BF), pltpu.VMEM((ROWS, MODEL_WIDTH), BF),
            pltpu.VMEM((ROWS, FF), BF), pltpu.VMEM((ROWS, 2 * FF), BF), DW_VMEM,
            pltpu.VMEM((ROWS, 8 * HALF), BF), pltpu.VMEM((MODEL_WIDTH, 8 * HALF), BF),
            pltpu.VMEM((3, T, MODEL_WIDTH), BF), pltpu.VMEM((T, MODEL_WIDTH), F32),
            pltpu.SemaphoreType.DMA((23,)), pltpu.SemaphoreType.DMA((6,)),
        ],
        args, "last_stage", 52, 2 * EXPERT_FLOPS,
    )


def settle(dr):
    def body(home_h, gu_ref, dn_ref, H, sem):
        c = pltpu.make_async_copy(home_h, H, sem.at[0])
        c.start()
        c.wait()
        for e in range(4):
            for h in range(2):
                part = H[2 * e + h].astype(F32)
                cols = slice(h * HALF, (h + 1) * HALF)
                gu_ref[:, e, cols] = part[:, 0:HALF]
                gu_ref[:, e, FF + h * HALF : FF + (h + 1) * HALF] = part[:, HALF:WIDE]
                dn_ref[:, e, cols] = part[:, WIDE:UNIT]

    return body


def columns_of(rowwise, lane):
    total = jnp.sum(rowwise, axis=0, keepdims=True)
    total = jnp.broadcast_to(total, (LANES, MODEL_WIDTH)).T
    lanes = lax.broadcasted_iota(jnp.int32, total.shape, 1)
    return jnp.where(lanes == lane, total, 0.0)


def join(e_ref, p_h, parts_h, gates_h, h1_h, n2_h, dy_h, wo_h, att_h, small_h,
         dh1_h, datt_h, dwo_h, P, R, GT, H1, N2, DY, WO, ATT, SMALL, DH1, DATT, DWO, si, so):
    copies = fetch(
        [(p_h, P)] + [(parts_h.at[e_ref[4] ^ t], R.at[t - 1]) for t in (1, 2, 3)]
        + [(gates_h.at[0:T], GT), (h1_h, H1), (dy_h, DY),
         (small_h, SMALL), (wo_h, WO), (att_h, ATT), (n2_h, N2)], si
    )
    wait(copies[0:8])
    gates = GT[...]
    total = P[...] + R[0].astype(F32) + R[1].astype(F32) + R[2].astype(F32)
    dg = total[:, MODEL_WIDTH:]
    dl = (gates * (dg - jnp.sum(gates * dg, axis=1, keepdims=True))).astype(BF)
    dn2 = total[:, :MODEL_WIDTH] + dot(dl, SMALL[...].astype(BF))
    h1 = H1[...]
    gain = SMALL[17:18]
    r2 = lax.rsqrt(jnp.mean(h1 * h1, axis=1, keepdims=True) + EPSILON)
    gd = gain * dn2
    inner = jnp.mean(gd * h1, axis=1, keepdims=True)
    dh1 = DY[...].astype(F32) + r2 * gd - h1 * (r2 * r2 * r2 * inner)
    DH1[...] = dh1
    db = dh1.astype(BF)
    outs = fetch([(DH1, dh1_h)], so)
    wait(copies[8:])
    for b in range(4):
        cols = slice(b * 256, (b + 1) * 256)
        DATT[b] = dot(db, WO[:, cols]).astype(BF)
        DWO[:, cols] = dotg(db, ATT[b], TN).astype(BF)
    outs += fetch([(DATT, datt_h)], so, 1)
    extra = dotg(N2[...], dl, TN) + columns_of(dn2 * h1 * r2, EXPERTS)
    DWO[:, 1024:1152] = extra.astype(BF)
    outs += fetch([(DWO, dwo_h)], so, 2)
    wait(outs)


def run_join(args):
    cols = MODEL_WIDTH + LANES
    return call(
        join,
        [((T, MODEL_WIDTH), F32), ((4, T, 256), BF), ((MODEL_WIDTH, 1152), BF)],
        [SM] + [HB] * 9, [HB] * 3,
        [
            pltpu.VMEM((T, cols), F32), pltpu.VMEM((3, T, cols), BF), pltpu.VMEM((T, LANES), F32), pltpu.VMEM((T, MODEL_WIDTH), F32),
            pltpu.VMEM((T, MODEL_WIDTH), BF), pltpu.VMEM((T, MODEL_WIDTH), BF),
            pltpu.VMEM((MODEL_WIDTH, MODEL_WIDTH), BF), pltpu.VMEM((4, T, 256), BF),
            pltpu.VMEM((LANES, MODEL_WIDTH), F32),
            pltpu.VMEM((T, MODEL_WIDTH), F32), pltpu.VMEM((4, T, 256), BF), pltpu.VMEM((MODEL_WIDTH, 1152), BF),
            pltpu.SemaphoreType.DMA((12,)), pltpu.SemaphoreType.DMA((3,)),
        ],
        args, "join", 40, 2.0e9,
    )


def attn_bwd(split, dr):
    def body(mine_ref, x_h, w_h, cos_h, sin_h, bias_h, n1_h, qkv_h, datt_h, dh1_h, small_h, *refs):
        n = 5 if split else 2
        dx_h, grads_h = refs[0], refs[1:n]
        x, w, cos, sin, bias, n1, qkv, datt, dh1, gain, dx, dw, dqkv, dk, dv, si, so = refs[n : n + 17]
        copies = fetch(
            [(bias_h, bias), (qkv_h, qkv), (datt_h, datt), (cos_h, cos), (sin_h, sin), (n1_h, n1),
             (w_h, w), (x_h, x), (dh1_h, dh1), (small_h.at[16:24], gain)], si
        )
        wait(copies[0:5])
        attn_bwd_heads(cos, sin, bias, qkv, datt, dqkv, dk, dv)
        wait(copies[5:])
        attn_bwd_body(x, gain.at[0:1], w, n1, dh1, dx, dw, dqkv)
        outs = fetch([(dx, dx_h)], so)
        if split:
            for r in range(4):
                mine = 2 * r + (mine_ref[0] & 1)
                for i, j in enumerate((mine, mine ^ 1)):
                    src = dw.at[pl.ds(pl.multiple_of(j * dr, dr), dr)]
                    at = (r % 2) * dr
                    outs += fetch([(src, grads_h[2 * i + r // 2].at[at : at + dr])], so, 1 + 2 * r + i)
        else:
            outs += fetch([(dw, grads_h[0])], so, 1)
        wait(outs)

    return body


def run_attn_bwd(split, dr, args):
    grads = [((2 * dr, 2176), BF)] * 4 if split else [((MODEL_WIDTH, 2176), BF)]
    tile = pltpu.VMEM((T, LANES), F32)
    return call(
        attn_bwd(split, dr),
        [((T, MODEL_WIDTH), F32)] + grads,
        [SM] + [HB] * 10, [HB] * (1 + len(grads)),
        [
            pltpu.VMEM((T, MODEL_WIDTH), BF), pltpu.VMEM((MODEL_WIDTH, 2048), BF), tile, tile,
            pltpu.VMEM((T, T), F32), pltpu.VMEM((T, MODEL_WIDTH), BF), pltpu.VMEM((4, T, 512), BF),
            pltpu.VMEM((4, T, 256), BF), pltpu.VMEM((T, MODEL_WIDTH), F32), pltpu.VMEM((8, MODEL_WIDTH), F32),
            pltpu.VMEM((T, MODEL_WIDTH), F32),
            pltpu.VMEM((MODEL_WIDTH, 2176), BF), pltpu.VMEM((4, T, 512), BF), tile, tile,
            pltpu.SemaphoreType.DMA((10,)), pltpu.SemaphoreType.DMA((9,)),
        ],
        args, "attn_bwd", 40, 6.0e9,
    )


def attn_bwd_heads(cos_ref, sin_ref, bias_ref, qkv_ref, datt_ref, dqkv, dk, dv):
    low = low_half((LANES, LANES))
    first = first_of_head((T, LANES))

    def block(b, carry):
        for c in (2, 1, 0):
            rows, seen, q, keys, p = attn_rows(qkv_ref, bias_ref, b, c, low)
            da = datt_ref[b, rows, 0:LANES]
            db = datt_ref[b, rows, LANES : 2 * LANES]
            zero = jnp.zeros_like(da)
            do = jnp.concatenate(
                [jnp.where(low, da, zero), jnp.where(low, db, zero), jnp.where(low, zero, da), jnp.where(low, zero, db)],
                axis=0,
            )
            dp = dotg(do, qkv_ref[b, :seen, 384:512], NT)
            ds = (p * (dp - jnp.sum(p * dp, axis=1, keepdims=True))).astype(BF)
            dq = dot(ds, keys) * SCALE
            dkc = dotg(ds, q, TN)
            dvc = dotg(p.astype(BF), do, TN)
            if c == 2:
                dk[...] = dkc
                dv[...] = dvc
            else:
                dk[:seen] += dkc
                dv[:seen] += dvc
            cos = cos_ref[rows, :]
            sin = -sin_ref[rows, :]
            ta = jnp.where(low, dq[0:LANES], dq[2 * LANES : 3 * LANES])
            tb = jnp.where(low, dq[LANES : 2 * LANES], dq[3 * LANES :])
            dqkv[b, rows, 0:LANES] = turn(ta, cos, sin, first[rows]).astype(BF)
            dqkv[b, rows, LANES : 2 * LANES] = turn(tb, cos, sin, first[rows]).astype(BF)
        dqkv[b, :, 256:384] = turn(dk[...] * SCALE, cos_ref[...], -sin_ref[...], first).astype(BF)
        dqkv[b, :, 384:512] = dv[...].astype(BF)
        return carry

    for b in range(4):
        block(b, 0)


def attn_bwd_body(x_ref, gain_ref, w_ref, n1_ref, dh1_ref, dx_ref, dw_ref, dqkv):
    n1 = n1_ref[...]
    cat = jnp.concatenate([dqkv[b] for b in range(4)], axis=1)
    dn1 = dotg(cat, w_ref[...], NT)
    dw_ref[:, 0:2048] = dotg(n1, cat, TN).astype(BF)
    x = x_ref[...].astype(F32)
    gain = gain_ref[...]
    r1 = lax.rsqrt(jnp.mean(x * x, axis=1, keepdims=True) + EPSILON)
    gd = gain * dn1
    inner = jnp.mean(gd * x, axis=1, keepdims=True)
    dx_ref[...] = dh1_ref[...] + r1 * gd - x * (r1 * r1 * r1 * inner)
    dw_ref[:, 2048:2176] = columns_of(dn1 * x * r1, 0).astype(BF)
def visible_bias(segment, parents):
    ids = jnp.arange(parents.shape[0], dtype=jnp.int32)
    one = jnp.sum(jnp.where(segment[:, None] == ids[None, :], parents[None, :], 0), axis=1)
    two = jnp.sum(jnp.where(one[:, None] == ids[None, :], parents[None, :], 0), axis=1)
    key = segment[None, :]
    related = (key == segment[:, None]) | (key == one[:, None]) | (key == two[:, None])
    places = jnp.arange(segment.shape[0], dtype=jnp.int32)
    return jnp.where(related & (places[None, :] <= places[:, None]), 0.0, NEG_FILL).astype(F32)


def turn_tables(positions):
    half = HEAD_SIZE // 2
    lane = jnp.arange(LANES, dtype=jnp.int32)
    frequency = ROPE_BASE ** (-((lane % half).astype(F32) * 2.0) / HEAD_SIZE)
    angle = positions.astype(F32)[:, None] * frequency[None, :]
    sign = jnp.where(lane % HEAD_SIZE < half, -1.0, 1.0).astype(F32)
    return jnp.cos(angle), jnp.sin(angle) * sign[None, :]


def make_shards(groups, fsdp):
    ring = list(range(0, groups, 1))
    if groups == 4:
        ring = [0, 1, 3, 2]
    place = [ring.index(g) for g in range(groups)]
    rest = fsdp // 8

    def shifted(k):
        return [(ring[p], ring[(p + k) % groups]) for p in range(groups)]

    def flip(bits):
        return [(i, i ^ bits) for i in range(fsdp)]

    low_groups = None if rest == 1 else [[8 * r + j for j in range(8)] for r in range(rest)]
    core_groups = [[8 * r + 2 * c + k for c in range(4)] for r in range(rest) for k in range(2)]
    rest_groups = [[8 * r + j for r in range(rest)] for j in range(8)]

    def z_next(a):
        return lax.ppermute(a, "grp", shifted(1))

    def to_x(a):
        return lax.ppermute(a, "fsdp", flip(2))

    def to_y(a):
        return lax.ppermute(a, "fsdp", flip(4))

    def to_diag(a):
        return lax.ppermute(a, "fsdp", flip(6))

    def to_core(a):
        return lax.ppermute(a, "fsdp", flip(1))

    def plane(top, bot):
        xb = to_x(bot)
        yt = to_y(top)
        xt = to_x(top)
        yb = to_y(bot)
        return (top, bot, xt, xb, yt, yb, to_x(yt), to_y(xb))

    def swap(a):
        return lax.all_to_all(a, "fsdp", 0, 0, axis_index_groups=core_groups)

    def swap_all(a):
        return lax.all_to_all(a, "fsdp", 0, 0, axis_index_groups=low_groups)

    def z_sum(blocks):
        total = blocks[0].astype(F32)
        for k in range(1, groups):
            total = total + lax.ppermute(blocks[k], "grp", shifted(groups - k)).astype(F32)
        return total

    def shards(tokens, segment, positions, parents, routes, attn_gain, query_weight, key_matrix,
               value_matrix, out_weight, ffn_gain, router_weight, gate_up_weight, down_weight, cotangent):
        dr = query_weight.shape[0]
        mine = lax.axis_index("fsdp")
        spot = jnp.array(place, jnp.int32)[lax.axis_index("grp")]
        ring_ids = jnp.array(ring, jnp.int32)

        def swapped(w):
            return [w[:, 0:64], w[:, 128:192], w[:, 64:128], w[:, 192:256]]

        def z_gather(a):
            got = [a]
            for _ in range(groups - 1):
                got.append(z_next(got[-1]))
            return got

        half = T // 2
        tie = lax.optimization_barrier
        own_qkv = jnp.concatenate(swapped(query_weight) + [key_matrix, value_matrix], axis=1)
        own_out = jnp.concatenate(swapped(out_weight), axis=1)

        def z_all(a):
            return [a] + [lax.ppermute(a, "grp", shifted(k)) for k in range(1, groups)]

        route_rows = routes.T.astype(BF)
        route_rows = [route_rows, to_x(route_rows), to_y(route_rows), to_diag(route_rows)]

        gu = gate_up_weight.reshape(dr, 4, 2, 2, HALF)
        dn = down_weight.reshape(dr, 4, 1, 2, HALF)
        parts = jnp.concatenate([gu, dn], axis=2)
        parts = jnp.transpose(parts, (1, 3, 0, 2, 4)).reshape(8, dr, 3 * HALF)
        parts, own_qkv, own_out = tie((parts, own_qkv, own_out))
        blocks = z_all(jnp.concatenate([own_qkv, own_out], axis=1))
        unit = lax.all_to_all(parts, "fsdp", 0, 0, axis_index_groups=low_groups)
        unit = unit.reshape(8 * dr, 3 * HALF)
        if rest > 1:
            unit = lax.all_gather(unit, "fsdp", axis=0, tiled=True, axis_index_groups=rest_groups)

        bias = visible_bias(segment, parents[0])
        cos, sin = turn_tables(positions)
        chip = (mine // 2) % 4
        planes = ring_ids[(spot - jnp.arange(groups, dtype=jnp.int32)) % groups]
        e = jnp.concatenate([4 * planes + chip, chip[None]]).astype(jnp.int32)
        small = jnp.concatenate(
            [router_weight, attn_gain[:, None], ffn_gain[:, None], jnp.zeros((dr, LANES - 18), BF)], axis=1
        )
        bias, cos, sin, e, small, unit, *blocks = tie((bias, cos, sin, e, small, unit, *blocks))
        cols_qkv = jnp.concatenate([b[:, :512] for b in blocks] + [small], axis=1)
        cols_out = jnp.concatenate([b[:, 512:] for b in blocks], axis=1)
        mine_s = mine.astype(jnp.int32).reshape(1)
        units_1 = z_next(unit)
        if rest == 1:
            h = dr // 2
            qx = to_x(cols_qkv)
            qy = to_y(cols_qkv)
            qc = to_core(cols_qkv)
            qx, qy, qc = tie((qx, qy, qc))
            qa = to_x(qy[:h])
            qb = to_y(qx[h:])
            cx, cy = to_core(qx), to_core(qy)
            qa, qb, units_1 = tie((qa, qb, units_1))
            pieces = [cols_qkv, qx, qy, qa, qb, qc, cx, cy, to_core(qa), to_core(qb)]
            places = [(0, 0, dr), (2, 0, dr), (4, 0, dr), (6, 0, h), (6, h, h),
                      (1, 0, dr), (3, 0, dr), (5, 0, dr), (7, 0, h), (7, h, h)]
        else:
            pieces = [lax.all_gather(cols_qkv, "fsdp", axis=0, tiled=True)]
            places = [(None, 0, MODEL_WIDTH)]
        w_out = lax.all_gather(cols_out, "fsdp", axis=0, tiled=True)
        core_0 = to_core(after(unit, *pieces))
        dyg = lax.all_gather(after(cotangent, cols_out), "fsdp", axis=0, tiled=True, axis_index_groups=core_groups)
        tokens_f = after(tokens, *pieces, *route_rows)
        units_2 = z_next(units_1)
        w_qkv, n1, qkv, att, h1, n2, small = call(
            attn_fwd(places, dr),
            [((MODEL_WIDTH, 2048), BF), ((T, MODEL_WIDTH), BF), ((4, T, 512), BF), ((4, T, 256), BF),
             ((T, MODEL_WIDTH), F32), ((T, MODEL_WIDTH), BF), ((LANES, MODEL_WIDTH), F32)],
            [SM] + [HB] * (len(pieces) + 5), [HB] * 7,
            [
                pltpu.VMEM((T, MODEL_WIDTH), BF), pltpu.VMEM((T, LANES), F32), pltpu.VMEM((T, LANES), F32),
                pltpu.VMEM((T, T), F32), pltpu.VMEM((MODEL_WIDTH, MODEL_WIDTH), BF),
                pltpu.VMEM((MODEL_WIDTH, 2176), BF), pltpu.VMEM((T, MODEL_WIDTH), BF),
                pltpu.VMEM((4, T, 512), BF), pltpu.VMEM((4, T, 256), BF), pltpu.VMEM((T, MODEL_WIDTH), F32),
                pltpu.VMEM((T, MODEL_WIDTH), BF), pltpu.VMEM((LANES, MODEL_WIDTH), F32),
                pltpu.SemaphoreType.DMA((len(pieces) + 5,)), pltpu.SemaphoreType.DMA((8,)),
            ],
            (mine_s, *pieces, tokens_f, cos, sin, bias, w_out), "attn_fwd", 40, 4.0e9,
        )
        n2, core_0 = tie((n2, core_0))
        nx = to_x(n2)
        ny = to_y(n2)
        core_1 = to_core(after(units_1, n2))
        nx, ny, units_2 = tie((nx, ny, units_2))
        xs = (n2, nx, ny, to_x(ny[:half]), to_y(nx[half:]))
        core_1, *xs = tie((core_1, *xs))
        units_3 = z_next(units_2)
        core_2 = to_core(units_2)

        def chip_sum(pair, *more):
            total = pair[0].astype(F32) + pair[1].astype(F32)
            for m in more:
                total = total + m.astype(F32)
            return total.astype(BF)

        gh1, dgu1, own_1, sib_1, gates, dgate = run_stage_a(e, xs, dyg, (units_1, core_1), small, route_rows)
        core_2, gates = tie((core_2, gates))
        sib_1 = to_core(sib_1)
        gh0, dgu0, gh2, dgu2, dgate, own_2, sib_2 = run_stage_b(
            e, xs, dyg, (unit, core_0, units_2, core_2), gates, dgate
        )
        units_3, sib_1, dgate = tie((units_3, sib_1, dgate))
        core_3 = to_core(units_3)
        ws = (unit, core_0, units_1, core_1, units_2, core_2, units_3, core_3)
        sum_1, dgate = tie((chip_sum((own_1, sib_1)), dgate))
        hop = z_next(sum_1)
        sib_2 = to_core(sib_2)
        gh3, dgu3, dgate, parts = run_stage_c(e, xs, dyg, ws, gates, dgate, (dgu0, dgu1, dgu2))
        sib_2, dgate, parts = tie((sib_2, dgate, parts))
        parts = swap(parts)
        dgus = (dgu0, dgu1, dgu2, dgu3)
        own_3, sib_3, own = run_late(e, xs, dyg, (gh3, dgu3), (*dgus, *ws, dgate))
        hop, own, gh0 = tie((hop, own, gh0))
        sum_2, gh0 = tie((chip_sum((own_2, sib_2), hop), gh0))
        hop = z_next(sum_2)
        sib_3 = to_core(sib_3)
        own_0, sib_0, outs, oown = run_last(e, xs, dyg, (gh0, dgu0), (gh0, gh1, gh2, gh3), ws)
        parts, own, outs, sib_3 = tie((parts, own, outs, sib_3))
        sib_0 = to_core(sib_0)
        outs = swap(outs)
        dh1, datt, dwo = run_join((e, own, parts, gates, h1, n2, cotangent, w_out, att, small))
        hop, dh1, sib_0 = tie((hop, dh1, sib_0))
        sum_3, dh1 = tie((chip_sum((own_3, sib_3), hop), dh1))
        hop = z_next(sum_3)
        rs_out = lax.psum_scatter(dwo, "fsdp", scatter_dimension=0, tiled=True)
        dx, *dw = run_attn_bwd(
            rest == 1, dr, (mine_s, tokens, w_qkv, cos, sin, bias, n1, qkv, datt, dh1, small)
        )
        if rest == 1:
            sib_a, sib_b, hop, rs_out, outs = tie((to_core(dw[2]), to_core(dw[3]), hop, rs_out, outs))
            total = jnp.concatenate([dw[0].astype(F32) + sib_a.astype(F32), dw[1].astype(F32) + sib_b.astype(F32)])
            total = swap(total.astype(BF).reshape(4, dr, -1))
            acc = chip_sum((own_0, sib_0), hop)
            acc, total = tie((acc, total))
            home = swap_all(acc.reshape(8, dr, UNIT))
            rs_qkv = jnp.sum(total.astype(F32), axis=0).astype(BF)
        else:
            rs_qkv = lax.psum_scatter(dw[0], "fsdp", scatter_dimension=0, tiled=True)

        if rest > 1:
            acc = lax.psum_scatter(
                chip_sum((own_0, sib_0), hop), "fsdp", scatter_dimension=0, tiled=True,
                axis_index_groups=rest_groups,
            )
            home = swap_all(acc.reshape(8, dr, UNIT))
        gate_up_grad, down_grad = call(
            settle(dr), [((dr, 4, 2 * FF), F32), ((dr, 4, FF), F32)], [HB], [VM] * 2,
            [pltpu.VMEM((8, dr, UNIT), BF), pltpu.SemaphoreType.DMA((1,))], (home,), "settle", 48, 0,
        )

        near = [
            lax.dynamic_index_in_dim(outs, chip ^ t, 0, keepdims=False).astype(F32) for t in (1, 2, 3)
        ]
        output = (h1 + oown + near[0] + near[1] + near[2]).astype(BF)
        z_qkv = z_sum([
            jnp.concatenate(
                [rs_qkv[:, k * 512 : (k + 1) * 512], rs_out[:, k * 256 : (k + 1) * 256],
                 rs_out[:, 1024 : 1024 + 64], rs_qkv[:, 2048 : 2048 + 64]], axis=1
            )
            for k in range(groups)
        ])
        z_out = z_qkv[:, 512:]
        return (
            output,
            dx,
            z_out[:, 320],
            jnp.concatenate(swapped(z_qkv[:, :256]), axis=1),
            z_qkv[:, 256:384],
            z_qkv[:, 384:512],
            jnp.concatenate(swapped(z_out[:, :256]), axis=1),
            z_out[:, 256 + EXPERTS],
            z_out[:, 256 : 256 + EXPERTS],
            gate_up_grad,
            down_grad,
        )

    return shards


def solution(mesh):
    both = ("grp", "fsdp")
    in_specs = (
        P(both, None), P(both), P(both), P(both, None), P(both, None),
        P("fsdp"), P("fsdp", "grp"), P("fsdp", "grp"), P("fsdp", "grp"), P("fsdp", "grp"),
        P("fsdp"), P("fsdp", None), P("fsdp", "grp", None), P("fsdp", "grp", None), P(both, None),
    )
    out_specs = (
        P(both, None), P(both, None), P("fsdp"),
        P("fsdp", "grp"), P("fsdp", "grp"), P("fsdp", "grp"), P("fsdp", "grp"),
        P("fsdp"), P("fsdp", None), P("fsdp", "grp", None), P("fsdp", "grp", None),
    )
    shards = make_shards(mesh.shape["grp"], mesh.shape["fsdp"])
    return jax.shard_map(shards, mesh=mesh, in_specs=in_specs, out_specs=out_specs, check_vma=False)
```

```python
import functools
import math

import jax
import jax.numpy as jnp
from jax import lax
from jax.experimental import pallas as pl
from jax.experimental.pallas import tpu as pltpu
from jax.sharding import PartitionSpec as P

MODEL_WIDTH = 1024
HEAD_SIZE = 64
FF = 512
HALF = FF // 2
EXPERTS = 16
T = 384
LANES = 128
EPSILON = 1e-06
ROPE_BASE = 10000.0
NEG_FILL = -1e30
SCALE = 1.0 / math.sqrt(HEAD_SIZE)
BF = jnp.bfloat16
F32 = jnp.float32
COST = 1.0
VMEM_MIB = 62

NT = (((1,), (1,)), ((), ()))
TN = (((0,), (0,)), ((), ()))

VM = pl.BlockSpec(memory_space=pltpu.VMEM)
SM = pl.BlockSpec(memory_space=pltpu.SMEM)
HB = pl.BlockSpec(memory_space=pltpu.HBM)


def dot(a, b):
    return jnp.dot(a, b, preferred_element_type=F32)


def dotg(a, b, dims, **kw):
    return lax.dot_general(a, b, dims, preferred_element_type=F32, **kw)


def call(body, outs, in_specs, out_specs, scratch, args, name, vmem=48, flops=0):
    nbytes = sum(math.prod(a.shape) * a.dtype.itemsize for a in args)
    nbytes += sum(math.prod(s) * jnp.dtype(d).itemsize for s, d in outs)
    return pl.pallas_call(
        body,
        out_shape=[jax.ShapeDtypeStruct(s, d) for s, d in outs],
        in_specs=in_specs,
        out_specs=out_specs,
        scratch_shapes=scratch,
        compiler_params=pltpu.CompilerParams(vmem_limit_bytes=VMEM_MIB << 20),
        cost_estimate=pl.CostEstimate(
            flops=int(flops * COST), transcendentals=0, bytes_accessed=int(nbytes * COST)
        ),
        name=name,
    )(*args)


def after(x, *deps):
    return lax.optimization_barrier((x, *deps))[0]


def low_half(shape):
    return lax.broadcasted_iota(jnp.int32, shape, 1) < HEAD_SIZE


def turn(part, cos, sin, first):
    partner = jnp.where(first, pltpu.roll(part, 96, 1), pltpu.roll(part, 32, 1))
    return part * cos + partner * sin


def first_of_head(shape):
    return (lax.broadcasted_iota(jnp.int32, shape, 1) % HEAD_SIZE) < HEAD_SIZE // 2


def attn_rows(qkv_ref, bias_ref, b, c, low):
    rows = slice(c * LANES, (c + 1) * LANES)
    seen = (c + 1) * LANES
    qa = qkv_ref[b, rows, 0:LANES]
    qb = qkv_ref[b, rows, LANES : 2 * LANES]
    zero = jnp.zeros_like(qa)
    q = jnp.concatenate(
        [jnp.where(low, qa, zero), jnp.where(low, qb, zero), jnp.where(low, zero, qa), jnp.where(low, zero, qb)], axis=0
    )
    keys = qkv_ref[b, :seen, 256:384]
    bias = bias_ref[rows, :seen]
    s = dotg(q, keys, NT) * SCALE + jnp.concatenate([bias] * 4, axis=0)
    p = jnp.exp(s - jnp.max(s, axis=1, keepdims=True))
    p = p * (1.0 / jnp.sum(p, axis=1, keepdims=True))
    return rows, seen, q, keys, p


def fetch(pairs, sems, first=0):
    copies = [pltpu.make_async_copy(a, b, sems.at[first + i]) for i, (a, b) in enumerate(pairs)]
    for c in copies:
        c.start()
    return copies


def wait(copies):
    for c in copies:
        c.wait()


def attn_fwd(places, dr):
    n = len(places)

    def body(mine_ref, *refs):
        pieces = refs[:n]
        x_h, cos_h, sin_h, bias_h, wo_h = refs[n : n + 5]
        w_h, n1_h, qkv_h, att_h, h1_h, n2_h, rows_h = refs[n + 5 : n + 12]
        x, cos, sin, bias, wo, w, n1, qkv, att, h1, n2, small, si, so = refs[n + 12 :]
        mine = mine_ref[0]
        pairs = [(x_h, x), (cos_h, cos), (sin_h, sin)]
        for p, (bits, off, rows) in zip(pieces, places):
            at = 0 if bits is None else pl.multiple_of((mine ^ bits) * dr + off, math.gcd(dr, off))
            pairs.append((p, w.at[pl.ds(at, rows)]))
        pairs += [(bias_h, bias), (wo_h, wo)]
        copies = fetch(pairs, si)
        wait(copies[:-1])
        outs = fetch([(w.at[:, 0:2048], w_h)], so)
        small[...] = w[:, 2048:2176].astype(F32).T
        outs += fetch([(small, rows_h)], so, 7)
        attn_fwd_body(x, small.at[16:17], w, cos, sin, bias, n1, qkv, att)
        outs += fetch([(n1, n1_h), (qkv, qkv_h), (att, att_h)], so, 1)
        copies[-1].wait()
        mid(x, att, wo, small.at[17:18], h1, n2)
        outs += fetch([(n2, n2_h), (h1, h1_h)], so, 4)
        wait(outs)

    return body


def attn_fwd_body(x_ref, gain_ref, w_ref, cos_ref, sin_ref, bias_ref, n1_ref, qkv_ref, att_ref):
    x = x_ref[...].astype(F32)
    r1 = lax.rsqrt(jnp.mean(x * x, axis=1, keepdims=True) + EPSILON)
    n1 = (x * r1 * gain_ref[...]).astype(BF)
    n1_ref[...] = n1
    cos = cos_ref[...]
    sin = sin_ref[...]
    first = first_of_head((T, LANES))
    low = low_half((LANES, LANES))
    for b in range(4):
        raw = dot(n1, w_ref[:, b * 512 : (b + 1) * 512])
        for s in range(4):
            part = raw[:, s * LANES : (s + 1) * LANES]
            if s < 3:
                part = turn(part, cos, sin, first)
            qkv_ref[b, :, s * LANES : (s + 1) * LANES] = part.astype(BF)

    def block(b, carry):
        for c in range(3):
            rows, seen, q, keys, p = attn_rows(qkv_ref, bias_ref, b, c, low)
            o = dot(p.astype(BF), qkv_ref[b, :seen, 384:512])
            att_ref[b, rows, 0:LANES] = jnp.where(low, o[0:LANES], o[2 * LANES : 3 * LANES]).astype(BF)
            att_ref[b, rows, LANES : 2 * LANES] = jnp.where(low, o[LANES : 2 * LANES], o[3 * LANES :]).astype(BF)
        return carry

    for b in range(4):
        block(b, 0)


def soft_gates(n2, rt, mask):
    logits = dotg(n2, rt, NT)
    top = jnp.max(jnp.where(mask > 0, logits, NEG_FILL), axis=1, keepdims=True)
    e = jnp.where(mask > 0, jnp.exp(jnp.minimum(logits - top, 0.0)), 0.0)
    return e / jnp.sum(e, axis=1, keepdims=True)


def route_mask(routes):
    ids = lax.broadcasted_iota(jnp.int32, (LANES, T), 0).astype(F32)
    hit = jnp.zeros((LANES, T), F32)
    for i in range(8):
        hit = hit + jnp.where(ids == routes[i : i + 1, :], 1.0, 0.0)
    return hit.T


def mid(x_ref, att_ref, wo_ref, gain_ref, h1_ref, n2_ref):
    att = jnp.concatenate([att_ref[b] for b in range(4)], axis=1)
    h1 = x_ref[...].astype(F32) + dotg(att, wo_ref[...], NT)
    h1_ref[...] = h1
    r2 = lax.rsqrt(jnp.mean(h1 * h1, axis=1, keepdims=True) + EPSILON)
    n2_ref[...] = (h1 * r2 * gain_ref[...]).astype(BF)


ROWS = 4 * T
WIDE = 2 * HALF
UNIT = 3 * HALF
TREE = [slice(t * T, (t + 1) * T) for t in range(4)]


def token_pairs(srcs, dst):
    pairs, at = [], 0
    for r in srcs:
        pairs.append((r, dst.at[at : at + r.shape[0]]))
        at += r.shape[0]
    return pairs


def chip_pairs(src, chip, dst):
    return [
        (src.at[pl.ds(pl.multiple_of((chip ^ t) * T, T), T)], dst.at[t * T : (t + 1) * T]) for t in range(4)
    ]


def act(t, e, X, Y, W, GT, GH, DGU):
    rows = TREE[t]
    lanes = lax.broadcasted_iota(jnp.int32, (T, LANES), 1)
    gate = jnp.sum(jnp.where(lanes == e, GT[rows, :], 0.0), axis=1, keepdims=True)
    dgate = jnp.zeros((T, 1), F32)
    for u in range(2):
        gu = dot(X[rows, :], W[u, :, 0:WIDE])
        dh = dot(Y[rows, :], W[u, :, WIDE:UNIT])
        g = gu[:, :HALF]
        up = gu[:, HALF:]
        s = 0.5 * jnp.tanh(0.5 * g) + 0.5
        silu = g * s
        hid = silu * up
        GH[rows, u * HALF : (u + 1) * HALF] = (gate * hid).astype(BF)
        dgate = dgate + jnp.sum(dh * hid, axis=1, keepdims=True)
        dh = dh * gate
        base = u * WIDE
        DGU[rows, base : base + HALF] = (dh * up * (s + silu * (1.0 - s))).astype(BF)
        DGU[rows, base + HALF : base + WIDE] = (dh * silu).astype(BF)
    return jnp.where(lanes == e, dgate, 0.0)


def wgrad_down(Y, GH, DW):
    step = 256
    for r in range(MODEL_WIDTH // step):
        cols = slice(r * step, (r + 1) * step)
        dd = dotg(Y[:, cols], GH[...], TN)
        for u in range(2):
            DW[u, cols, WIDE:UNIT] = dd[:, u * HALF : (u + 1) * HALF].astype(BF)


def wgrad_up(X, DGU, DW):
    step = 256
    for r in range(MODEL_WIDTH // step):
        cols = slice(r * step, (r + 1) * step)
        dg = dotg(X[:, cols], DGU[...], TN)
        for u in range(2):
            DW[u, cols, 0:WIDE] = dg[:, u * WIDE : (u + 1) * WIDE].astype(BF)


def wgrad(X, Y, GH, DGU, DW):
    wgrad_down(Y, GH, DW)
    wgrad_up(X, DGU, DW)


def stage_scratch(n, extra, loads, stores):
    return [
        pltpu.VMEM((ROWS, MODEL_WIDTH), BF), pltpu.VMEM((ROWS, MODEL_WIDTH), BF),
        pltpu.VMEM((n, 2, MODEL_WIDTH, UNIT), BF),
        pltpu.VMEM((n, ROWS, FF), BF), pltpu.VMEM((n, ROWS, 2 * FF), BF),
        pltpu.VMEM((ROWS, LANES), F32), pltpu.VMEM((ROWS, LANES), F32),
        *extra,
        pltpu.SemaphoreType.DMA((loads,)), pltpu.SemaphoreType.DMA((stores,)),
    ]


def load_tokens(xs, dyg, chip, X, Y, head, rest, si):
    px, py = token_pairs(xs, X), chip_pairs(dyg, chip, Y)
    urgent = fetch(px[0:1] + head + py[0:1], si)
    wait(urgent)
    n = len(urgent)
    more = fetch([px[1], py[1], px[2], py[2], px[3], px[4], py[3]] + rest, si, n)
    return [[], more[0:2], more[2:4], more[4:7]], more[7:]


def stage_a(e_ref, *refs):
    xs, dyg, ws = refs[0:5], refs[5], refs[6:8]
    rt_h, routes = refs[8], refs[9:13]
    gh_h, dgu_h, dwo_h, dws_h, gates_h, dgate_h = refs[13:19]
    X, Y, W, GH, DGU, GT, DG, DW, rt, si, so = refs[19:]
    trees, _ = load_tokens(
        xs, dyg, e_ref[4], X, Y, [(rt_h, rt)] + [(ws[i], W.at[0, i]) for i in range(2)], [], si
    )
    router = rt[...].astype(BF)
    for t in range(4):
        wait(trees[t])
        GT[TREE[t], :] = soft_gates(X[TREE[t], :], router, route_mask(routes[t][...].astype(F32)))
        DG[TREE[t], :] = act(t, e_ref[1], X, Y, W.at[0], GT, GH.at[0], DGU.at[0])
    outs = fetch([(GH.at[0], gh_h), (DGU.at[0], dgu_h), (GT, gates_h), (DG, dgate_h)], so)
    wgrad(X, Y, GH.at[0], DGU.at[0], DW)
    outs += fetch([(DW.at[0], dwo_h), (DW.at[1], dws_h)], so, 4)
    wait(outs)


ACT_OUT = [((ROWS, FF), BF), ((ROWS, 2 * FF), BF)]
GATE_OUT = [((ROWS, LANES), F32)]
DW_OUT = [((MODEL_WIDTH, UNIT), BF)] * 2
DW_VMEM = pltpu.VMEM((2, MODEL_WIDTH, UNIT), BF)
EXPERT_FLOPS = 2 * ROWS * MODEL_WIDTH * 3 * FF


def run_stage_a(e, xs, dyg, pair, rt, routes):
    extra = [DW_VMEM, pltpu.VMEM((LANES, MODEL_WIDTH), F32)]
    return call(
        stage_a, ACT_OUT + DW_OUT + GATE_OUT * 2, [SM] + [HB] * 9 + [VM] * 4, [HB] * 6,
        stage_scratch(1, extra, 12, 6), (e, *xs, dyg, *pair, rt, *routes), "stage_a", 48, 2 * EXPERT_FLOPS,
    )


def stage_b(e_ref, *refs):
    xs, dyg, ws = refs[0:5], refs[5], refs[6:10]
    gates_h, dgate_i = refs[10:12]
    gh0_h, dgu0_h, gh2_h, dgu2_h, dgate_h = refs[12:17]
    X, Y, W, GH, DGU, GT, DG, si, so = refs[17:]
    hw = [(ws[i], W.at[i // 2, i % 2]) for i in range(4)]
    trees, second = load_tokens(
        xs, dyg, e_ref[4], X, Y, hw[0:2] + [(gates_h, GT), (dgate_i, DG)], hw[2:], si
    )
    for t in range(4):
        wait(trees[t])
        DG[TREE[t], :] += act(t, e_ref[0], X, Y, W.at[0], GT, GH.at[0], DGU.at[0])
    outs = fetch([(GH.at[0], gh0_h), (DGU.at[0], dgu0_h)], so)
    wait(second)
    for t in range(4):
        DG[TREE[t], :] += act(t, e_ref[2], X, Y, W.at[1], GT, GH.at[1], DGU.at[1])
    outs += fetch([(GH.at[1], gh2_h), (DGU.at[1], dgu2_h), (DG, dgate_h)], so, 2)
    wait(outs)


def run_stage_b(e, xs, dyg, ws, gates, dgate):
    return call(
        stage_b, ACT_OUT * 2 + GATE_OUT, [SM] + [HB] * 12, [HB] * 5,
        stage_scratch(2, [], 15, 5), (e, *xs, dyg, *ws, gates, dgate), "stage_b", 48, 2 * EXPERT_FLOPS,
    )


def stage_c(e_ref, *refs):
    xs, dyg, ws = refs[0:5], refs[5], refs[6:14]
    gates_h, dgate_i = refs[14:16]
    dgus = refs[16:19]
    gh_h, dgu_h, dgate_h, parts_h = refs[19:23]
    X, Y, W, GH, DGU, GT, DG, WB, DF, OUT, si, so = refs[23:]
    late = [(ws[i].at[:, 0:WIDE], WB.at[:, i * WIDE : (i + 1) * WIDE]) for i in range(6)]
    late += [(dgus[i].at[T:ROWS], DF.at[:, 2 * i * FF : 2 * (i + 1) * FF]) for i in range(3)]
    trees, late = load_tokens(
        xs, dyg, e_ref[4], X, Y,
        [(ws[6 + i], W.at[0, i]) for i in range(2)] + [(gates_h, GT), (dgate_i, DG)], late, si,
    )
    for t in range(4):
        wait(trees[t])
        DG[TREE[t], :] += act(t, e_ref[3], X, Y, W.at[0], GT, GH.at[0], DGU.at[0])
    outs = fetch([(GH.at[0], gh_h), (DGU.at[0], dgu_h), (DG, dgate_h)], so)
    wait(late)
    w = jnp.concatenate([WB[...]] + [W[0, i, :, 0:WIDE] for i in range(2)], axis=1)
    for i, t in enumerate((3, 1, 2)):
        a = jnp.concatenate([DF[TREE[t - 1], :], DGU[0, TREE[t], :]], axis=1)
        OUT[i, :, 0:MODEL_WIDTH] = dotg(a, w, NT).astype(BF)
        OUT[i, :, MODEL_WIDTH:] = DG[TREE[t], :].astype(BF)
        outs += fetch([(OUT.at[i], parts_h.at[e_ref[4] ^ t])], so, 3 + i)
    wait(outs)


def run_stage_c(e, xs, dyg, ws, gates, dgate, dgus):
    cols = MODEL_WIDTH + LANES
    extra = [
        pltpu.VMEM((MODEL_WIDTH, 6 * WIDE), BF), pltpu.VMEM((3 * T, 6 * FF), BF), pltpu.VMEM((3, T, cols), BF),
    ]
    return call(
        stage_c, ACT_OUT + GATE_OUT + [((4, T, cols), BF)], [SM] + [HB] * 19, [HB] * 4,
        stage_scratch(1, extra, 22, 6), (e, *xs, dyg, *ws, gates, dgate, *dgus), "stage_c", 48, 2 * EXPERT_FLOPS,
    )


def back_pairs(acts, ws, lo, m, width, first_col, A, W):
    pairs = []
    for k in range(4):
        pairs.append((acts[k].at[lo : lo + m], A.at[:, k * 2 * width : (k + 1) * 2 * width]))
        for u in range(2):
            at = (2 * k + u) * width
            pairs.append((ws[2 * k + u].at[:, first_col : first_col + width], W.at[:, at : at + width]))
    return pairs


def late_stage(e_ref, *refs):
    xs, dyg, gh_h, dgu_h = refs[0:5], refs[5], refs[6], refs[7]
    dgus, ws, dgate_h = refs[8:12], refs[12:20], refs[20]
    dwo_h, dws_h, own_h = refs[21:24]
    X, Y, GH, DGU, DW, A, W, DG, O, si, so = refs[24:]
    first = fetch(chip_pairs(dyg, e_ref[4], Y) + [(gh_h, GH)], si)
    wait(first)
    second = fetch(token_pairs(xs, X) + [(dgu_h, DGU)], si, 5)
    third = fetch(back_pairs(dgus, ws, 0, T, WIDE, 0, A, W) + [(dgate_h.at[0:T], DG)], si, 11)
    wgrad_down(Y, GH, DW)
    wait(second)
    wgrad_up(X, DGU, DW)
    outs = fetch([(DW.at[0], dwo_h), (DW.at[1], dws_h)], so)
    wait(third)
    O[:, 0:MODEL_WIDTH] = dotg(A[...], W[...], NT)
    O[:, MODEL_WIDTH:] = DG[...]
    outs += fetch([(O, own_h)], so, 2)
    wait(outs)


def run_late(e, xs, dyg, acts, back):
    cols = MODEL_WIDTH + LANES
    args = (e, *xs, dyg, *acts, *back)
    return call(
        late_stage, DW_OUT + [((T, cols), F32)], [SM] + [HB] * (len(args) - 1), [HB] * 3,
        [
            pltpu.VMEM((ROWS, MODEL_WIDTH), BF), pltpu.VMEM((ROWS, MODEL_WIDTH), BF),
            pltpu.VMEM((ROWS, FF), BF), pltpu.VMEM((ROWS, 2 * FF), BF), DW_VMEM,
            pltpu.VMEM((T, 8 * WIDE), BF), pltpu.VMEM((MODEL_WIDTH, 8 * WIDE), BF),
            pltpu.VMEM((T, LANES), F32), pltpu.VMEM((T, cols), F32),
            pltpu.SemaphoreType.DMA((24,)), pltpu.SemaphoreType.DMA((3,)),
        ],
        args, "late_stage", 52, 2 * EXPERT_FLOPS,
    )


def grads_stage(e_ref, *refs):
    xs, dyg, acts = refs[0:5], refs[5], refs[6:10]
    dws = refs[10:14]
    X, Y, GH, DGU, DW, si, so = refs[14:]
    first = fetch(chip_pairs(dyg, e_ref[4], Y) + [(acts[0], GH.at[0])], si)
    wait(first)
    second = fetch(token_pairs(xs, X) + [(acts[1], DGU.at[0])], si, 5)
    third = fetch([(acts[2], GH.at[1]), (acts[3], DGU.at[1])], si, 11)
    outs = []
    for i in range(2):
        wgrad_down(Y, GH.at[i], DW.at[i])
        if i == 0:
            wait(second)
        wgrad_up(X, DGU.at[i], DW.at[i])
        outs += fetch([(DW.at[i, 0], dws[2 * i]), (DW.at[i, 1], dws[2 * i + 1])], so, 2 * i)
        if i == 0:
            wait(third)
    wait(outs)


def run_grads(e, xs, dyg, acts):
    args = (e, *xs, dyg, *acts)
    return call(
        grads_stage, DW_OUT * 2, [SM] + [HB] * (len(args) - 1), [HB] * 4,
        [
            pltpu.VMEM((ROWS, MODEL_WIDTH), BF), pltpu.VMEM((ROWS, MODEL_WIDTH), BF),
            pltpu.VMEM((2, ROWS, FF), BF), pltpu.VMEM((2, ROWS, 2 * FF), BF),
            pltpu.VMEM((2, 2, MODEL_WIDTH, UNIT), BF),
            pltpu.SemaphoreType.DMA((13,)), pltpu.SemaphoreType.DMA((4,)),
        ],
        args, "grads_stage", 52, 2 * EXPERT_FLOPS,
    )


def out_stage(e_ref, *refs):
    ghs, ws = refs[0:4], refs[4:12]
    parts_h, own_h = refs[12:14]
    A, W, O, OF, si, so = refs[14:]
    wait(fetch(back_pairs(ghs, ws, 0, ROWS, HALF, WIDE, A, W), si))
    outs = []
    for i, t in enumerate((3, 1, 2, 0)):
        total = dotg(A[TREE[t], :], W[...], NT)
        dst = O.at[i] if t else OF
        dst[...] = total.astype(BF) if t else total
        outs += fetch([(dst, parts_h.at[e_ref[4] ^ t] if t else own_h)], so, i)
    wait(outs)


def run_out(e, ghs, ws):
    return call(
        out_stage, [((4, T, MODEL_WIDTH), BF), ((T, MODEL_WIDTH), F32)], [SM] + [HB] * 12, [HB] * 2,
        [
            pltpu.VMEM((ROWS, 8 * HALF), BF), pltpu.VMEM((MODEL_WIDTH, 8 * HALF), BF),
            pltpu.VMEM((3, T, MODEL_WIDTH), BF), pltpu.VMEM((T, MODEL_WIDTH), F32),
            pltpu.SemaphoreType.DMA((12,)), pltpu.SemaphoreType.DMA((4,)),
        ],
        (e, *ghs, *ws), "out_stage", 32, 2 * ROWS * MODEL_WIDTH * 8 * HALF,
    )


def fold(*refs):
    totals, outs, H, sem = refs[0:4], refs[4:8], refs[8], refs[9]
    wait(fetch([(t, H.at[i]) for i, t in enumerate(totals)], sem))
    for k, o in enumerate(outs):
        for at, first, width in ((0, k * 512, 512), (512, 2176 + k * 256, 256), (768, 2048, LANES), (896, 3200, LANES)):
            cols = slice(first, first + width)
            part = H[0, :, cols].astype(F32) + H[1, :, cols].astype(F32)
            part = part + (H[2, :, cols].astype(F32) + H[3, :, cols].astype(F32))
            o[:, at : at + width] = part.astype(BF)


def run_fold(total):
    dr, cols = total[0].shape
    return call(
        fold, [((dr, 1024), BF)] * 4, [HB] * 4, [VM] * 4,
        [pltpu.VMEM((4, dr, cols), BF), pltpu.SemaphoreType.DMA((4,))], total, "fold", 48, 0,
    )


def settle(dr):
    def body(home_h, gu_ref, dn_ref, H, sem):
        c = pltpu.make_async_copy(home_h, H, sem.at[0])
        c.start()
        c.wait()
        for e in range(4):
            for h in range(2):
                part = H[2 * e + h].astype(F32)
                cols = slice(h * HALF, (h + 1) * HALF)
                gu_ref[:, e, cols] = part[:, 0:HALF]
                gu_ref[:, e, FF + h * HALF : FF + (h + 1) * HALF] = part[:, HALF:WIDE]
                dn_ref[:, e, cols] = part[:, WIDE:UNIT]

    return body


def columns_of(rowwise, lane):
    total = jnp.sum(rowwise, axis=0, keepdims=True)
    total = jnp.broadcast_to(total, (LANES, MODEL_WIDTH)).T
    lanes = lax.broadcasted_iota(jnp.int32, total.shape, 1)
    return jnp.where(lanes == lane, total, 0.0)


def join(split, dr, e_ref, p_h, parts_h, gates_h, h1_h, n2_h, dy_h, wo_h, att_h, small_h,
         dh1_h, datt_h, *refs):
    n = 2 if split else 1
    dwo_h = refs[:n]
    P, R, GT, H1, N2, DY, WO, ATT, SMALL, DH1, DATT, DWO, si, so = refs[n:]
    copies = fetch(
        [(p_h, P)] + [(parts_h.at[e_ref[4] ^ t], R.at[t - 1]) for t in (1, 2, 3)]
        + [(gates_h.at[0:T], GT), (h1_h, H1), (dy_h, DY),
         (small_h, SMALL), (wo_h, WO), (att_h, ATT), (n2_h, N2)], si
    )
    wait(copies[0:8])
    gates = GT[...]
    total = P[...] + R[0].astype(F32) + R[1].astype(F32) + R[2].astype(F32)
    dg = total[:, MODEL_WIDTH:]
    dl = (gates * (dg - jnp.sum(gates * dg, axis=1, keepdims=True))).astype(BF)
    dn2 = total[:, :MODEL_WIDTH] + dot(dl, SMALL[...].astype(BF))
    h1 = H1[...]
    gain = SMALL[17:18]
    r2 = lax.rsqrt(jnp.mean(h1 * h1, axis=1, keepdims=True) + EPSILON)
    gd = gain * dn2
    inner = jnp.mean(gd * h1, axis=1, keepdims=True)
    dh1 = DY[...].astype(F32) + r2 * gd - h1 * (r2 * r2 * r2 * inner)
    DH1[...] = dh1
    db = dh1.astype(BF)
    outs = fetch([(DH1, dh1_h)], so)
    wait(copies[8:])
    for b in range(4):
        cols = slice(b * 256, (b + 1) * 256)
        DATT[b] = dot(db, WO[:, cols]).astype(BF)
        DWO[:, cols] = dotg(db, ATT[b], TN).astype(BF)
    outs += fetch([(DATT, datt_h)], so, 1)
    extra = dotg(N2[...], dl, TN) + columns_of(dn2 * h1 * r2, EXPERTS)
    DWO[:, 1024:1152] = extra.astype(BF)
    if split:
        for r in range(4):
            mine = 2 * (e_ref[4] ^ r) + e_ref[5]
            for i, at in enumerate((mine, mine ^ 1)):
                src = DWO.at[pl.ds(pl.multiple_of(at * dr, dr), dr)]
                outs += fetch([(src, dwo_h[i].at[r * dr : (r + 1) * dr])], so, 2 + 2 * r + i)
    else:
        outs += fetch([(DWO, dwo_h[0])], so, 2)
    wait(outs)


def run_join(split, dr, args):
    cols = MODEL_WIDTH + LANES
    grads = [((4 * dr, 1152), BF)] * 2 if split else [((MODEL_WIDTH, 1152), BF)]
    return call(
        functools.partial(join, split, dr),
        [((T, MODEL_WIDTH), F32), ((4, T, 256), BF)] + grads,
        [SM] + [HB] * 9, [HB] * (2 + len(grads)),
        [
            pltpu.VMEM((T, cols), F32), pltpu.VMEM((3, T, cols), BF), pltpu.VMEM((T, LANES), F32), pltpu.VMEM((T, MODEL_WIDTH), F32),
            pltpu.VMEM((T, MODEL_WIDTH), BF), pltpu.VMEM((T, MODEL_WIDTH), BF),
            pltpu.VMEM((MODEL_WIDTH, MODEL_WIDTH), BF), pltpu.VMEM((4, T, 256), BF),
            pltpu.VMEM((LANES, MODEL_WIDTH), F32),
            pltpu.VMEM((T, MODEL_WIDTH), F32), pltpu.VMEM((4, T, 256), BF), pltpu.VMEM((MODEL_WIDTH, 1152), BF),
            pltpu.SemaphoreType.DMA((12,)), pltpu.SemaphoreType.DMA((10,)),
        ],
        args, "join", 40, 2.0e9,
    )


def attn_bwd(split, dr):
    def body(mine_ref, x_h, w_h, cos_h, sin_h, bias_h, n1_h, qkv_h, datt_h, dh1_h, small_h, *refs):
        n = 5 if split else 2
        dx_h, grads_h = refs[0], refs[1:n]
        x, w, cos, sin, bias, n1, qkv, datt, dh1, gain, dx, dw, dqkv, dk, dv, si, so = refs[n : n + 17]
        copies = fetch(
            [(bias_h, bias), (qkv_h, qkv), (datt_h, datt), (cos_h, cos), (sin_h, sin), (n1_h, n1),
             (w_h, w), (x_h, x), (dh1_h, dh1), (small_h.at[16:24], gain)], si
        )
        wait(copies[0:5])
        attn_bwd_heads(cos, sin, bias, qkv, datt, dqkv, dk, dv)
        wait(copies[5:])
        attn_bwd_body(x, gain.at[0:1], w, n1, dh1, dx, dw, dqkv)
        outs = fetch([(dx, dx_h)], so)
        if split:
            for r in range(4):
                mine = mine_ref[0] ^ (2 * r)
                for i, j in enumerate((mine, mine ^ 1)):
                    src = dw.at[pl.ds(pl.multiple_of(j * dr, dr), dr)]
                    at = (r % 2) * dr
                    outs += fetch([(src, grads_h[2 * i + r // 2].at[at : at + dr])], so, 1 + 2 * r + i)
        else:
            outs += fetch([(dw, grads_h[0])], so, 1)
        wait(outs)

    return body


def run_attn_bwd(split, dr, args):
    grads = [((2 * dr, 2176), BF)] * 4 if split else [((MODEL_WIDTH, 2176), BF)]
    tile = pltpu.VMEM((T, LANES), F32)
    return call(
        attn_bwd(split, dr),
        [((T, MODEL_WIDTH), F32)] + grads,
        [SM] + [HB] * 10, [HB] * (1 + len(grads)),
        [
            pltpu.VMEM((T, MODEL_WIDTH), BF), pltpu.VMEM((MODEL_WIDTH, 2048), BF), tile, tile,
            pltpu.VMEM((T, T), F32), pltpu.VMEM((T, MODEL_WIDTH), BF), pltpu.VMEM((4, T, 512), BF),
            pltpu.VMEM((4, T, 256), BF), pltpu.VMEM((T, MODEL_WIDTH), F32), pltpu.VMEM((8, MODEL_WIDTH), F32),
            pltpu.VMEM((T, MODEL_WIDTH), F32),
            pltpu.VMEM((MODEL_WIDTH, 2176), BF), pltpu.VMEM((4, T, 512), BF), tile, tile,
            pltpu.SemaphoreType.DMA((10,)), pltpu.SemaphoreType.DMA((9,)),
        ],
        args, "attn_bwd", 40, 6.0e9,
    )


def attn_bwd_heads(cos_ref, sin_ref, bias_ref, qkv_ref, datt_ref, dqkv, dk, dv):
    low = low_half((LANES, LANES))
    first = first_of_head((T, LANES))

    def block(b, carry):
        for c in (2, 1, 0):
            rows, seen, q, keys, p = attn_rows(qkv_ref, bias_ref, b, c, low)
            da = datt_ref[b, rows, 0:LANES]
            db = datt_ref[b, rows, LANES : 2 * LANES]
            zero = jnp.zeros_like(da)
            do = jnp.concatenate(
                [jnp.where(low, da, zero), jnp.where(low, db, zero), jnp.where(low, zero, da), jnp.where(low, zero, db)],
                axis=0,
            )
            dp = dotg(do, qkv_ref[b, :seen, 384:512], NT)
            ds = (p * (dp - jnp.sum(p * dp, axis=1, keepdims=True))).astype(BF)
            dq = dot(ds, keys) * SCALE
            dkc = dotg(ds, q, TN)
            dvc = dotg(p.astype(BF), do, TN)
            if c == 2:
                dk[...] = dkc
                dv[...] = dvc
            else:
                dk[:seen] += dkc
                dv[:seen] += dvc
            cos = cos_ref[rows, :]
            sin = -sin_ref[rows, :]
            ta = jnp.where(low, dq[0:LANES], dq[2 * LANES : 3 * LANES])
            tb = jnp.where(low, dq[LANES : 2 * LANES], dq[3 * LANES :])
            dqkv[b, rows, 0:LANES] = turn(ta, cos, sin, first[rows]).astype(BF)
            dqkv[b, rows, LANES : 2 * LANES] = turn(tb, cos, sin, first[rows]).astype(BF)
        dqkv[b, :, 256:384] = turn(dk[...] * SCALE, cos_ref[...], -sin_ref[...], first).astype(BF)
        dqkv[b, :, 384:512] = dv[...].astype(BF)
        return carry

    for b in range(4):
        block(b, 0)


def attn_bwd_body(x_ref, gain_ref, w_ref, n1_ref, dh1_ref, dx_ref, dw_ref, dqkv):
    n1 = n1_ref[...]
    cat = jnp.concatenate([dqkv[b] for b in range(4)], axis=1)
    dn1 = dotg(cat, w_ref[...], NT)
    dw_ref[:, 0:2048] = dotg(n1, cat, TN).astype(BF)
    x = x_ref[...].astype(F32)
    gain = gain_ref[...]
    r1 = lax.rsqrt(jnp.mean(x * x, axis=1, keepdims=True) + EPSILON)
    gd = gain * dn1
    inner = jnp.mean(gd * x, axis=1, keepdims=True)
    dx_ref[...] = dh1_ref[...] + r1 * gd - x * (r1 * r1 * r1 * inner)
    dw_ref[:, 2048:2176] = columns_of(dn1 * x * r1, 0).astype(BF)
def visible_bias(segment, parents):
    ids = jnp.arange(parents.shape[0], dtype=jnp.int32)
    one = jnp.sum(jnp.where(segment[:, None] == ids[None, :], parents[None, :], 0), axis=1)
    two = jnp.sum(jnp.where(one[:, None] == ids[None, :], parents[None, :], 0), axis=1)
    key = segment[None, :]
    related = (key == segment[:, None]) | (key == one[:, None]) | (key == two[:, None])
    places = jnp.arange(segment.shape[0], dtype=jnp.int32)
    return jnp.where(related & (places[None, :] <= places[:, None]), 0.0, NEG_FILL).astype(F32)


def turn_tables(positions):
    half = HEAD_SIZE // 2
    lane = jnp.arange(LANES, dtype=jnp.int32)
    frequency = ROPE_BASE ** (-((lane % half).astype(F32) * 2.0) / HEAD_SIZE)
    angle = positions.astype(F32)[:, None] * frequency[None, :]
    sign = jnp.where(lane % HEAD_SIZE < half, -1.0, 1.0).astype(F32)
    return jnp.cos(angle), jnp.sin(angle) * sign[None, :]


def make_shards(groups, fsdp):
    ring = list(range(0, groups, 1))
    if groups == 4:
        ring = [0, 1, 3, 2]
    place = [ring.index(g) for g in range(groups)]
    rest = fsdp // 8

    def shifted(k):
        return [(ring[p], ring[(p + k) % groups]) for p in range(groups)]

    def flip(bits):
        return [(i, i ^ bits) for i in range(fsdp)]

    low_groups = None if rest == 1 else [[8 * r + j for j in range(8)] for r in range(rest)]
    core_groups = [[8 * r + 2 * c + k for c in range(4)] for r in range(rest) for k in range(2)]
    rest_groups = [[8 * r + j for r in range(rest)] for j in range(8)]

    def z_next(a):
        return lax.ppermute(a, "grp", shifted(1))

    def to_x(a):
        return lax.ppermute(a, "fsdp", flip(2))

    def to_y(a):
        return lax.ppermute(a, "fsdp", flip(4))

    def to_diag(a):
        return lax.ppermute(a, "fsdp", flip(6))

    def to_core(a):
        return lax.ppermute(a, "fsdp", flip(1))

    def plane(top, bot):
        xb = to_x(bot)
        yt = to_y(top)
        xt = to_x(top)
        yb = to_y(bot)
        return (top, bot, xt, xb, yt, yb, to_x(yt), to_y(xb))

    def swap(a):
        return lax.all_to_all(a, "fsdp", 0, 0, axis_index_groups=core_groups)

    def swap_all(a):
        return lax.all_to_all(a, "fsdp", 0, 0, axis_index_groups=low_groups)

    def z_sum(blocks):
        total = blocks[0].astype(F32)
        for k in range(1, groups):
            total = total + lax.ppermute(blocks[k], "grp", shifted(groups - k)).astype(F32)
        return total

    def shards(tokens, segment, positions, parents, routes, attn_gain, query_weight, key_matrix,
               value_matrix, out_weight, ffn_gain, router_weight, gate_up_weight, down_weight, cotangent):
        dr = query_weight.shape[0]
        mine = lax.axis_index("fsdp")
        spot = jnp.array(place, jnp.int32)[lax.axis_index("grp")]
        ring_ids = jnp.array(ring, jnp.int32)

        def swapped(w):
            return [w[:, 0:64], w[:, 128:192], w[:, 64:128], w[:, 192:256]]

        def z_gather(a):
            got = [a]
            for _ in range(groups - 1):
                got.append(z_next(got[-1]))
            return got

        half = T // 2
        tie = lax.optimization_barrier
        own_qkv = jnp.concatenate(swapped(query_weight) + [key_matrix, value_matrix], axis=1)
        own_out = jnp.concatenate(swapped(out_weight), axis=1)

        def z_all(a):
            return [a] + [lax.ppermute(a, "grp", shifted(k)) for k in range(1, groups)]

        route_rows = routes.T.astype(BF)
        route_rows = [route_rows, to_x(route_rows), to_y(route_rows), to_diag(route_rows)]

        gu = gate_up_weight.reshape(dr, 4, 2, 2, HALF)
        dn = down_weight.reshape(dr, 4, 1, 2, HALF)
        parts = jnp.concatenate([gu, dn], axis=2)
        parts = jnp.transpose(parts, (1, 3, 0, 2, 4)).reshape(8, dr, 3 * HALF)
        parts, own_qkv, own_out = tie((parts, own_qkv, own_out))
        blocks = z_all(jnp.concatenate([own_qkv, own_out], axis=1))
        unit = lax.all_to_all(parts, "fsdp", 0, 0, axis_index_groups=low_groups)
        unit = unit.reshape(8 * dr, 3 * HALF)
        if rest > 1:
            unit = lax.all_gather(unit, "fsdp", axis=0, tiled=True, axis_index_groups=rest_groups)

        bias = visible_bias(segment, parents[0])
        cos, sin = turn_tables(positions)
        chip = (mine // 2) % 4
        planes = ring_ids[(spot - jnp.arange(groups, dtype=jnp.int32)) % groups]
        e = jnp.concatenate([4 * planes + chip, chip[None], (mine % 2)[None]]).astype(jnp.int32)
        small = jnp.concatenate(
            [router_weight, attn_gain[:, None], ffn_gain[:, None], jnp.zeros((dr, LANES - 18), BF)], axis=1
        )
        bias, cos, sin, e, small, unit, *blocks = tie((bias, cos, sin, e, small, unit, *blocks))
        cols_qkv = jnp.concatenate([b[:, :512] for b in blocks] + [small], axis=1)
        cols_out = jnp.concatenate([b[:, 512:] for b in blocks], axis=1)
        mine_s = mine.astype(jnp.int32).reshape(1)
        units_1 = z_next(unit)
        if rest == 1:
            h = dr // 2
            qx = to_x(cols_qkv)
            qy = to_y(cols_qkv)
            qc = to_core(cols_qkv)
            qx, qy, qc = tie((qx, qy, qc))
            qa = to_x(qy[:h])
            qb = to_y(qx[h:])
            cx, cy = to_core(qx), to_core(qy)
            qa, qb, units_1 = tie((qa, qb, units_1))
            pieces = [cols_qkv, qx, qy, qa, qb, qc, cx, cy, to_core(qa), to_core(qb)]
            places = [(0, 0, dr), (2, 0, dr), (4, 0, dr), (6, 0, h), (6, h, h),
                      (1, 0, dr), (3, 0, dr), (5, 0, dr), (7, 0, h), (7, h, h)]
        else:
            pieces = [lax.all_gather(cols_qkv, "fsdp", axis=0, tiled=True)]
            places = [(None, 0, MODEL_WIDTH)]
        w_out = lax.all_gather(cols_out, "fsdp", axis=0, tiled=True)
        core_0 = to_core(after(unit, *pieces))
        dyg = lax.all_gather(after(cotangent, cols_out), "fsdp", axis=0, tiled=True, axis_index_groups=core_groups)
        tokens_f = after(tokens, *pieces)
        units_2 = z_next(units_1)
        w_qkv, n1, qkv, att, h1, n2, small = call(
            attn_fwd(places, dr),
            [((MODEL_WIDTH, 2048), BF), ((T, MODEL_WIDTH), BF), ((4, T, 512), BF), ((4, T, 256), BF),
             ((T, MODEL_WIDTH), F32), ((T, MODEL_WIDTH), BF), ((LANES, MODEL_WIDTH), F32)],
            [SM] + [HB] * (len(pieces) + 5), [HB] * 7,
            [
                pltpu.VMEM((T, MODEL_WIDTH), BF), pltpu.VMEM((T, LANES), F32), pltpu.VMEM((T, LANES), F32),
                pltpu.VMEM((T, T), F32), pltpu.VMEM((MODEL_WIDTH, MODEL_WIDTH), BF),
                pltpu.VMEM((MODEL_WIDTH, 2176), BF), pltpu.VMEM((T, MODEL_WIDTH), BF),
                pltpu.VMEM((4, T, 512), BF), pltpu.VMEM((4, T, 256), BF), pltpu.VMEM((T, MODEL_WIDTH), F32),
                pltpu.VMEM((T, MODEL_WIDTH), BF), pltpu.VMEM((LANES, MODEL_WIDTH), F32),
                pltpu.SemaphoreType.DMA((len(pieces) + 5,)), pltpu.SemaphoreType.DMA((8,)),
            ],
            (mine_s, *pieces, tokens_f, cos, sin, bias, w_out), "attn_fwd", 40, 4.0e9,
        )
        n2, core_0 = tie((n2, core_0))
        nx = to_x(n2)
        ny = to_y(n2)
        core_1 = to_core(after(units_1, n2))
        nx, ny, units_2 = tie((nx, ny, units_2))
        xs = (n2, nx, ny, to_x(ny[:half]), to_y(nx[half:]))
        core_1, *xs = tie((core_1, *xs))
        units_3 = z_next(units_2)
        core_2 = to_core(units_2)

        def chip_sum(pair, *more):
            total = pair[0].astype(F32) + pair[1].astype(F32)
            for m in more:
                total = total + m.astype(F32)
            return total.astype(BF)

        gh1, dgu1, own_1, sib_1, gates, dgate = run_stage_a(e, xs, dyg, (units_1, core_1), small, route_rows)
        core_2, gates = tie((core_2, gates))
        sib_1 = to_core(sib_1)
        gh0, dgu0, gh2, dgu2, dgate = run_stage_b(e, xs, dyg, (unit, core_0, units_2, core_2), gates, dgate)
        units_3, sib_1, dgate = tie((units_3, sib_1, dgate))
        core_3 = to_core(units_3)
        ws = (unit, core_0, units_1, core_1, units_2, core_2, units_3, core_3)
        sum_1, dgate = tie((chip_sum((own_1, sib_1)), dgate))
        hop = z_next(sum_1)
        gh3, dgu3, dgate, parts = run_stage_c(e, xs, dyg, ws, gates, dgate, (dgu0, dgu1, dgu2))
        dgate, parts = tie((dgate, parts))
        parts = swap(parts)
        dgus = (dgu0, dgu1, dgu2, dgu3)
        own_2, sib_2, own = run_late(e, xs, dyg, (gh2, dgu2), (*dgus, *ws, dgate))
        sib_2 = to_core(sib_2)
        hop, own, gh3 = tie((hop, own, gh3))
        own_3, sib_3, own_0, sib_0 = run_grads(e, xs, dyg, (gh3, dgu3, gh0, dgu0))
        sib_2, gh0, own_3 = tie((sib_2, gh0, own_3))
        sum_2, gh0 = tie((chip_sum((own_2, sib_2), hop), gh0))
        hop = z_next(sum_2)
        sib_3 = to_core(sib_3)
        sib_0 = to_core(sib_0)
        outs, oown = run_out(e, (gh0, gh1, gh2, gh3), ws)
        parts, own, outs, sib_3, sib_0 = tie((parts, own, outs, sib_3, sib_0))
        outs = swap(outs)
        dh1, datt, *dwo = run_join(
            rest == 1, dr, (e, own, parts, gates, h1, n2, cotangent, w_out, att, small)
        )
        if rest == 1:
            sib_o = to_core(dwo[1])
        else:
            rs_out = lax.psum_scatter(dwo[0], "fsdp", scatter_dimension=0, tiled=True)
        dx, *dw = run_attn_bwd(
            rest == 1, dr, (mine_s, tokens, w_qkv, cos, sin, bias, n1, qkv, datt, dh1, small)
        )
        hop, *dw = tie((hop, *dw))
        hop = z_next(chip_sum((own_3, sib_3), hop))
        if rest == 1:
            sib_a, sib_b, sib_o, outs = tie((to_core(dw[2]), to_core(dw[3]), sib_o, outs))
            def chip_part(r):
                pair = (dw[r // 2], sib_a if r < 2 else sib_b)
                here = slice((r % 2) * dr, (r % 2 + 1) * dr)
                there = slice(r * dr, (r + 1) * dr)
                return jnp.concatenate([
                    pair[0][here].astype(F32) + pair[1][here].astype(F32),
                    dwo[0][there].astype(F32) + sib_o[there].astype(F32),
                ], axis=1).astype(BF)

            total = (chip_part(0), to_x(chip_part(1)), to_y(chip_part(2)), to_diag(chip_part(3)))
            acc = chip_sum((own_0, sib_0), hop)
            acc, *total = tie((acc, *total))
            home = swap_all(acc.reshape(8, dr, UNIT))
            blocks = run_fold(total)
        else:
            rs_qkv = lax.psum_scatter(dw[0], "fsdp", scatter_dimension=0, tiled=True)

        if rest > 1:
            acc = lax.psum_scatter(
                chip_sum((own_0, sib_0), hop), "fsdp", scatter_dimension=0, tiled=True,
                axis_index_groups=rest_groups,
            )
            home = swap_all(acc.reshape(8, dr, UNIT))
        gate_up_grad, down_grad = call(
            settle(dr), [((dr, 4, 2 * FF), F32), ((dr, 4, FF), F32)], [HB], [VM] * 2,
            [pltpu.VMEM((8, dr, UNIT), BF), pltpu.SemaphoreType.DMA((1,))], (home,), "settle", 48, 0,
        )

        near = [
            lax.dynamic_index_in_dim(outs, chip ^ t, 0, keepdims=False).astype(F32) for t in (1, 2, 3)
        ]
        output = (h1 + oown + near[0] + near[1] + near[2]).astype(BF)
        if rest > 1:
            blocks = [
                jnp.concatenate(
                    [rs_qkv[:, k * 512 : (k + 1) * 512], rs_out[:, k * 256 : (k + 1) * 256],
                     rs_qkv[:, 2048:], rs_out[:, 1024:]], axis=1
                )
                for k in range(groups)
            ]
        z_qkv = z_sum(blocks)
        z_out = z_qkv[:, 512:]
        return (
            output,
            dx,
            z_out[:, 256],
            jnp.concatenate(swapped(z_qkv[:, :256]), axis=1),
            z_qkv[:, 256:384],
            z_qkv[:, 384:512],
            jnp.concatenate(swapped(z_out[:, :256]), axis=1),
            z_out[:, 384 + EXPERTS],
            z_out[:, 384 : 384 + EXPERTS],
            gate_up_grad,
            down_grad,
        )

    return shards


def solution(mesh):
    both = ("grp", "fsdp")
    in_specs = (
        P(both, None), P(both), P(both), P(both, None), P(both, None),
        P("fsdp"), P("fsdp", "grp"), P("fsdp", "grp"), P("fsdp", "grp"), P("fsdp", "grp"),
        P("fsdp"), P("fsdp", None), P("fsdp", "grp", None), P("fsdp", "grp", None), P(both, None),
    )
    out_specs = (
        P(both, None), P(both, None), P("fsdp"),
        P("fsdp", "grp"), P("fsdp", "grp"), P("fsdp", "grp"), P("fsdp", "grp"),
        P("fsdp"), P("fsdp", None), P("fsdp", "grp", None), P("fsdp", "grp", None),
    )
    shards = make_shards(mesh.shape["grp"], mesh.shape["fsdp"])
    return jax.shard_map(shards, mesh=mesh, in_specs=in_specs, out_specs=out_specs, check_vma=False)
```

```python
import functools
import math

import jax
import jax.numpy as jnp
from jax import lax
from jax.experimental import pallas as pl
from jax.experimental.pallas import tpu as pltpu
from jax.sharding import PartitionSpec as P

MODEL_WIDTH = 1024
HEAD_SIZE = 64
FF = 512
HALF = FF // 2
EXPERTS = 16
T = 384
LANES = 128
EPSILON = 1e-06
ROPE_BASE = 10000.0
NEG_FILL = -1e30
SCALE = 1.0 / math.sqrt(HEAD_SIZE)
BF = jnp.bfloat16
F32 = jnp.float32
COST = 1.0
VMEM_MIB = 62

NT = (((1,), (1,)), ((), ()))
TN = (((0,), (0,)), ((), ()))

VM = pl.BlockSpec(memory_space=pltpu.VMEM)
SM = pl.BlockSpec(memory_space=pltpu.SMEM)
HB = pl.BlockSpec(memory_space=pltpu.HBM)


def dot(a, b):
    return jnp.dot(a, b, preferred_element_type=F32)


def dotg(a, b, dims, **kw):
    return lax.dot_general(a, b, dims, preferred_element_type=F32, **kw)


def call(body, outs, in_specs, out_specs, scratch, args, name, vmem=48, flops=0):
    nbytes = sum(math.prod(a.shape) * a.dtype.itemsize for a in args)
    nbytes += sum(math.prod(s) * jnp.dtype(d).itemsize for s, d in outs)
    return pl.pallas_call(
        body,
        out_shape=[jax.ShapeDtypeStruct(s, d) for s, d in outs],
        in_specs=in_specs,
        out_specs=out_specs,
        scratch_shapes=scratch,
        compiler_params=pltpu.CompilerParams(vmem_limit_bytes=VMEM_MIB << 20),
        cost_estimate=pl.CostEstimate(
            flops=int(flops * COST), transcendentals=0, bytes_accessed=int(nbytes * COST)
        ),
        name=name,
    )(*args)


def after(x, *deps):
    return lax.optimization_barrier((x, *deps))[0]


def low_half(shape):
    return lax.broadcasted_iota(jnp.int32, shape, 1) < HEAD_SIZE


def turn(part, cos, sin, first):
    partner = jnp.where(first, pltpu.roll(part, 96, 1), pltpu.roll(part, 32, 1))
    return part * cos + partner * sin


def first_of_head(shape):
    return (lax.broadcasted_iota(jnp.int32, shape, 1) % HEAD_SIZE) < HEAD_SIZE // 2


def attn_rows(qkv_ref, bias_ref, b, c, low):
    rows = slice(c * LANES, (c + 1) * LANES)
    seen = (c + 1) * LANES
    qa = qkv_ref[b, rows, 0:LANES]
    qb = qkv_ref[b, rows, LANES : 2 * LANES]
    zero = jnp.zeros_like(qa)
    q = jnp.concatenate(
        [jnp.where(low, qa, zero), jnp.where(low, qb, zero), jnp.where(low, zero, qa), jnp.where(low, zero, qb)], axis=0
    )
    keys = qkv_ref[b, :seen, 256:384]
    bias = bias_ref[rows, :seen]
    s = dotg(q, keys, NT) * SCALE + jnp.concatenate([bias] * 4, axis=0)
    p = jnp.exp(s - jnp.max(s, axis=1, keepdims=True))
    p = p * (1.0 / jnp.sum(p, axis=1, keepdims=True))
    return rows, seen, q, keys, p


def fetch(pairs, sems, first=0):
    copies = [pltpu.make_async_copy(a, b, sems.at[first + i]) for i, (a, b) in enumerate(pairs)]
    for c in copies:
        c.start()
    return copies


def wait(copies):
    for c in copies:
        c.wait()


def attn_fwd(places, dr):
    n = len(places)

    def body(mine_ref, *refs):
        pieces = refs[:n]
        x_h, cos_h, sin_h, bias_h, wo_h = refs[n : n + 5]
        w_h, n1_h, qkv_h, att_h, h1_h, n2_h, rows_h = refs[n + 5 : n + 12]
        x, cos, sin, bias, wo, w, n1, qkv, att, h1, n2, small, si, so = refs[n + 12 :]
        mine = mine_ref[0]
        pairs = [(x_h, x), (cos_h, cos), (sin_h, sin)]
        for p, (bits, off, rows) in zip(pieces, places):
            at = 0 if bits is None else pl.multiple_of((mine ^ bits) * dr + off, math.gcd(dr, off))
            pairs.append((p, w.at[pl.ds(at, rows)]))
        pairs += [(bias_h, bias), (wo_h, wo)]
        copies = fetch(pairs, si)
        wait(copies[:-1])
        outs = fetch([(w.at[:, 0:2048], w_h)], so)
        small[...] = w[:, 2048:2176].astype(F32).T
        outs += fetch([(small, rows_h)], so, 7)
        attn_fwd_body(x, small.at[16:17], w, cos, sin, bias, n1, qkv, att)
        outs += fetch([(n1, n1_h), (qkv, qkv_h), (att, att_h)], so, 1)
        copies[-1].wait()
        mid(x, att, wo, small.at[17:18], h1, n2)
        outs += fetch([(n2, n2_h), (h1, h1_h)], so, 4)
        wait(outs)

    return body


def attn_fwd_body(x_ref, gain_ref, w_ref, cos_ref, sin_ref, bias_ref, n1_ref, qkv_ref, att_ref):
    x = x_ref[...].astype(F32)
    r1 = lax.rsqrt(jnp.mean(x * x, axis=1, keepdims=True) + EPSILON)
    n1 = (x * r1 * gain_ref[...]).astype(BF)
    n1_ref[...] = n1
    cos = cos_ref[...]
    sin = sin_ref[...]
    first = first_of_head((T, LANES))
    low = low_half((LANES, LANES))
    for b in range(4):
        raw = dot(n1, w_ref[:, b * 512 : (b + 1) * 512])
        for s in range(4):
            part = raw[:, s * LANES : (s + 1) * LANES]
            if s < 3:
                part = turn(part, cos, sin, first)
            qkv_ref[b, :, s * LANES : (s + 1) * LANES] = part.astype(BF)

    def block(b, carry):
        for c in range(3):
            rows, seen, q, keys, p = attn_rows(qkv_ref, bias_ref, b, c, low)
            o = dot(p.astype(BF), qkv_ref[b, :seen, 384:512])
            att_ref[b, rows, 0:LANES] = jnp.where(low, o[0:LANES], o[2 * LANES : 3 * LANES]).astype(BF)
            att_ref[b, rows, LANES : 2 * LANES] = jnp.where(low, o[LANES : 2 * LANES], o[3 * LANES :]).astype(BF)
        return carry

    for b in range(4):
        block(b, 0)


def soft_gates(n2, rt, mask):
    logits = dotg(n2, rt, NT)
    top = jnp.max(jnp.where(mask > 0, logits, NEG_FILL), axis=1, keepdims=True)
    e = jnp.where(mask > 0, jnp.exp(jnp.minimum(logits - top, 0.0)), 0.0)
    return e / jnp.sum(e, axis=1, keepdims=True)


def route_mask(routes):
    ids = lax.broadcasted_iota(jnp.int32, (LANES, T), 0).astype(F32)
    hit = jnp.zeros((LANES, T), F32)
    for i in range(8):
        hit = hit + jnp.where(ids == routes[i : i + 1, :], 1.0, 0.0)
    return hit.T


def mid(x_ref, att_ref, wo_ref, gain_ref, h1_ref, n2_ref):
    att = jnp.concatenate([att_ref[b] for b in range(4)], axis=1)
    h1 = x_ref[...].astype(F32) + dotg(att, wo_ref[...], NT)
    h1_ref[...] = h1
    r2 = lax.rsqrt(jnp.mean(h1 * h1, axis=1, keepdims=True) + EPSILON)
    n2_ref[...] = (h1 * r2 * gain_ref[...]).astype(BF)


ROWS = 4 * T
WIDE = 2 * HALF
UNIT = 3 * HALF
TREE = [slice(t * T, (t + 1) * T) for t in range(4)]


def token_pairs(srcs, dst):
    pairs, at = [], 0
    for r in srcs:
        pairs.append((r, dst.at[at : at + r.shape[0]]))
        at += r.shape[0]
    return pairs


def chip_pairs(src, chip, dst):
    return [
        (src.at[pl.ds(pl.multiple_of((chip ^ t) * T, T), T)], dst.at[t * T : (t + 1) * T]) for t in range(4)
    ]


def act(t, e, X, Y, W, GT, GH, DGU):
    rows = TREE[t]
    lanes = lax.broadcasted_iota(jnp.int32, (T, LANES), 1)
    gate = jnp.sum(jnp.where(lanes == e, GT[rows, :], 0.0), axis=1, keepdims=True)
    dgate = jnp.zeros((T, 1), F32)
    for u in range(2):
        gu = dot(X[rows, :], W[u, :, 0:WIDE])
        dh = dot(Y[rows, :], W[u, :, WIDE:UNIT])
        g = gu[:, :HALF]
        up = gu[:, HALF:]
        s = 0.5 * jnp.tanh(0.5 * g) + 0.5
        silu = g * s
        hid = silu * up
        GH[rows, u * HALF : (u + 1) * HALF] = (gate * hid).astype(BF)
        dgate = dgate + jnp.sum(dh * hid, axis=1, keepdims=True)
        dh = dh * gate
        base = u * WIDE
        DGU[rows, base : base + HALF] = (dh * up * (s + silu * (1.0 - s))).astype(BF)
        DGU[rows, base + HALF : base + WIDE] = (dh * silu).astype(BF)
    return jnp.where(lanes == e, dgate, 0.0)


def wgrad_down(Y, GH, DW):
    step = 256
    for r in range(MODEL_WIDTH // step):
        cols = slice(r * step, (r + 1) * step)
        dd = dotg(Y[:, cols], GH[...], TN)
        for u in range(2):
            DW[u, cols, WIDE:UNIT] = dd[:, u * HALF : (u + 1) * HALF].astype(BF)


def wgrad_up(X, DGU, DW):
    step = 256
    for r in range(MODEL_WIDTH // step):
        cols = slice(r * step, (r + 1) * step)
        dg = dotg(X[:, cols], DGU[...], TN)
        for u in range(2):
            DW[u, cols, 0:WIDE] = dg[:, u * WIDE : (u + 1) * WIDE].astype(BF)


def wgrad(X, Y, GH, DGU, DW):
    wgrad_down(Y, GH, DW)
    wgrad_up(X, DGU, DW)


def stage_scratch(n, extra, loads, stores):
    return [
        pltpu.VMEM((ROWS, MODEL_WIDTH), BF), pltpu.VMEM((ROWS, MODEL_WIDTH), BF),
        pltpu.VMEM((n, 2, MODEL_WIDTH, UNIT), BF),
        pltpu.VMEM((n, ROWS, FF), BF), pltpu.VMEM((n, ROWS, 2 * FF), BF),
        pltpu.VMEM((ROWS, LANES), F32), pltpu.VMEM((ROWS, LANES), F32),
        *extra,
        pltpu.SemaphoreType.DMA((loads,)), pltpu.SemaphoreType.DMA((stores,)),
    ]


def load_tokens(xs, dyg, chip, X, Y, head, rest, si):
    px, py = token_pairs(xs, X), chip_pairs(dyg, chip, Y)
    urgent = fetch(px[0:1] + head + py[0:1], si)
    wait(urgent)
    n = len(urgent)
    more = fetch([px[1], py[1], px[2], py[2], px[3], px[4], py[3]] + rest, si, n)
    return [[], more[0:2], more[2:4], more[4:7]], more[7:]


def stage_a(e_ref, *refs):
    xs, dyg, ws = refs[0:5], refs[5], refs[6:8]
    rt_h, routes = refs[8], refs[9:13]
    gh_h, dgu_h, dwo_h, dws_h, gates_h, dgate_h = refs[13:19]
    X, Y, W, GH, DGU, GT, DG, DW, rt, si, so = refs[19:]
    trees, _ = load_tokens(
        xs, dyg, e_ref[4], X, Y, [(rt_h, rt)] + [(ws[i], W.at[0, i]) for i in range(2)], [], si
    )
    router = rt[...].astype(BF)
    for t in range(4):
        wait(trees[t])
        GT[TREE[t], :] = soft_gates(X[TREE[t], :], router, route_mask(routes[t][...].astype(F32)))
        DG[TREE[t], :] = act(t, e_ref[1], X, Y, W.at[0], GT, GH.at[0], DGU.at[0])
    outs = fetch([(GH.at[0], gh_h), (DGU.at[0], dgu_h), (GT, gates_h), (DG, dgate_h)], so)
    wgrad(X, Y, GH.at[0], DGU.at[0], DW)
    outs += fetch([(DW.at[0], dwo_h), (DW.at[1], dws_h)], so, 4)
    wait(outs)


ACT_OUT = [((ROWS, FF), BF), ((ROWS, 2 * FF), BF)]
GATE_OUT = [((ROWS, LANES), F32)]
DW_OUT = [((MODEL_WIDTH, UNIT), BF)] * 2
DW_VMEM = pltpu.VMEM((2, MODEL_WIDTH, UNIT), BF)
EXPERT_FLOPS = 2 * ROWS * MODEL_WIDTH * 3 * FF


def run_stage_a(e, xs, dyg, pair, rt, routes):
    extra = [DW_VMEM, pltpu.VMEM((LANES, MODEL_WIDTH), F32)]
    return call(
        stage_a, ACT_OUT + DW_OUT + GATE_OUT * 2, [SM] + [HB] * 9 + [VM] * 4, [HB] * 6,
        stage_scratch(1, extra, 12, 6), (e, *xs, dyg, *pair, rt, *routes), "stage_a", 48, 2 * EXPERT_FLOPS,
    )


def stage_b(e_ref, *refs):
    xs, dyg, ws = refs[0:5], refs[5], refs[6:10]
    gates_h, dgate_i = refs[10:12]
    gh0_h, dgu0_h, gh2_h, dgu2_h, dgate_h = refs[12:17]
    X, Y, W, GH, DGU, GT, DG, si, so = refs[17:]
    hw = [(ws[i], W.at[i // 2, i % 2]) for i in range(4)]
    trees, second = load_tokens(
        xs, dyg, e_ref[4], X, Y, hw[0:2] + [(gates_h, GT), (dgate_i, DG)], hw[2:], si
    )
    for t in range(4):
        wait(trees[t])
        DG[TREE[t], :] += act(t, e_ref[0], X, Y, W.at[0], GT, GH.at[0], DGU.at[0])
    outs = fetch([(GH.at[0], gh0_h), (DGU.at[0], dgu0_h)], so)
    wait(second)
    for t in range(4):
        DG[TREE[t], :] += act(t, e_ref[2], X, Y, W.at[1], GT, GH.at[1], DGU.at[1])
    outs += fetch([(GH.at[1], gh2_h), (DGU.at[1], dgu2_h), (DG, dgate_h)], so, 2)
    wait(outs)


def run_stage_b(e, xs, dyg, ws, gates, dgate):
    return call(
        stage_b, ACT_OUT * 2 + GATE_OUT, [SM] + [HB] * 12, [HB] * 5,
        stage_scratch(2, [], 15, 5), (e, *xs, dyg, *ws, gates, dgate), "stage_b", 48, 2 * EXPERT_FLOPS,
    )


def stage_c(e_ref, *refs):
    xs, dyg, ws = refs[0:5], refs[5], refs[6:14]
    gates_h, dgate_i = refs[14:16]
    dgus = refs[16:19]
    gh_h, dgu_h, dgate_h, parts_h = refs[19:23]
    X, Y, W, GH, DGU, GT, DG, WB, DF, OUT, si, so = refs[23:]
    late = [(ws[i].at[:, 0:WIDE], WB.at[:, i * WIDE : (i + 1) * WIDE]) for i in range(6)]
    late += [(dgus[i].at[T:ROWS], DF.at[:, 2 * i * FF : 2 * (i + 1) * FF]) for i in range(3)]
    trees, late = load_tokens(
        xs, dyg, e_ref[4], X, Y,
        [(ws[6 + i], W.at[0, i]) for i in range(2)] + [(gates_h, GT), (dgate_i, DG)], late, si,
    )
    for t in range(4):
        wait(trees[t])
        DG[TREE[t], :] += act(t, e_ref[3], X, Y, W.at[0], GT, GH.at[0], DGU.at[0])
    outs = fetch([(GH.at[0], gh_h), (DGU.at[0], dgu_h), (DG, dgate_h)], so)
    wait(late)
    w = jnp.concatenate([WB[...]] + [W[0, i, :, 0:WIDE] for i in range(2)], axis=1)
    for i, t in enumerate((3, 1, 2)):
        a = jnp.concatenate([DF[TREE[t - 1], :], DGU[0, TREE[t], :]], axis=1)
        OUT[i, :, 0:MODEL_WIDTH] = dotg(a, w, NT).astype(BF)
        OUT[i, :, MODEL_WIDTH:] = DG[TREE[t], :].astype(BF)
        outs += fetch([(OUT.at[i], parts_h.at[e_ref[4] ^ t])], so, 3 + i)
    wait(outs)


def run_stage_c(e, xs, dyg, ws, gates, dgate, dgus):
    cols = MODEL_WIDTH + LANES
    extra = [
        pltpu.VMEM((MODEL_WIDTH, 6 * WIDE), BF), pltpu.VMEM((3 * T, 6 * FF), BF), pltpu.VMEM((3, T, cols), BF),
    ]
    return call(
        stage_c, ACT_OUT + GATE_OUT + [((4, T, cols), BF)], [SM] + [HB] * 19, [HB] * 4,
        stage_scratch(1, extra, 22, 6), (e, *xs, dyg, *ws, gates, dgate, *dgus), "stage_c", 48, 2 * EXPERT_FLOPS,
    )


def back_pairs(acts, ws, lo, m, width, first_col, A, W):
    pairs = []
    for k in range(4):
        pairs.append((acts[k].at[lo : lo + m], A.at[:, k * 2 * width : (k + 1) * 2 * width]))
        for u in range(2):
            at = (2 * k + u) * width
            pairs.append((ws[2 * k + u].at[:, first_col : first_col + width], W.at[:, at : at + width]))
    return pairs


def late_stage(e_ref, *refs):
    xs, dyg, gh_h, dgu_h = refs[0:5], refs[5], refs[6], refs[7]
    dgus, ws, dgate_h = refs[8:12], refs[12:20], refs[20]
    dwo_h, dws_h, own_h = refs[21:24]
    X, Y, GH, DGU, DW, A, W, DG, O, si, so = refs[24:]
    first = fetch(chip_pairs(dyg, e_ref[4], Y) + [(gh_h, GH)], si)
    wait(first)
    second = fetch(token_pairs(xs, X) + [(dgu_h, DGU)], si, 5)
    third = fetch(back_pairs(dgus, ws, 0, T, WIDE, 0, A, W) + [(dgate_h.at[0:T], DG)], si, 11)
    wgrad_down(Y, GH, DW)
    wait(second)
    wgrad_up(X, DGU, DW)
    outs = fetch([(DW.at[0], dwo_h), (DW.at[1], dws_h)], so)
    wait(third)
    O[:, 0:MODEL_WIDTH] = dotg(A[...], W[...], NT)
    O[:, MODEL_WIDTH:] = DG[...]
    outs += fetch([(O, own_h)], so, 2)
    wait(outs)


def run_late(e, xs, dyg, acts, back):
    cols = MODEL_WIDTH + LANES
    args = (e, *xs, dyg, *acts, *back)
    return call(
        late_stage, DW_OUT + [((T, cols), F32)], [SM] + [HB] * (len(args) - 1), [HB] * 3,
        [
            pltpu.VMEM((ROWS, MODEL_WIDTH), BF), pltpu.VMEM((ROWS, MODEL_WIDTH), BF),
            pltpu.VMEM((ROWS, FF), BF), pltpu.VMEM((ROWS, 2 * FF), BF), DW_VMEM,
            pltpu.VMEM((T, 8 * WIDE), BF), pltpu.VMEM((MODEL_WIDTH, 8 * WIDE), BF),
            pltpu.VMEM((T, LANES), F32), pltpu.VMEM((T, cols), F32),
            pltpu.SemaphoreType.DMA((24,)), pltpu.SemaphoreType.DMA((3,)),
        ],
        args, "late_stage", 52, 2 * EXPERT_FLOPS,
    )


def grads_stage(e_ref, *refs):
    xs, dyg, acts = refs[0:5], refs[5], refs[6:10]
    dws = refs[10:14]
    X, Y, GH, DGU, DW, si, so = refs[14:]
    first = fetch(chip_pairs(dyg, e_ref[4], Y) + [(acts[0], GH.at[0])], si)
    wait(first)
    second = fetch(token_pairs(xs, X) + [(acts[1], DGU.at[0])], si, 5)
    third = fetch([(acts[2], GH.at[1]), (acts[3], DGU.at[1])], si, 11)
    outs = []
    for i in range(2):
        wgrad_down(Y, GH.at[i], DW.at[i])
        if i == 0:
            wait(second)
        wgrad_up(X, DGU.at[i], DW.at[i])
        outs += fetch([(DW.at[i, 0], dws[2 * i]), (DW.at[i, 1], dws[2 * i + 1])], so, 2 * i)
        if i == 0:
            wait(third)
    wait(outs)


def run_grads(e, xs, dyg, acts):
    args = (e, *xs, dyg, *acts)
    return call(
        grads_stage, DW_OUT * 2, [SM] + [HB] * (len(args) - 1), [HB] * 4,
        [
            pltpu.VMEM((ROWS, MODEL_WIDTH), BF), pltpu.VMEM((ROWS, MODEL_WIDTH), BF),
            pltpu.VMEM((2, ROWS, FF), BF), pltpu.VMEM((2, ROWS, 2 * FF), BF),
            pltpu.VMEM((2, 2, MODEL_WIDTH, UNIT), BF),
            pltpu.SemaphoreType.DMA((13,)), pltpu.SemaphoreType.DMA((4,)),
        ],
        args, "grads_stage", 52, 2 * EXPERT_FLOPS,
    )


def out_stage(e_ref, *refs):
    ghs, ws = refs[0:4], refs[4:12]
    parts_h, own_h = refs[12:14]
    A, W, O, OF, si, so = refs[14:]
    order = (3, 1, 2, 0)
    pairs = [
        (ws[i].at[:, WIDE:UNIT], W.at[:, i * HALF : (i + 1) * HALF]) for i in range(8)
    ]
    for t in order:
        pairs += [(ghs[k].at[TREE[t]], A.at[TREE[t], k * FF : (k + 1) * FF]) for k in range(4)]
    copies = fetch(pairs, si)
    wait(copies[:8])
    outs = []
    for i, t in enumerate(order):
        wait(copies[8 + 4 * i : 12 + 4 * i])
        total = dotg(A[TREE[t], :], W[...], NT)
        dst = O.at[i] if t else OF
        dst[...] = total.astype(BF) if t else total
        outs += fetch([(dst, parts_h.at[e_ref[4] ^ t] if t else own_h)], so, i)
    wait(outs)


def run_out(e, ghs, ws):
    return call(
        out_stage, [((4, T, MODEL_WIDTH), BF), ((T, MODEL_WIDTH), F32)], [SM] + [HB] * 12, [HB] * 2,
        [
            pltpu.VMEM((ROWS, 8 * HALF), BF), pltpu.VMEM((MODEL_WIDTH, 8 * HALF), BF),
            pltpu.VMEM((3, T, MODEL_WIDTH), BF), pltpu.VMEM((T, MODEL_WIDTH), F32),
            pltpu.SemaphoreType.DMA((24,)), pltpu.SemaphoreType.DMA((4,)),
        ],
        (e, *ghs, *ws), "out_stage", 32, 2 * ROWS * MODEL_WIDTH * 8 * HALF,
    )


def fold(*refs):
    totals, outs, H, sem = refs[0:4], refs[4:8], refs[8], refs[9]
    wait(fetch([(t, H.at[i]) for i, t in enumerate(totals)], sem))
    for k, o in enumerate(outs):
        for at, first, width in ((0, k * 512, 512), (512, 2048 + k * 256, 256), (768, 3072, LANES)):
            cols = slice(first, first + width)
            part = H[0, :, cols].astype(F32) + H[1, :, cols].astype(F32)
            part = part + (H[2, :, cols].astype(F32) + H[3, :, cols].astype(F32))
            o[:, at : at + width] = part.astype(BF)


def run_fold(total):
    dr, cols = total[0].shape
    return call(
        fold, [((dr, 896), BF)] * 4, [HB] * 4, [VM] * 4,
        [pltpu.VMEM((4, dr, cols), BF), pltpu.SemaphoreType.DMA((4,))], total, "fold", 48, 0,
    )


def settle(dr):
    def body(home_h, gu_ref, dn_ref, H, sem):
        c = pltpu.make_async_copy(home_h, H, sem.at[0])
        c.start()
        c.wait()
        for e in range(4):
            for h in range(2):
                part = H[2 * e + h].astype(F32)
                cols = slice(h * HALF, (h + 1) * HALF)
                gu_ref[:, e, cols] = part[:, 0:HALF]
                gu_ref[:, e, FF + h * HALF : FF + (h + 1) * HALF] = part[:, HALF:WIDE]
                dn_ref[:, e, cols] = part[:, WIDE:UNIT]

    return body


def columns_of(rowwise, lane):
    total = jnp.sum(rowwise, axis=0, keepdims=True)
    total = jnp.broadcast_to(total, (LANES, MODEL_WIDTH)).T
    lanes = lax.broadcasted_iota(jnp.int32, total.shape, 1)
    return jnp.where(lanes == lane, total, 0.0)


def join(split, dr, e_ref, p_h, parts_h, gates_h, h1_h, n2_h, dy_h, wo_h, att_h, small_h,
         dh1_h, datt_h, *refs):
    n = 2 if split else 1
    dwo_h = refs[:n]
    P, R, GT, H1, N2, DY, WO, ATT, SMALL, DH1, DATT, DWO, si, so = refs[n:]
    copies = fetch(
        [(p_h, P)] + [(parts_h.at[e_ref[4] ^ t], R.at[t - 1]) for t in (1, 2, 3)]
        + [(gates_h.at[0:T], GT), (h1_h, H1), (dy_h, DY),
         (small_h, SMALL), (wo_h, WO), (att_h, ATT), (n2_h, N2)], si
    )
    wait(copies[0:8])
    gates = GT[...]
    total = P[...] + R[0].astype(F32) + R[1].astype(F32) + R[2].astype(F32)
    dg = total[:, MODEL_WIDTH:]
    dl = (gates * (dg - jnp.sum(gates * dg, axis=1, keepdims=True))).astype(BF)
    dn2 = total[:, :MODEL_WIDTH] + dot(dl, SMALL[...].astype(BF))
    h1 = H1[...]
    gain = SMALL[17:18]
    r2 = lax.rsqrt(jnp.mean(h1 * h1, axis=1, keepdims=True) + EPSILON)
    gd = gain * dn2
    inner = jnp.mean(gd * h1, axis=1, keepdims=True)
    dh1 = DY[...].astype(F32) + r2 * gd - h1 * (r2 * r2 * r2 * inner)
    DH1[...] = dh1
    db = dh1.astype(BF)
    outs = fetch([(DH1, dh1_h)], so)
    wait(copies[8:])
    for b in range(4):
        cols = slice(b * 256, (b + 1) * 256)
        DATT[b] = dot(db, WO[:, cols]).astype(BF)
        DWO[:, cols] = dotg(db, ATT[b], TN).astype(BF)
    outs += fetch([(DATT, datt_h)], so, 1)
    extra = dotg(N2[...], dl, TN) + columns_of(dn2 * h1 * r2, EXPERTS)
    DWO[:, 1024:1152] = extra.astype(BF)
    if split:
        for r in range(4):
            mine = 2 * (e_ref[4] ^ r) + e_ref[5]
            for i, at in enumerate((mine, mine ^ 1)):
                src = DWO.at[pl.ds(pl.multiple_of(at * dr, dr), dr)]
                outs += fetch([(src, dwo_h[i].at[r * dr : (r + 1) * dr])], so, 2 + 2 * r + i)
    else:
        outs += fetch([(DWO, dwo_h[0])], so, 2)
    wait(outs)


def run_join(split, dr, args):
    cols = MODEL_WIDTH + LANES
    grads = [((4 * dr, 1152), BF)] * 2 if split else [((MODEL_WIDTH, 1152), BF)]
    return call(
        functools.partial(join, split, dr),
        [((T, MODEL_WIDTH), F32), ((4, T, 256), BF)] + grads,
        [SM] + [HB] * 9, [HB] * (2 + len(grads)),
        [
            pltpu.VMEM((T, cols), F32), pltpu.VMEM((3, T, cols), BF), pltpu.VMEM((T, LANES), F32), pltpu.VMEM((T, MODEL_WIDTH), F32),
            pltpu.VMEM((T, MODEL_WIDTH), BF), pltpu.VMEM((T, MODEL_WIDTH), BF),
            pltpu.VMEM((MODEL_WIDTH, MODEL_WIDTH), BF), pltpu.VMEM((4, T, 256), BF),
            pltpu.VMEM((LANES, MODEL_WIDTH), F32),
            pltpu.VMEM((T, MODEL_WIDTH), F32), pltpu.VMEM((4, T, 256), BF), pltpu.VMEM((MODEL_WIDTH, 1152), BF),
            pltpu.SemaphoreType.DMA((12,)), pltpu.SemaphoreType.DMA((10,)),
        ],
        args, "join", 40, 2.0e9,
    )


def attn_bwd(split, dr):
    def body(mine_ref, x_h, w_h, cos_h, sin_h, bias_h, n1_h, qkv_h, datt_h, dh1_h, small_h, *refs):
        n = 5 if split else 2
        dx_h, grads_h = refs[0], refs[1:n]
        x, w, cos, sin, bias, n1, qkv, datt, dh1, gain, dx, dw, dqkv, dk, dv, si, so = refs[n : n + 17]
        copies = fetch(
            [(bias_h, bias), (qkv_h, qkv), (datt_h, datt), (cos_h, cos), (sin_h, sin), (n1_h, n1),
             (w_h, w), (x_h, x), (dh1_h, dh1), (small_h.at[16:24], gain)], si
        )
        wait(copies[0:5])
        attn_bwd_heads(cos, sin, bias, qkv, datt, dqkv, dk, dv)
        wait(copies[5:])
        attn_bwd_body(x, gain.at[0:1], w, n1, dh1, dx, dw, dqkv)
        outs = fetch([(dx, dx_h)], so)
        if split:
            for r in range(4):
                mine = mine_ref[0] ^ (2 * r)
                for i, j in enumerate((mine, mine ^ 1)):
                    src = dw.at[pl.ds(pl.multiple_of(j * dr, dr), dr)]
                    at = (r % 2) * dr
                    outs += fetch([(src, grads_h[2 * i + r // 2].at[at : at + dr])], so, 1 + 2 * r + i)
        else:
            outs += fetch([(dw, grads_h[0])], so, 1)
        wait(outs)

    return body


def run_attn_bwd(split, dr, args):
    grads = [((2 * dr, 2176), BF)] * 4 if split else [((MODEL_WIDTH, 2176), BF)]
    tile = pltpu.VMEM((T, LANES), F32)
    return call(
        attn_bwd(split, dr),
        [((T, MODEL_WIDTH), F32)] + grads,
        [SM] + [HB] * 10, [HB] * (1 + len(grads)),
        [
            pltpu.VMEM((T, MODEL_WIDTH), BF), pltpu.VMEM((MODEL_WIDTH, 2048), BF), tile, tile,
            pltpu.VMEM((T, T), F32), pltpu.VMEM((T, MODEL_WIDTH), BF), pltpu.VMEM((4, T, 512), BF),
            pltpu.VMEM((4, T, 256), BF), pltpu.VMEM((T, MODEL_WIDTH), F32), pltpu.VMEM((8, MODEL_WIDTH), F32),
            pltpu.VMEM((T, MODEL_WIDTH), F32),
            pltpu.VMEM((MODEL_WIDTH, 2176), BF), pltpu.VMEM((4, T, 512), BF), tile, tile,
            pltpu.SemaphoreType.DMA((10,)), pltpu.SemaphoreType.DMA((9,)),
        ],
        args, "attn_bwd", 40, 6.0e9,
    )


def attn_bwd_heads(cos_ref, sin_ref, bias_ref, qkv_ref, datt_ref, dqkv, dk, dv):
    low = low_half((LANES, LANES))
    first = first_of_head((T, LANES))

    def block(b, carry):
        for c in (2, 1, 0):
            rows, seen, q, keys, p = attn_rows(qkv_ref, bias_ref, b, c, low)
            da = datt_ref[b, rows, 0:LANES]
            db = datt_ref[b, rows, LANES : 2 * LANES]
            zero = jnp.zeros_like(da)
            do = jnp.concatenate(
                [jnp.where(low, da, zero), jnp.where(low, db, zero), jnp.where(low, zero, da), jnp.where(low, zero, db)],
                axis=0,
            )
            dp = dotg(do, qkv_ref[b, :seen, 384:512], NT)
            ds = (p * (dp - jnp.sum(p * dp, axis=1, keepdims=True))).astype(BF)
            dq = dot(ds, keys) * SCALE
            dkc = dotg(ds, q, TN)
            dvc = dotg(p.astype(BF), do, TN)
            if c == 2:
                dk[...] = dkc
                dv[...] = dvc
            else:
                dk[:seen] += dkc
                dv[:seen] += dvc
            cos = cos_ref[rows, :]
            sin = -sin_ref[rows, :]
            ta = jnp.where(low, dq[0:LANES], dq[2 * LANES : 3 * LANES])
            tb = jnp.where(low, dq[LANES : 2 * LANES], dq[3 * LANES :])
            dqkv[b, rows, 0:LANES] = turn(ta, cos, sin, first[rows]).astype(BF)
            dqkv[b, rows, LANES : 2 * LANES] = turn(tb, cos, sin, first[rows]).astype(BF)
        dqkv[b, :, 256:384] = turn(dk[...] * SCALE, cos_ref[...], -sin_ref[...], first).astype(BF)
        dqkv[b, :, 384:512] = dv[...].astype(BF)
        return carry

    for b in range(4):
        block(b, 0)


def attn_bwd_body(x_ref, gain_ref, w_ref, n1_ref, dh1_ref, dx_ref, dw_ref, dqkv):
    n1 = n1_ref[...]
    cat = jnp.concatenate([dqkv[b] for b in range(4)], axis=1)
    dn1 = dotg(cat, w_ref[...], NT)
    dw_ref[:, 0:2048] = dotg(n1, cat, TN).astype(BF)
    x = x_ref[...].astype(F32)
    gain = gain_ref[...]
    r1 = lax.rsqrt(jnp.mean(x * x, axis=1, keepdims=True) + EPSILON)
    gd = gain * dn1
    inner = jnp.mean(gd * x, axis=1, keepdims=True)
    dx_ref[...] = dh1_ref[...] + r1 * gd - x * (r1 * r1 * r1 * inner)
    dw_ref[:, 2048:2176] = columns_of(dn1 * x * r1, 32).astype(BF)
def visible_bias(segment, parents):
    ids = jnp.arange(parents.shape[0], dtype=jnp.int32)
    one = jnp.sum(jnp.where(segment[:, None] == ids[None, :], parents[None, :], 0), axis=1)
    two = jnp.sum(jnp.where(one[:, None] == ids[None, :], parents[None, :], 0), axis=1)
    key = segment[None, :]
    related = (key == segment[:, None]) | (key == one[:, None]) | (key == two[:, None])
    places = jnp.arange(segment.shape[0], dtype=jnp.int32)
    return jnp.where(related & (places[None, :] <= places[:, None]), 0.0, NEG_FILL).astype(F32)


def turn_tables(positions):
    half = HEAD_SIZE // 2
    lane = jnp.arange(LANES, dtype=jnp.int32)
    frequency = ROPE_BASE ** (-((lane % half).astype(F32) * 2.0) / HEAD_SIZE)
    angle = positions.astype(F32)[:, None] * frequency[None, :]
    sign = jnp.where(lane % HEAD_SIZE < half, -1.0, 1.0).astype(F32)
    return jnp.cos(angle), jnp.sin(angle) * sign[None, :]


def make_shards(groups, fsdp):
    ring = list(range(0, groups, 1))
    if groups == 4:
        ring = [0, 1, 3, 2]
    place = [ring.index(g) for g in range(groups)]
    rest = fsdp // 8

    def shifted(k):
        return [(ring[p], ring[(p + k) % groups]) for p in range(groups)]

    def flip(bits):
        return [(i, i ^ bits) for i in range(fsdp)]

    low_groups = None if rest == 1 else [[8 * r + j for j in range(8)] for r in range(rest)]
    core_groups = [[8 * r + 2 * c + k for c in range(4)] for r in range(rest) for k in range(2)]
    rest_groups = [[8 * r + j for r in range(rest)] for j in range(8)]

    def z_next(a):
        return lax.ppermute(a, "grp", shifted(1))

    def to_x(a):
        return lax.ppermute(a, "fsdp", flip(2))

    def to_y(a):
        return lax.ppermute(a, "fsdp", flip(4))

    def to_diag(a):
        return lax.ppermute(a, "fsdp", flip(6))

    def to_core(a):
        return lax.ppermute(a, "fsdp", flip(1))

    def plane(top, bot):
        xb = to_x(bot)
        yt = to_y(top)
        xt = to_x(top)
        yb = to_y(bot)
        return (top, bot, xt, xb, yt, yb, to_x(yt), to_y(xb))

    def swap(a):
        return lax.all_to_all(a, "fsdp", 0, 0, axis_index_groups=core_groups)

    def swap_all(a):
        return lax.all_to_all(a, "fsdp", 0, 0, axis_index_groups=low_groups)

    def z_sum(blocks):
        total = blocks[0].astype(F32)
        for k in range(1, groups):
            total = total + lax.ppermute(blocks[k], "grp", shifted(groups - k)).astype(F32)
        return total

    def shards(tokens, segment, positions, parents, routes, attn_gain, query_weight, key_matrix,
               value_matrix, out_weight, ffn_gain, router_weight, gate_up_weight, down_weight, cotangent):
        dr = query_weight.shape[0]
        mine = lax.axis_index("fsdp")
        spot = jnp.array(place, jnp.int32)[lax.axis_index("grp")]
        ring_ids = jnp.array(ring, jnp.int32)

        def swapped(w):
            return [w[:, 0:64], w[:, 128:192], w[:, 64:128], w[:, 192:256]]

        def z_gather(a):
            got = [a]
            for _ in range(groups - 1):
                got.append(z_next(got[-1]))
            return got

        half = T // 2
        tie = lax.optimization_barrier
        own_qkv = jnp.concatenate(swapped(query_weight) + [key_matrix, value_matrix], axis=1)
        own_out = jnp.concatenate(swapped(out_weight), axis=1)

        def z_all(a):
            return [a] + [lax.ppermute(a, "grp", shifted(k)) for k in range(1, groups)]

        route_rows = routes.T.astype(BF)
        route_rows = [route_rows, to_x(route_rows), to_y(route_rows), to_diag(route_rows)]

        gu = gate_up_weight.reshape(dr, 4, 2, 2, HALF)
        dn = down_weight.reshape(dr, 4, 1, 2, HALF)
        parts = jnp.concatenate([gu, dn], axis=2)
        parts = jnp.transpose(parts, (1, 3, 0, 2, 4)).reshape(8, dr, 3 * HALF)
        parts, own_qkv, own_out = tie((parts, own_qkv, own_out))
        blocks = z_all(jnp.concatenate([own_qkv, own_out], axis=1))
        unit = lax.all_to_all(parts, "fsdp", 0, 0, axis_index_groups=low_groups)
        unit = unit.reshape(8 * dr, 3 * HALF)
        if rest > 1:
            unit = lax.all_gather(unit, "fsdp", axis=0, tiled=True, axis_index_groups=rest_groups)

        bias = visible_bias(segment, parents[0])
        cos, sin = turn_tables(positions)
        chip = (mine // 2) % 4
        planes = ring_ids[(spot - jnp.arange(groups, dtype=jnp.int32)) % groups]
        e = jnp.concatenate([4 * planes + chip, chip[None], (mine % 2)[None]]).astype(jnp.int32)
        small = jnp.concatenate(
            [router_weight, attn_gain[:, None], ffn_gain[:, None], jnp.zeros((dr, LANES - 18), BF)], axis=1
        )
        bias, cos, sin, e, small, unit, *blocks = tie((bias, cos, sin, e, small, unit, *blocks))
        cols_qkv = jnp.concatenate([b[:, :512] for b in blocks] + [small], axis=1)
        cols_out = jnp.concatenate([b[:, 512:] for b in blocks], axis=1)
        mine_s = mine.astype(jnp.int32).reshape(1)
        units_1 = z_next(unit)
        if rest == 1:
            h = dr // 2
            qx = to_x(cols_qkv)
            qy = to_y(cols_qkv)
            qc = to_core(cols_qkv)
            qx, qy, qc = tie((qx, qy, qc))
            qa = to_x(qy[:h])
            qb = to_y(qx[h:])
            cx, cy = to_core(qx), to_core(qy)
            qa, qb, units_1 = tie((qa, qb, units_1))
            pieces = [cols_qkv, qx, qy, qa, qb, qc, cx, cy, to_core(qa), to_core(qb)]
            places = [(0, 0, dr), (2, 0, dr), (4, 0, dr), (6, 0, h), (6, h, h),
                      (1, 0, dr), (3, 0, dr), (5, 0, dr), (7, 0, h), (7, h, h)]
        else:
            pieces = [lax.all_gather(cols_qkv, "fsdp", axis=0, tiled=True)]
            places = [(None, 0, MODEL_WIDTH)]
        w_out = lax.all_gather(cols_out, "fsdp", axis=0, tiled=True)
        core_0 = to_core(after(unit, *pieces))
        dyg = lax.all_gather(after(cotangent, cols_out), "fsdp", axis=0, tiled=True, axis_index_groups=core_groups)
        tokens_f = after(tokens, *pieces)
        units_2 = z_next(units_1)
        w_qkv, n1, qkv, att, h1, n2, small = call(
            attn_fwd(places, dr),
            [((MODEL_WIDTH, 2048), BF), ((T, MODEL_WIDTH), BF), ((4, T, 512), BF), ((4, T, 256), BF),
             ((T, MODEL_WIDTH), F32), ((T, MODEL_WIDTH), BF), ((LANES, MODEL_WIDTH), F32)],
            [SM] + [HB] * (len(pieces) + 5), [HB] * 7,
            [
                pltpu.VMEM((T, MODEL_WIDTH), BF), pltpu.VMEM((T, LANES), F32), pltpu.VMEM((T, LANES), F32),
                pltpu.VMEM((T, T), F32), pltpu.VMEM((MODEL_WIDTH, MODEL_WIDTH), BF),
                pltpu.VMEM((MODEL_WIDTH, 2176), BF), pltpu.VMEM((T, MODEL_WIDTH), BF),
                pltpu.VMEM((4, T, 512), BF), pltpu.VMEM((4, T, 256), BF), pltpu.VMEM((T, MODEL_WIDTH), F32),
                pltpu.VMEM((T, MODEL_WIDTH), BF), pltpu.VMEM((LANES, MODEL_WIDTH), F32),
                pltpu.SemaphoreType.DMA((len(pieces) + 5,)), pltpu.SemaphoreType.DMA((8,)),
            ],
            (mine_s, *pieces, tokens_f, cos, sin, bias, w_out), "attn_fwd", 40, 4.0e9,
        )
        n2, core_0 = tie((n2, core_0))
        nx = to_x(n2)
        ny = to_y(n2)
        core_1 = to_core(after(units_1, n2))
        nx, ny, units_2 = tie((nx, ny, units_2))
        xs = (n2, nx, ny, to_x(ny[:half]), to_y(nx[half:]))
        core_1, *xs = tie((core_1, *xs))
        units_3 = z_next(units_2)
        core_2 = to_core(units_2)

        def chip_sum(pair, *more):
            total = pair[0].astype(F32) + pair[1].astype(F32)
            for m in more:
                total = total + m.astype(F32)
            return total.astype(BF)

        gh1, dgu1, own_1, sib_1, gates, dgate = run_stage_a(e, xs, dyg, (units_1, core_1), small, route_rows)
        core_2, gates = tie((core_2, gates))
        sib_1 = to_core(sib_1)
        gh0, dgu0, gh2, dgu2, dgate = run_stage_b(e, xs, dyg, (unit, core_0, units_2, core_2), gates, dgate)
        units_3, sib_1, dgate = tie((units_3, sib_1, dgate))
        core_3 = to_core(units_3)
        ws = (unit, core_0, units_1, core_1, units_2, core_2, units_3, core_3)
        sum_1, dgate = tie((chip_sum((own_1, sib_1)), dgate))
        hop = z_next(sum_1)
        gh3, dgu3, dgate, parts = run_stage_c(e, xs, dyg, ws, gates, dgate, (dgu0, dgu1, dgu2))
        dgate, parts = tie((dgate, parts))
        parts = swap(parts)
        dgus = (dgu0, dgu1, dgu2, dgu3)
        own_2, sib_2, own = run_late(e, xs, dyg, (gh2, dgu2), (*dgus, *ws, dgate))
        sib_2 = to_core(sib_2)
        hop, own, gh3 = tie((hop, own, gh3))
        own_3, sib_3, own_0, sib_0 = run_grads(e, xs, dyg, (gh3, dgu3, gh0, dgu0))
        sib_2, gh0, own_3 = tie((sib_2, gh0, own_3))
        sum_2, gh0 = tie((chip_sum((own_2, sib_2), hop), gh0))
        hop = z_next(sum_2)
        sib_3 = to_core(sib_3)
        sib_0 = to_core(sib_0)
        outs, oown = run_out(e, (gh0, gh1, gh2, gh3), ws)
        parts, own, outs, sib_3, sib_0 = tie((parts, own, outs, sib_3, sib_0))
        outs = swap(outs)
        dh1, datt, *dwo = run_join(
            rest == 1, dr, (e, own, parts, gates, h1, n2, cotangent, w_out, att, small)
        )
        if rest == 1:
            sib_o = to_core(dwo[1])
        else:
            rs_out = lax.psum_scatter(dwo[0], "fsdp", scatter_dimension=0, tiled=True)
        dx, *dw = run_attn_bwd(
            rest == 1, dr, (mine_s, tokens, w_qkv, cos, sin, bias, n1, qkv, datt, dh1, small)
        )
        hop, *dw = tie((hop, *dw))
        hop = z_next(chip_sum((own_3, sib_3), hop))
        if rest == 1:
            sib_a, sib_b, sib_o, outs = tie((to_core(dw[2]), to_core(dw[3]), sib_o, outs))
            def chip_part(r):
                pair = (dw[r // 2], sib_a if r < 2 else sib_b)
                here = slice((r % 2) * dr, (r % 2 + 1) * dr)
                there = slice(r * dr, (r + 1) * dr)
                mine_q = pair[0][here].astype(F32) + pair[1][here].astype(F32)
                mine_o = dwo[0][there].astype(F32) + sib_o[there].astype(F32)
                return jnp.concatenate(
                    [mine_q[:, :2048], mine_o[:, :1024], mine_q[:, 2048:] + mine_o[:, 1024:]], axis=1
                ).astype(BF)

            total = (chip_part(0), to_x(chip_part(1)), to_y(chip_part(2)), to_diag(chip_part(3)))
            acc = chip_sum((own_0, sib_0), hop)
            acc, *total = tie((acc, *total))
            home = swap_all(acc.reshape(8, dr, UNIT))
            blocks = run_fold(total)
        else:
            rs_qkv = lax.psum_scatter(dw[0], "fsdp", scatter_dimension=0, tiled=True)

        if rest > 1:
            acc = lax.psum_scatter(
                chip_sum((own_0, sib_0), hop), "fsdp", scatter_dimension=0, tiled=True,
                axis_index_groups=rest_groups,
            )
            home = swap_all(acc.reshape(8, dr, UNIT))
        gate_up_grad, down_grad = call(
            settle(dr), [((dr, 4, 2 * FF), F32), ((dr, 4, FF), F32)], [HB], [VM] * 2,
            [pltpu.VMEM((8, dr, UNIT), BF), pltpu.SemaphoreType.DMA((1,))], (home,), "settle", 48, 0,
        )

        near = [
            lax.dynamic_index_in_dim(outs, chip ^ t, 0, keepdims=False).astype(F32) for t in (1, 2, 3)
        ]
        output = (h1 + oown + near[0] + near[1] + near[2]).astype(BF)
        if rest > 1:
            blocks = [
                jnp.concatenate(
                    [rs_qkv[:, k * 512 : (k + 1) * 512], rs_out[:, k * 256 : (k + 1) * 256],
                     rs_qkv[:, 2048:] + rs_out[:, 1024:]], axis=1
                )
                for k in range(groups)
            ]
        z_qkv = z_sum(blocks)
        z_out = z_qkv[:, 512:]
        return (
            output,
            dx,
            z_out[:, 256 + 32],
            jnp.concatenate(swapped(z_qkv[:, :256]), axis=1),
            z_qkv[:, 256:384],
            z_qkv[:, 384:512],
            jnp.concatenate(swapped(z_out[:, :256]), axis=1),
            z_out[:, 256 + EXPERTS],
            z_out[:, 256 : 256 + EXPERTS],
            gate_up_grad,
            down_grad,
        )

    return shards


def solution(mesh):
    both = ("grp", "fsdp")
    in_specs = (
        P(both, None), P(both), P(both), P(both, None), P(both, None),
        P("fsdp"), P("fsdp", "grp"), P("fsdp", "grp"), P("fsdp", "grp"), P("fsdp", "grp"),
        P("fsdp"), P("fsdp", None), P("fsdp", "grp", None), P("fsdp", "grp", None), P(both, None),
    )
    out_specs = (
        P(both, None), P(both, None), P("fsdp"),
        P("fsdp", "grp"), P("fsdp", "grp"), P("fsdp", "grp"), P("fsdp", "grp"),
        P("fsdp"), P("fsdp", None), P("fsdp", "grp", None), P("fsdp", "grp", None),
    )
    shards = make_shards(mesh.shape["grp"], mesh.shape["fsdp"])
    return jax.shard_map(shards, mesh=mesh, in_specs=in_specs, out_specs=out_specs, check_vma=False)
```

```python
import functools
import math

import jax
import jax.numpy as jnp
from jax import lax
from jax.experimental import pallas as pl
from jax.experimental.pallas import tpu as pltpu
from jax.sharding import PartitionSpec as P

MODEL_WIDTH = 1024
HEAD_SIZE = 64
FF = 512
HALF = FF // 2
EXPERTS = 16
T = 384
LANES = 128
EPSILON = 1e-06
ROPE_BASE = 10000.0
NEG_FILL = -1e30
SCALE = 1.0 / math.sqrt(HEAD_SIZE)
BF = jnp.bfloat16
F32 = jnp.float32
COST = 1.0
VMEM_MIB = 62

NT = (((1,), (1,)), ((), ()))
TN = (((0,), (0,)), ((), ()))

VM = pl.BlockSpec(memory_space=pltpu.VMEM)
SM = pl.BlockSpec(memory_space=pltpu.SMEM)
HB = pl.BlockSpec(memory_space=pltpu.HBM)


def dot(a, b):
    return jnp.dot(a, b, preferred_element_type=F32)


def dotg(a, b, dims, **kw):
    return lax.dot_general(a, b, dims, preferred_element_type=F32, **kw)


def call(body, outs, in_specs, out_specs, scratch, args, name, vmem=48, flops=0):
    nbytes = sum(math.prod(a.shape) * a.dtype.itemsize for a in args)
    nbytes += sum(math.prod(s) * jnp.dtype(d).itemsize for s, d in outs)
    return pl.pallas_call(
        body,
        out_shape=[jax.ShapeDtypeStruct(s, d) for s, d in outs],
        in_specs=in_specs,
        out_specs=out_specs,
        scratch_shapes=scratch,
        compiler_params=pltpu.CompilerParams(vmem_limit_bytes=VMEM_MIB << 20),
        cost_estimate=pl.CostEstimate(
            flops=int(flops * COST), transcendentals=0, bytes_accessed=int(nbytes * COST)
        ),
        name=name,
    )(*args)


def after(x, *deps):
    return lax.optimization_barrier((x, *deps))[0]


def low_half(shape):
    return lax.broadcasted_iota(jnp.int32, shape, 1) < HEAD_SIZE


def turn(part, cos, sin, first):
    partner = jnp.where(first, pltpu.roll(part, 96, 1), pltpu.roll(part, 32, 1))
    return part * cos + partner * sin


def first_of_head(shape):
    return (lax.broadcasted_iota(jnp.int32, shape, 1) % HEAD_SIZE) < HEAD_SIZE // 2


def attn_rows(qkv_ref, bias_ref, b, c, low):
    rows = slice(c * LANES, (c + 1) * LANES)
    seen = (c + 1) * LANES
    qa = qkv_ref[b, rows, 0:LANES]
    qb = qkv_ref[b, rows, LANES : 2 * LANES]
    zero = jnp.zeros_like(qa)
    q = jnp.concatenate(
        [jnp.where(low, qa, zero), jnp.where(low, qb, zero), jnp.where(low, zero, qa), jnp.where(low, zero, qb)], axis=0
    )
    keys = qkv_ref[b, :seen, 256:384]
    bias = bias_ref[rows, :seen]
    s = dotg(q, keys, NT) * SCALE + jnp.concatenate([bias] * 4, axis=0)
    p = jnp.exp(s - jnp.max(s, axis=1, keepdims=True))
    p = p * (1.0 / jnp.sum(p, axis=1, keepdims=True))
    return rows, seen, q, keys, p


def fetch(pairs, sems, first=0):
    copies = [pltpu.make_async_copy(a, b, sems.at[first + i]) for i, (a, b) in enumerate(pairs)]
    for c in copies:
        c.start()
    return copies


def wait(copies):
    for c in copies:
        c.wait()


def attn_fwd(places, dr):
    n = len(places)

    def body(mine_ref, *refs):
        pieces = refs[:n]
        x_h, cos_h, sin_h, bias_h, wo_h = refs[n : n + 5]
        w_h, n1_h, qkv_h, att_h, h1_h, n2_h, rows_h = refs[n + 5 : n + 12]
        x, cos, sin, bias, wo, w, n1, qkv, att, h1, n2, small, si, so = refs[n + 12 :]
        mine = mine_ref[0]
        pairs = [(x_h, x), (cos_h, cos), (sin_h, sin)]
        for p, (bits, off, rows) in zip(pieces, places):
            at = 0 if bits is None else pl.multiple_of((mine ^ bits) * dr + off, math.gcd(dr, off))
            pairs.append((p, w.at[pl.ds(at, rows)]))
        pairs += [(bias_h, bias), (wo_h, wo)]
        copies = fetch(pairs, si)
        wait(copies[:-1])
        outs = fetch([(w.at[:, 0:2048], w_h)], so)
        small[...] = w[:, 2048:2176].astype(F32).T
        outs += fetch([(small, rows_h)], so, 7)
        attn_fwd_body(x, small.at[16:17], w, cos, sin, bias, n1, qkv, att)
        outs += fetch([(n1, n1_h), (qkv, qkv_h), (att, att_h)], so, 1)
        copies[-1].wait()
        mid(x, att, wo, small.at[17:18], h1, n2)
        outs += fetch([(n2, n2_h), (h1, h1_h)], so, 4)
        wait(outs)

    return body


def attn_fwd_body(x_ref, gain_ref, w_ref, cos_ref, sin_ref, bias_ref, n1_ref, qkv_ref, att_ref):
    x = x_ref[...].astype(F32)
    r1 = lax.rsqrt(jnp.mean(x * x, axis=1, keepdims=True) + EPSILON)
    n1 = (x * r1 * gain_ref[...]).astype(BF)
    n1_ref[...] = n1
    cos = cos_ref[...]
    sin = sin_ref[...]
    first = first_of_head((T, LANES))
    low = low_half((LANES, LANES))
    for b in range(4):
        raw = dot(n1, w_ref[:, b * 512 : (b + 1) * 512])
        for s in range(4):
            part = raw[:, s * LANES : (s + 1) * LANES]
            if s < 3:
                part = turn(part, cos, sin, first)
            qkv_ref[b, :, s * LANES : (s + 1) * LANES] = part.astype(BF)

    def block(b, carry):
        for c in range(3):
            rows, seen, q, keys, p = attn_rows(qkv_ref, bias_ref, b, c, low)
            o = dot(p.astype(BF), qkv_ref[b, :seen, 384:512])
            att_ref[b, rows, 0:LANES] = jnp.where(low, o[0:LANES], o[2 * LANES : 3 * LANES]).astype(BF)
            att_ref[b, rows, LANES : 2 * LANES] = jnp.where(low, o[LANES : 2 * LANES], o[3 * LANES :]).astype(BF)
        return carry

    for b in range(4):
        block(b, 0)


def soft_gates(n2, rt, mask):
    logits = dotg(n2, rt, NT)
    top = jnp.max(jnp.where(mask > 0, logits, NEG_FILL), axis=1, keepdims=True)
    e = jnp.where(mask > 0, jnp.exp(jnp.minimum(logits - top, 0.0)), 0.0)
    return e / jnp.sum(e, axis=1, keepdims=True)


def route_mask(routes):
    ids = lax.broadcasted_iota(jnp.int32, (LANES, T), 0).astype(F32)
    hit = jnp.zeros((LANES, T), F32)
    for i in range(8):
        hit = hit + jnp.where(ids == routes[i : i + 1, :], 1.0, 0.0)
    return hit.T


def mid(x_ref, att_ref, wo_ref, gain_ref, h1_ref, n2_ref):
    att = jnp.concatenate([att_ref[b] for b in range(4)], axis=1)
    h1 = x_ref[...].astype(F32) + dotg(att, wo_ref[...], NT)
    h1_ref[...] = h1
    r2 = lax.rsqrt(jnp.mean(h1 * h1, axis=1, keepdims=True) + EPSILON)
    n2_ref[...] = (h1 * r2 * gain_ref[...]).astype(BF)


ROWS = 4 * T
WIDE = 2 * HALF
UNIT = 3 * HALF
TREE = [slice(t * T, (t + 1) * T) for t in range(4)]


def token_pairs(srcs, dst):
    pairs, at = [], 0
    for r in srcs:
        pairs.append((r, dst.at[at : at + r.shape[0]]))
        at += r.shape[0]
    return pairs


def chip_pairs(src, chip, dst):
    return [
        (src.at[pl.ds(pl.multiple_of((chip ^ t) * T, T), T)], dst.at[t * T : (t + 1) * T]) for t in range(4)
    ]


def act(rows, e, X, Y, W, GT, GH, DGU):
    lanes = lax.broadcasted_iota(jnp.int32, (T, LANES), 1)
    gate = jnp.sum(jnp.where(lanes == e, GT[rows, :], 0.0), axis=1, keepdims=True)
    dgate = jnp.zeros((T, 1), F32)
    for u in range(2):
        gu = dot(X[rows, :], W[u, :, 0:WIDE])
        dh = dot(Y[rows, :], W[u, :, WIDE:UNIT])
        g = gu[:, :HALF]
        up = gu[:, HALF:]
        s = 0.5 * jnp.tanh(0.5 * g) + 0.5
        silu = g * s
        hid = silu * up
        GH[rows, u * HALF : (u + 1) * HALF] = (gate * hid).astype(BF)
        dgate = dgate + jnp.sum(dh * hid, axis=1, keepdims=True)
        dh = dh * gate
        base = u * WIDE
        DGU[rows, base : base + HALF] = (dh * up * (s + silu * (1.0 - s))).astype(BF)
        DGU[rows, base + HALF : base + WIDE] = (dh * silu).astype(BF)
    return jnp.where(lanes == e, dgate, 0.0)


def wgrad_down(Y, GH, DW):
    step = 256
    for r in range(MODEL_WIDTH // step):
        cols = slice(r * step, (r + 1) * step)
        dd = dotg(Y[:, cols], GH[...], TN)
        for u in range(2):
            DW[u, cols, WIDE:UNIT] = dd[:, u * HALF : (u + 1) * HALF].astype(BF)


def wgrad_up(X, DGU, DW):
    step = 256
    for r in range(MODEL_WIDTH // step):
        cols = slice(r * step, (r + 1) * step)
        dg = dotg(X[:, cols], DGU[...], TN)
        for u in range(2):
            DW[u, cols, 0:WIDE] = dg[:, u * WIDE : (u + 1) * WIDE].astype(BF)


def wgrad(X, Y, GH, DGU, DW):
    wgrad_down(Y, GH, DW)
    wgrad_up(X, DGU, DW)


def stage_scratch(n, extra, loads, stores):
    return [
        pltpu.VMEM((ROWS, MODEL_WIDTH), BF), pltpu.VMEM((ROWS, MODEL_WIDTH), BF),
        pltpu.VMEM((n, 2, MODEL_WIDTH, UNIT), BF),
        pltpu.VMEM((n, ROWS, FF), BF), pltpu.VMEM((n, ROWS, 2 * FF), BF),
        pltpu.VMEM((ROWS, LANES), F32), pltpu.VMEM((ROWS, LANES), F32),
        *extra,
        pltpu.SemaphoreType.DMA((loads,)), pltpu.SemaphoreType.DMA((stores,)),
    ]


def load_tokens(xs, dyg, chip, X, Y, head, rest, si):
    px, py = token_pairs(xs, X), chip_pairs(dyg, chip, Y)
    urgent = fetch(px[0:1] + head + py[0:1], si)
    wait(urgent)
    n = len(urgent)
    more = fetch([px[1], py[1], px[2], py[2], px[3], px[4], py[3]] + rest, si, n)
    return [[], more[0:2], more[2:4], more[4:7]], more[7:]


def stage_a(e_ref, *refs):
    xs, dyg, ws = refs[0:5], refs[5], refs[6:8]
    rt_h, routes = refs[8], refs[9:13]
    gh_h, dgu_h, dwo_h, dws_h, gates_h, dgate_h = refs[13:19]
    X, Y, W, GH, DGU, GT, DG, DW, rt, si, so = refs[19:]
    trees, _ = load_tokens(
        xs, dyg, e_ref[4], X, Y, [(rt_h, rt)] + [(ws[i], W.at[0, i]) for i in range(2)], [], si
    )
    router = rt[...].astype(BF)
    for t in range(4):
        wait(trees[t])
        GT[TREE[t], :] = soft_gates(X[TREE[t], :], router, route_mask(routes[t][...].astype(F32)))
        DG[TREE[t], :] = act(TREE[t], e_ref[1], X, Y, W.at[0], GT, GH.at[0], DGU.at[0])
    outs = fetch([(GH.at[0], gh_h), (DGU.at[0], dgu_h), (GT, gates_h), (DG, dgate_h)], so)
    wgrad(X, Y, GH.at[0], DGU.at[0], DW)
    outs += fetch([(DW.at[0], dwo_h), (DW.at[1], dws_h)], so, 4)
    wait(outs)


ACT_OUT = [((ROWS, FF), BF), ((ROWS, 2 * FF), BF)]
GATE_OUT = [((ROWS, LANES), F32)]
DW_OUT = [((MODEL_WIDTH, UNIT), BF)] * 2
DW_VMEM = pltpu.VMEM((2, MODEL_WIDTH, UNIT), BF)
EXPERT_FLOPS = 2 * ROWS * MODEL_WIDTH * 3 * FF


def run_stage_a(e, xs, dyg, pair, rt, routes):
    extra = [DW_VMEM, pltpu.VMEM((LANES, MODEL_WIDTH), F32)]
    return call(
        stage_a, ACT_OUT + DW_OUT + GATE_OUT * 2, [SM] + [HB] * 9 + [VM] * 4, [HB] * 6,
        stage_scratch(1, extra, 12, 6), (e, *xs, dyg, *pair, rt, *routes), "stage_a", 48, 2 * EXPERT_FLOPS,
    )


def stage_b(e_ref, *refs):
    xs, dyg, ws = refs[0:5], refs[5], refs[6:10]
    gates_h, dgate_i = refs[10:12]
    gh0_h, dgu0_h, gh2_h, dgu2_h, dgate_h = refs[12:17]
    X, Y, W, GH, DGU, GT, DG, si, so = refs[17:]
    hw = [(ws[i], W.at[i // 2, i % 2]) for i in range(4)]
    trees, second = load_tokens(
        xs, dyg, e_ref[4], X, Y, hw[0:2] + [(gates_h, GT), (dgate_i, DG)], hw[2:], si
    )
    for t in range(4):
        wait(trees[t])
        DG[TREE[t], :] += act(TREE[t], e_ref[0], X, Y, W.at[0], GT, GH.at[0], DGU.at[0])
    outs = fetch([(GH.at[0], gh0_h), (DGU.at[0], dgu0_h)], so)
    wait(second)
    for t in range(4):
        DG[TREE[t], :] += act(TREE[t], e_ref[2], X, Y, W.at[1], GT, GH.at[1], DGU.at[1])
    outs += fetch([(GH.at[1], gh2_h), (DGU.at[1], dgu2_h), (DG, dgate_h)], so, 2)
    wait(outs)


def run_stage_b(e, xs, dyg, ws, gates, dgate):
    return call(
        stage_b, ACT_OUT * 2 + GATE_OUT, [SM] + [HB] * 12, [HB] * 5,
        stage_scratch(2, [], 15, 5), (e, *xs, dyg, *ws, gates, dgate), "stage_b", 48, 2 * EXPERT_FLOPS,
    )


def stage_c(e_ref, *refs):
    xs, dyg, ws = refs[0:5], refs[5], refs[6:14]
    gates_h, dgate_i = refs[14:16]
    dgus = refs[16:19]
    gh_h, dgu_h, dgate_h, parts_h = refs[19:23]
    X, Y, W, GH, DGU, GT, DG, WB, DF, OUT, si, so = refs[23:]
    late = [(ws[i].at[:, 0:WIDE], WB.at[:, i * WIDE : (i + 1) * WIDE]) for i in range(6)]
    late += [(dgus[i].at[T:ROWS], DF.at[:, 2 * i * FF : 2 * (i + 1) * FF]) for i in range(3)]
    trees, late = load_tokens(
        xs, dyg, e_ref[4], X, Y,
        [(ws[6 + i], W.at[0, i]) for i in range(2)] + [(gates_h, GT), (dgate_i, DG)], late, si,
    )
    def tree(t, carry):
        for k in range(1, 4):
            @pl.when(t == k)
            def _():
                wait(trees[k])
        rows = pl.ds(pl.multiple_of(t * T, T), T)
        DG[rows, :] += act(rows, e_ref[3], X, Y, W.at[0], GT, GH.at[0], DGU.at[0])
        return carry

    lax.fori_loop(0, 4, tree, 0)
    outs = fetch([(GH.at[0], gh_h), (DGU.at[0], dgu_h), (DG, dgate_h)], so)
    wait(late)
    w = jnp.concatenate([WB[...]] + [W[0, i, :, 0:WIDE] for i in range(2)], axis=1)
    for i, t in enumerate((3, 1, 2)):
        a = jnp.concatenate([DF[TREE[t - 1], :], DGU[0, TREE[t], :]], axis=1)
        OUT[i, :, 0:MODEL_WIDTH] = dotg(a, w, NT).astype(BF)
        OUT[i, :, MODEL_WIDTH:] = DG[TREE[t], :].astype(BF)
        outs += fetch([(OUT.at[i], parts_h.at[e_ref[4] ^ t])], so, 3 + i)
    wait(outs)


def run_stage_c(e, xs, dyg, ws, gates, dgate, dgus):
    cols = MODEL_WIDTH + LANES
    extra = [
        pltpu.VMEM((MODEL_WIDTH, 6 * WIDE), BF), pltpu.VMEM((3 * T, 6 * FF), BF), pltpu.VMEM((3, T, cols), BF),
    ]
    return call(
        stage_c, ACT_OUT + GATE_OUT + [((4, T, cols), BF)], [SM] + [HB] * 19, [HB] * 4,
        stage_scratch(1, extra, 22, 6), (e, *xs, dyg, *ws, gates, dgate, *dgus), "stage_c", 48, 2 * EXPERT_FLOPS,
    )


def back_pairs(acts, ws, lo, m, width, first_col, A, W):
    pairs = []
    for k in range(4):
        pairs.append((acts[k].at[lo : lo + m], A.at[:, k * 2 * width : (k + 1) * 2 * width]))
        for u in range(2):
            at = (2 * k + u) * width
            pairs.append((ws[2 * k + u].at[:, first_col : first_col + width], W.at[:, at : at + width]))
    return pairs


def late_stage(e_ref, *refs):
    xs, dyg, gh_h, dgu_h = refs[0:5], refs[5], refs[6], refs[7]
    dgus, ws, dgate_h = refs[8:12], refs[12:20], refs[20]
    dwo_h, dws_h, own_h = refs[21:24]
    X, Y, GH, DGU, DW, A, W, DG, O, si, so = refs[24:]
    first = fetch(chip_pairs(dyg, e_ref[4], Y) + [(gh_h, GH)], si)
    wait(first)
    second = fetch(token_pairs(xs, X) + [(dgu_h, DGU)], si, 5)
    third = fetch(back_pairs(dgus, ws, 0, T, WIDE, 0, A, W) + [(dgate_h.at[0:T], DG)], si, 11)
    wgrad_down(Y, GH, DW)
    wait(second)
    wgrad_up(X, DGU, DW)
    outs = fetch([(DW.at[0], dwo_h), (DW.at[1], dws_h)], so)
    wait(third)
    O[:, 0:MODEL_WIDTH] = dotg(A[...], W[...], NT)
    O[:, MODEL_WIDTH:] = DG[...]
    outs += fetch([(O, own_h)], so, 2)
    wait(outs)


def run_late(e, xs, dyg, acts, back):
    cols = MODEL_WIDTH + LANES
    args = (e, *xs, dyg, *acts, *back)
    return call(
        late_stage, DW_OUT + [((T, cols), F32)], [SM] + [HB] * (len(args) - 1), [HB] * 3,
        [
            pltpu.VMEM((ROWS, MODEL_WIDTH), BF), pltpu.VMEM((ROWS, MODEL_WIDTH), BF),
            pltpu.VMEM((ROWS, FF), BF), pltpu.VMEM((ROWS, 2 * FF), BF), DW_VMEM,
            pltpu.VMEM((T, 8 * WIDE), BF), pltpu.VMEM((MODEL_WIDTH, 8 * WIDE), BF),
            pltpu.VMEM((T, LANES), F32), pltpu.VMEM((T, cols), F32),
            pltpu.SemaphoreType.DMA((24,)), pltpu.SemaphoreType.DMA((3,)),
        ],
        args, "late_stage", 52, 2 * EXPERT_FLOPS,
    )


def grads_stage(e_ref, *refs):
    xs, dyg, acts = refs[0:5], refs[5], refs[6:10]
    dws = refs[10:14]
    X, Y, GH, DGU, DW, si, so = refs[14:]
    first = fetch(chip_pairs(dyg, e_ref[4], Y) + [(acts[0], GH.at[0])], si)
    wait(first)
    second = fetch(token_pairs(xs, X) + [(acts[1], DGU.at[0])], si, 5)
    third = fetch([(acts[2], GH.at[1]), (acts[3], DGU.at[1])], si, 11)
    outs = []
    for i in range(2):
        wgrad_down(Y, GH.at[i], DW.at[i])
        if i == 0:
            wait(second)
        wgrad_up(X, DGU.at[i], DW.at[i])
        outs += fetch([(DW.at[i, 0], dws[2 * i]), (DW.at[i, 1], dws[2 * i + 1])], so, 2 * i)
        if i == 0:
            wait(third)
    wait(outs)


def run_grads(e, xs, dyg, acts):
    args = (e, *xs, dyg, *acts)
    return call(
        grads_stage, DW_OUT * 2, [SM] + [HB] * (len(args) - 1), [HB] * 4,
        [
            pltpu.VMEM((ROWS, MODEL_WIDTH), BF), pltpu.VMEM((ROWS, MODEL_WIDTH), BF),
            pltpu.VMEM((2, ROWS, FF), BF), pltpu.VMEM((2, ROWS, 2 * FF), BF),
            pltpu.VMEM((2, 2, MODEL_WIDTH, UNIT), BF),
            pltpu.SemaphoreType.DMA((13,)), pltpu.SemaphoreType.DMA((4,)),
        ],
        args, "grads_stage", 52, 2 * EXPERT_FLOPS,
    )


def out_stage(e_ref, *refs):
    ghs, ws = refs[0:4], refs[4:12]
    parts_h, own_h = refs[12:14]
    A, W, O, OF, si, so = refs[14:]
    order = (3, 1, 2, 0)
    pairs = [
        (ws[i].at[:, WIDE:UNIT], W.at[:, i * HALF : (i + 1) * HALF]) for i in range(8)
    ]
    for t in order:
        pairs += [(ghs[k].at[TREE[t]], A.at[TREE[t], k * FF : (k + 1) * FF]) for k in range(4)]
    copies = fetch(pairs, si)
    wait(copies[:8])
    outs = []
    for i, t in enumerate(order):
        wait(copies[8 + 4 * i : 12 + 4 * i])
        total = dotg(A[TREE[t], :], W[...], NT)
        dst = O.at[i] if t else OF
        dst[...] = total.astype(BF) if t else total
        outs += fetch([(dst, parts_h.at[e_ref[4] ^ t] if t else own_h)], so, i)
    wait(outs)


def run_out(e, ghs, ws):
    return call(
        out_stage, [((4, T, MODEL_WIDTH), BF), ((T, MODEL_WIDTH), F32)], [SM] + [HB] * 12, [HB] * 2,
        [
            pltpu.VMEM((ROWS, 8 * HALF), BF), pltpu.VMEM((MODEL_WIDTH, 8 * HALF), BF),
            pltpu.VMEM((3, T, MODEL_WIDTH), BF), pltpu.VMEM((T, MODEL_WIDTH), F32),
            pltpu.SemaphoreType.DMA((24,)), pltpu.SemaphoreType.DMA((4,)),
        ],
        (e, *ghs, *ws), "out_stage", 32, 2 * ROWS * MODEL_WIDTH * 8 * HALF,
    )


def fold(*refs):
    totals, outs, H, sem = refs[0:4], refs[4:8], refs[8], refs[9]
    wait(fetch([(t, H.at[i]) for i, t in enumerate(totals)], sem))
    for k, o in enumerate(outs):
        for at, first, width in ((0, k * 512, 512), (512, 2048 + k * 256, 256), (768, 3072, LANES)):
            cols = slice(first, first + width)
            part = H[0, :, cols].astype(F32) + H[1, :, cols].astype(F32)
            part = part + (H[2, :, cols].astype(F32) + H[3, :, cols].astype(F32))
            o[:, at : at + width] = part.astype(BF)


def run_fold(total):
    dr, cols = total[0].shape
    return call(
        fold, [((dr, 896), BF)] * 4, [HB] * 4, [VM] * 4,
        [pltpu.VMEM((4, dr, cols), BF), pltpu.SemaphoreType.DMA((4,))], total, "fold", 48, 0,
    )


def settle(dr):
    def body(home_h, gu_ref, dn_ref, H, sem):
        c = pltpu.make_async_copy(home_h, H, sem.at[0])
        c.start()
        c.wait()
        for e in range(4):
            for h in range(2):
                part = H[2 * e + h].astype(F32)
                cols = slice(h * HALF, (h + 1) * HALF)
                gu_ref[:, e, cols] = part[:, 0:HALF]
                gu_ref[:, e, FF + h * HALF : FF + (h + 1) * HALF] = part[:, HALF:WIDE]
                dn_ref[:, e, cols] = part[:, WIDE:UNIT]

    return body


def columns_of(rowwise, lane):
    total = jnp.sum(rowwise, axis=0, keepdims=True)
    total = jnp.broadcast_to(total, (LANES, MODEL_WIDTH)).T
    lanes = lax.broadcasted_iota(jnp.int32, total.shape, 1)
    return jnp.where(lanes == lane, total, 0.0)


def join(split, dr, e_ref, p_h, parts_h, gates_h, h1_h, n2_h, dy_h, wo_h, att_h, small_h,
         dh1_h, datt_h, *refs):
    n = 2 if split else 1
    dwo_h = refs[:n]
    P, R, GT, H1, N2, DY, WO, ATT, SMALL, DH1, DATT, DWO, si, so = refs[n:]
    copies = fetch(
        [(p_h, P)] + [(parts_h.at[e_ref[4] ^ t], R.at[t - 1]) for t in (1, 2, 3)]
        + [(gates_h.at[0:T], GT), (h1_h, H1), (dy_h, DY),
         (small_h, SMALL), (wo_h, WO), (att_h, ATT), (n2_h, N2)], si
    )
    wait(copies[0:8])
    gates = GT[...]
    total = P[...] + R[0].astype(F32) + R[1].astype(F32) + R[2].astype(F32)
    dg = total[:, MODEL_WIDTH:]
    dl = (gates * (dg - jnp.sum(gates * dg, axis=1, keepdims=True))).astype(BF)
    dn2 = total[:, :MODEL_WIDTH] + dot(dl, SMALL[...].astype(BF))
    h1 = H1[...]
    gain = SMALL[17:18]
    r2 = lax.rsqrt(jnp.mean(h1 * h1, axis=1, keepdims=True) + EPSILON)
    gd = gain * dn2
    inner = jnp.mean(gd * h1, axis=1, keepdims=True)
    dh1 = DY[...].astype(F32) + r2 * gd - h1 * (r2 * r2 * r2 * inner)
    DH1[...] = dh1
    db = dh1.astype(BF)
    outs = fetch([(DH1, dh1_h)], so)
    wait(copies[8:])
    for b in range(4):
        cols = slice(b * 256, (b + 1) * 256)
        DATT[b] = dot(db, WO[:, cols]).astype(BF)
        DWO[:, cols] = dotg(db, ATT[b], TN).astype(BF)
    outs += fetch([(DATT, datt_h)], so, 1)
    extra = dotg(N2[...], dl, TN) + columns_of(dn2 * h1 * r2, EXPERTS)
    DWO[:, 1024:1152] = extra.astype(BF)
    if split:
        for r in range(4):
            mine = 2 * (e_ref[4] ^ r) + e_ref[5]
            for i, at in enumerate((mine, mine ^ 1)):
                src = DWO.at[pl.ds(pl.multiple_of(at * dr, dr), dr)]
                outs += fetch([(src, dwo_h[i].at[r * dr : (r + 1) * dr])], so, 2 + 2 * r + i)
    else:
        outs += fetch([(DWO, dwo_h[0])], so, 2)
    wait(outs)


def run_join(split, dr, args):
    cols = MODEL_WIDTH + LANES
    grads = [((4 * dr, 1152), BF)] * 2 if split else [((MODEL_WIDTH, 1152), BF)]
    return call(
        functools.partial(join, split, dr),
        [((T, MODEL_WIDTH), F32), ((4, T, 256), BF)] + grads,
        [SM] + [HB] * 9, [HB] * (2 + len(grads)),
        [
            pltpu.VMEM((T, cols), F32), pltpu.VMEM((3, T, cols), BF), pltpu.VMEM((T, LANES), F32), pltpu.VMEM((T, MODEL_WIDTH), F32),
            pltpu.VMEM((T, MODEL_WIDTH), BF), pltpu.VMEM((T, MODEL_WIDTH), BF),
            pltpu.VMEM((MODEL_WIDTH, MODEL_WIDTH), BF), pltpu.VMEM((4, T, 256), BF),
            pltpu.VMEM((LANES, MODEL_WIDTH), F32),
            pltpu.VMEM((T, MODEL_WIDTH), F32), pltpu.VMEM((4, T, 256), BF), pltpu.VMEM((MODEL_WIDTH, 1152), BF),
            pltpu.SemaphoreType.DMA((12,)), pltpu.SemaphoreType.DMA((10,)),
        ],
        args, "join", 40, 2.0e9,
    )


def attn_bwd(split, dr):
    def body(mine_ref, x_h, w_h, cos_h, sin_h, bias_h, n1_h, qkv_h, datt_h, dh1_h, small_h, *refs):
        n = 5 if split else 2
        dx_h, grads_h = refs[0], refs[1:n]
        x, w, cos, sin, bias, n1, qkv, datt, dh1, gain, dx, dw, dqkv, dk, dv, si, so = refs[n : n + 17]
        copies = fetch(
            [(bias_h, bias), (qkv_h, qkv), (datt_h, datt), (cos_h, cos), (sin_h, sin), (n1_h, n1),
             (w_h, w), (x_h, x), (dh1_h, dh1), (small_h.at[16:24], gain)], si
        )
        wait(copies[0:5])
        attn_bwd_heads(cos, sin, bias, qkv, datt, dqkv, dk, dv)
        wait(copies[5:])
        attn_bwd_body(x, gain.at[0:1], w, n1, dh1, dx, dw, dqkv)
        outs = fetch([(dx, dx_h)], so)
        if split:
            for r in range(4):
                mine = mine_ref[0] ^ (2 * r)
                for i, j in enumerate((mine, mine ^ 1)):
                    src = dw.at[pl.ds(pl.multiple_of(j * dr, dr), dr)]
                    at = (r % 2) * dr
                    outs += fetch([(src, grads_h[2 * i + r // 2].at[at : at + dr])], so, 1 + 2 * r + i)
        else:
            outs += fetch([(dw, grads_h[0])], so, 1)
        wait(outs)

    return body


def run_attn_bwd(split, dr, args):
    grads = [((2 * dr, 2176), BF)] * 4 if split else [((MODEL_WIDTH, 2176), BF)]
    tile = pltpu.VMEM((T, LANES), F32)
    return call(
        attn_bwd(split, dr),
        [((T, MODEL_WIDTH), F32)] + grads,
        [SM] + [HB] * 10, [HB] * (1 + len(grads)),
        [
            pltpu.VMEM((T, MODEL_WIDTH), BF), pltpu.VMEM((MODEL_WIDTH, 2048), BF), tile, tile,
            pltpu.VMEM((T, T), F32), pltpu.VMEM((T, MODEL_WIDTH), BF), pltpu.VMEM((4, T, 512), BF),
            pltpu.VMEM((4, T, 256), BF), pltpu.VMEM((T, MODEL_WIDTH), F32), pltpu.VMEM((8, MODEL_WIDTH), F32),
            pltpu.VMEM((T, MODEL_WIDTH), F32),
            pltpu.VMEM((MODEL_WIDTH, 2176), BF), pltpu.VMEM((4, T, 512), BF), tile, tile,
            pltpu.SemaphoreType.DMA((10,)), pltpu.SemaphoreType.DMA((9,)),
        ],
        args, "attn_bwd", 40, 6.0e9,
    )


def attn_bwd_heads(cos_ref, sin_ref, bias_ref, qkv_ref, datt_ref, dqkv, dk, dv):
    low = low_half((LANES, LANES))
    first = first_of_head((T, LANES))

    def block(b, carry):
        for c in (2, 1, 0):
            rows, seen, q, keys, p = attn_rows(qkv_ref, bias_ref, b, c, low)
            da = datt_ref[b, rows, 0:LANES]
            db = datt_ref[b, rows, LANES : 2 * LANES]
            zero = jnp.zeros_like(da)
            do = jnp.concatenate(
                [jnp.where(low, da, zero), jnp.where(low, db, zero), jnp.where(low, zero, da), jnp.where(low, zero, db)],
                axis=0,
            )
            dp = dotg(do, qkv_ref[b, :seen, 384:512], NT)
            ds = (p * (dp - jnp.sum(p * dp, axis=1, keepdims=True))).astype(BF)
            dq = dot(ds, keys) * SCALE
            dkc = dotg(ds, q, TN)
            dvc = dotg(p.astype(BF), do, TN)
            if c == 2:
                dk[...] = dkc
                dv[...] = dvc
            else:
                dk[:seen] += dkc
                dv[:seen] += dvc
            cos = cos_ref[rows, :]
            sin = -sin_ref[rows, :]
            ta = jnp.where(low, dq[0:LANES], dq[2 * LANES : 3 * LANES])
            tb = jnp.where(low, dq[LANES : 2 * LANES], dq[3 * LANES :])
            dqkv[b, rows, 0:LANES] = turn(ta, cos, sin, first[rows]).astype(BF)
            dqkv[b, rows, LANES : 2 * LANES] = turn(tb, cos, sin, first[rows]).astype(BF)
        dqkv[b, :, 256:384] = turn(dk[...] * SCALE, cos_ref[...], -sin_ref[...], first).astype(BF)
        dqkv[b, :, 384:512] = dv[...].astype(BF)
        return carry

    for b in range(4):
        block(b, 0)


def attn_bwd_body(x_ref, gain_ref, w_ref, n1_ref, dh1_ref, dx_ref, dw_ref, dqkv):
    n1 = n1_ref[...]
    cat = jnp.concatenate([dqkv[b] for b in range(4)], axis=1)
    dn1 = dotg(cat, w_ref[...], NT)
    dw_ref[:, 0:2048] = dotg(n1, cat, TN).astype(BF)
    x = x_ref[...].astype(F32)
    gain = gain_ref[...]
    r1 = lax.rsqrt(jnp.mean(x * x, axis=1, keepdims=True) + EPSILON)
    gd = gain * dn1
    inner = jnp.mean(gd * x, axis=1, keepdims=True)
    dx_ref[...] = dh1_ref[...] + r1 * gd - x * (r1 * r1 * r1 * inner)
    dw_ref[:, 2048:2176] = columns_of(dn1 * x * r1, 32).astype(BF)
def visible_bias(segment, parents):
    ids = jnp.arange(parents.shape[0], dtype=jnp.int32)
    one = jnp.sum(jnp.where(segment[:, None] == ids[None, :], parents[None, :], 0), axis=1)
    two = jnp.sum(jnp.where(one[:, None] == ids[None, :], parents[None, :], 0), axis=1)
    key = segment[None, :]
    related = (key == segment[:, None]) | (key == one[:, None]) | (key == two[:, None])
    places = jnp.arange(segment.shape[0], dtype=jnp.int32)
    return jnp.where(related & (places[None, :] <= places[:, None]), 0.0, NEG_FILL).astype(F32)


def turn_tables(positions):
    half = HEAD_SIZE // 2
    lane = jnp.arange(LANES, dtype=jnp.int32)
    frequency = ROPE_BASE ** (-((lane % half).astype(F32) * 2.0) / HEAD_SIZE)
    angle = positions.astype(F32)[:, None] * frequency[None, :]
    sign = jnp.where(lane % HEAD_SIZE < half, -1.0, 1.0).astype(F32)
    return jnp.cos(angle), jnp.sin(angle) * sign[None, :]


def make_shards(groups, fsdp):
    ring = list(range(0, groups, 1))
    if groups == 4:
        ring = [0, 1, 3, 2]
    place = [ring.index(g) for g in range(groups)]
    rest = fsdp // 8

    def shifted(k):
        return [(ring[p], ring[(p + k) % groups]) for p in range(groups)]

    def flip(bits):
        return [(i, i ^ bits) for i in range(fsdp)]

    low_groups = None if rest == 1 else [[8 * r + j for j in range(8)] for r in range(rest)]
    core_groups = [[8 * r + 2 * c + k for c in range(4)] for r in range(rest) for k in range(2)]
    rest_groups = [[8 * r + j for r in range(rest)] for j in range(8)]

    def z_next(a):
        return lax.ppermute(a, "grp", shifted(1))

    def to_x(a):
        return lax.ppermute(a, "fsdp", flip(2))

    def to_y(a):
        return lax.ppermute(a, "fsdp", flip(4))

    def to_diag(a):
        return lax.ppermute(a, "fsdp", flip(6))

    def to_core(a):
        return lax.ppermute(a, "fsdp", flip(1))

    def plane(top, bot):
        xb = to_x(bot)
        yt = to_y(top)
        xt = to_x(top)
        yb = to_y(bot)
        return (top, bot, xt, xb, yt, yb, to_x(yt), to_y(xb))

    def swap(a):
        return lax.all_to_all(a, "fsdp", 0, 0, axis_index_groups=core_groups)

    def swap_all(a):
        return lax.all_to_all(a, "fsdp", 0, 0, axis_index_groups=low_groups)

    def z_sum(blocks):
        total = blocks[0].astype(F32)
        for k in range(1, groups):
            total = total + lax.ppermute(blocks[k], "grp", shifted(groups - k)).astype(F32)
        return total

    def shards(tokens, segment, positions, parents, routes, attn_gain, query_weight, key_matrix,
               value_matrix, out_weight, ffn_gain, router_weight, gate_up_weight, down_weight, cotangent):
        dr = query_weight.shape[0]
        mine = lax.axis_index("fsdp")
        spot = jnp.array(place, jnp.int32)[lax.axis_index("grp")]
        ring_ids = jnp.array(ring, jnp.int32)

        def swapped(w):
            return [w[:, 0:64], w[:, 128:192], w[:, 64:128], w[:, 192:256]]

        def z_gather(a):
            got = [a]
            for _ in range(groups - 1):
                got.append(z_next(got[-1]))
            return got

        half = T // 2
        tie = lax.optimization_barrier
        own_qkv = jnp.concatenate(swapped(query_weight) + [key_matrix, value_matrix], axis=1)
        own_out = jnp.concatenate(swapped(out_weight), axis=1)

        def z_all(a):
            return [a] + [lax.ppermute(a, "grp", shifted(k)) for k in range(1, groups)]

        route_rows = routes.T.astype(BF)
        route_rows = [route_rows, to_x(route_rows), to_y(route_rows), to_diag(route_rows)]

        gu = gate_up_weight.reshape(dr, 4, 2, 2, HALF)
        dn = down_weight.reshape(dr, 4, 1, 2, HALF)
        parts = jnp.concatenate([gu, dn], axis=2)
        parts = jnp.transpose(parts, (1, 3, 0, 2, 4)).reshape(8, dr, 3 * HALF)
        parts, own_qkv, own_out = tie((parts, own_qkv, own_out))
        blocks = z_all(jnp.concatenate([own_qkv, own_out], axis=1))
        unit = lax.all_to_all(parts, "fsdp", 0, 0, axis_index_groups=low_groups)
        unit = unit.reshape(8 * dr, 3 * HALF)
        if rest > 1:
            unit = lax.all_gather(unit, "fsdp", axis=0, tiled=True, axis_index_groups=rest_groups)

        bias = visible_bias(segment, parents[0])
        cos, sin = turn_tables(positions)
        chip = (mine // 2) % 4
        planes = ring_ids[(spot - jnp.arange(groups, dtype=jnp.int32)) % groups]
        e = jnp.concatenate([4 * planes + chip, chip[None], (mine % 2)[None]]).astype(jnp.int32)
        small = jnp.concatenate(
            [router_weight, attn_gain[:, None], ffn_gain[:, None], jnp.zeros((dr, LANES - 18), BF)], axis=1
        )
        bias, cos, sin, e, small, unit, *blocks = tie((bias, cos, sin, e, small, unit, *blocks))
        cols_qkv = jnp.concatenate([b[:, :512] for b in blocks] + [small], axis=1)
        cols_out = jnp.concatenate([b[:, 512:] for b in blocks], axis=1)
        mine_s = mine.astype(jnp.int32).reshape(1)
        units_1 = z_next(unit)
        if rest == 1:
            h = dr // 2
            qx = to_x(cols_qkv)
            qy = to_y(cols_qkv)
            qc = to_core(cols_qkv)
            qx, qy, qc = tie((qx, qy, qc))
            qa = to_x(qy[:h])
            qb = to_y(qx[h:])
            cx, cy = to_core(qx), to_core(qy)
            qa, qb, units_1 = tie((qa, qb, units_1))
            pieces = [cols_qkv, qx, qy, qa, qb, qc, cx, cy, to_core(qa), to_core(qb)]
            places = [(0, 0, dr), (2, 0, dr), (4, 0, dr), (6, 0, h), (6, h, h),
                      (1, 0, dr), (3, 0, dr), (5, 0, dr), (7, 0, h), (7, h, h)]
        else:
            pieces = [lax.all_gather(cols_qkv, "fsdp", axis=0, tiled=True)]
            places = [(None, 0, MODEL_WIDTH)]
        w_out = lax.all_gather(cols_out, "fsdp", axis=0, tiled=True)
        core_0 = to_core(after(unit, *pieces))
        dyg = lax.all_gather(after(cotangent, cols_out), "fsdp", axis=0, tiled=True, axis_index_groups=core_groups)
        tokens_f = after(tokens, *pieces)
        units_2 = z_next(units_1)
        w_qkv, n1, qkv, att, h1, n2, small = call(
            attn_fwd(places, dr),
            [((MODEL_WIDTH, 2048), BF), ((T, MODEL_WIDTH), BF), ((4, T, 512), BF), ((4, T, 256), BF),
             ((T, MODEL_WIDTH), F32), ((T, MODEL_WIDTH), BF), ((LANES, MODEL_WIDTH), F32)],
            [SM] + [HB] * (len(pieces) + 5), [HB] * 7,
            [
                pltpu.VMEM((T, MODEL_WIDTH), BF), pltpu.VMEM((T, LANES), F32), pltpu.VMEM((T, LANES), F32),
                pltpu.VMEM((T, T), F32), pltpu.VMEM((MODEL_WIDTH, MODEL_WIDTH), BF),
                pltpu.VMEM((MODEL_WIDTH, 2176), BF), pltpu.VMEM((T, MODEL_WIDTH), BF),
                pltpu.VMEM((4, T, 512), BF), pltpu.VMEM((4, T, 256), BF), pltpu.VMEM((T, MODEL_WIDTH), F32),
                pltpu.VMEM((T, MODEL_WIDTH), BF), pltpu.VMEM((LANES, MODEL_WIDTH), F32),
                pltpu.SemaphoreType.DMA((len(pieces) + 5,)), pltpu.SemaphoreType.DMA((8,)),
            ],
            (mine_s, *pieces, tokens_f, cos, sin, bias, w_out), "attn_fwd", 40, 4.0e9,
        )
        n2, core_0 = tie((n2, core_0))
        nx = to_x(n2)
        ny = to_y(n2)
        core_1 = to_core(after(units_1, n2))
        nx, ny, units_2 = tie((nx, ny, units_2))
        xs = (n2, nx, ny, to_x(ny[:half]), to_y(nx[half:]))
        core_1, *xs = tie((core_1, *xs))
        units_3 = z_next(units_2)
        core_2 = to_core(units_2)

        def chip_sum(pair, *more):
            total = pair[0].astype(F32) + pair[1].astype(F32)
            for m in more:
                total = total + m.astype(F32)
            return total.astype(BF)

        gh1, dgu1, own_1, sib_1, gates, dgate = run_stage_a(e, xs, dyg, (units_1, core_1), small, route_rows)
        core_2, gates = tie((core_2, gates))
        sib_1 = to_core(sib_1)
        gh0, dgu0, gh2, dgu2, dgate = run_stage_b(e, xs, dyg, (unit, core_0, units_2, core_2), gates, dgate)
        units_3, sib_1, dgate = tie((units_3, sib_1, dgate))
        core_3 = to_core(units_3)
        ws = (unit, core_0, units_1, core_1, units_2, core_2, units_3, core_3)
        sum_1, dgate = tie((chip_sum((own_1, sib_1)), dgate))
        hop = z_next(sum_1)
        gh3, dgu3, dgate, parts = run_stage_c(e, xs, dyg, ws, gates, dgate, (dgu0, dgu1, dgu2))
        dgate, parts = tie((dgate, parts))
        parts = swap(parts)
        dgus = (dgu0, dgu1, dgu2, dgu3)
        own_2, sib_2, own = run_late(e, xs, dyg, (gh2, dgu2), (*dgus, *ws, dgate))
        sib_2 = to_core(sib_2)
        hop, own, gh3 = tie((hop, own, gh3))
        own_3, sib_3, own_0, sib_0 = run_grads(e, xs, dyg, (gh3, dgu3, gh0, dgu0))
        sib_2, gh0, own_3 = tie((sib_2, gh0, own_3))
        sum_2, gh0 = tie((chip_sum((own_2, sib_2), hop), gh0))
        hop = z_next(sum_2)
        sib_3 = to_core(sib_3)
        sib_0 = to_core(sib_0)
        outs, oown = run_out(e, (gh0, gh1, gh2, gh3), ws)
        parts, own, outs, sib_3, sib_0 = tie((parts, own, outs, sib_3, sib_0))
        outs = swap(outs)
        dh1, datt, *dwo = run_join(
            rest == 1, dr, (e, own, parts, gates, h1, n2, cotangent, w_out, att, small)
        )
        if rest == 1:
            sib_o = to_core(dwo[1])
        else:
            rs_out = lax.psum_scatter(dwo[0], "fsdp", scatter_dimension=0, tiled=True)
        dx, *dw = run_attn_bwd(
            rest == 1, dr, (mine_s, tokens, w_qkv, cos, sin, bias, n1, qkv, datt, dh1, small)
        )
        hop, *dw = tie((hop, *dw))
        hop = z_next(chip_sum((own_3, sib_3), hop))
        if rest == 1:
            sib_a, sib_b, sib_o, outs = tie((to_core(dw[2]), to_core(dw[3]), sib_o, outs))
            def chip_part(r):
                pair = (dw[r // 2], sib_a if r < 2 else sib_b)
                here = slice((r % 2) * dr, (r % 2 + 1) * dr)
                there = slice(r * dr, (r + 1) * dr)
                mine_q = pair[0][here].astype(F32) + pair[1][here].astype(F32)
                mine_o = dwo[0][there].astype(F32) + sib_o[there].astype(F32)
                return jnp.concatenate(
                    [mine_q[:, :2048], mine_o[:, :1024], mine_q[:, 2048:] + mine_o[:, 1024:]], axis=1
                ).astype(BF)

            total = (chip_part(0), to_x(chip_part(1)), to_y(chip_part(2)), to_diag(chip_part(3)))
            acc = chip_sum((own_0, sib_0), hop)
            acc, *total = tie((acc, *total))
            home = swap_all(acc.reshape(8, dr, UNIT))
            blocks = run_fold(total)
        else:
            rs_qkv = lax.psum_scatter(dw[0], "fsdp", scatter_dimension=0, tiled=True)

        if rest > 1:
            acc = lax.psum_scatter(
                chip_sum((own_0, sib_0), hop), "fsdp", scatter_dimension=0, tiled=True,
                axis_index_groups=rest_groups,
            )
            home = swap_all(acc.reshape(8, dr, UNIT))
        gate_up_grad, down_grad = call(
            settle(dr), [((dr, 4, 2 * FF), F32), ((dr, 4, FF), F32)], [HB], [VM] * 2,
            [pltpu.VMEM((8, dr, UNIT), BF), pltpu.SemaphoreType.DMA((1,))], (home,), "settle", 48, 0,
        )

        near = [
            lax.dynamic_index_in_dim(outs, chip ^ t, 0, keepdims=False).astype(F32) for t in (1, 2, 3)
        ]
        output = (h1 + oown + near[0] + near[1] + near[2]).astype(BF)
        if rest > 1:
            blocks = [
                jnp.concatenate(
                    [rs_qkv[:, k * 512 : (k + 1) * 512], rs_out[:, k * 256 : (k + 1) * 256],
                     rs_qkv[:, 2048:] + rs_out[:, 1024:]], axis=1
                )
                for k in range(groups)
            ]
        z_qkv = z_sum(blocks)
        z_out = z_qkv[:, 512:]
        return (
            output,
            dx,
            z_out[:, 256 + 32],
            jnp.concatenate(swapped(z_qkv[:, :256]), axis=1),
            z_qkv[:, 256:384],
            z_qkv[:, 384:512],
            jnp.concatenate(swapped(z_out[:, :256]), axis=1),
            z_out[:, 256 + EXPERTS],
            z_out[:, 256 : 256 + EXPERTS],
            gate_up_grad,
            down_grad,
        )

    return shards


def solution(mesh):
    both = ("grp", "fsdp")
    in_specs = (
        P(both, None), P(both), P(both), P(both, None), P(both, None),
        P("fsdp"), P("fsdp", "grp"), P("fsdp", "grp"), P("fsdp", "grp"), P("fsdp", "grp"),
        P("fsdp"), P("fsdp", None), P("fsdp", "grp", None), P("fsdp", "grp", None), P(both, None),
    )
    out_specs = (
        P(both, None), P(both, None), P("fsdp"),
        P("fsdp", "grp"), P("fsdp", "grp"), P("fsdp", "grp"), P("fsdp", "grp"),
        P("fsdp"), P("fsdp", None), P("fsdp", "grp", None), P("fsdp", "grp", None),
    )
    shards = make_shards(mesh.shape["grp"], mesh.shape["fsdp"])
    return jax.shard_map(shards, mesh=mesh, in_specs=in_specs, out_specs=out_specs, check_vma=False)
```
